32 devices in a mesh: group: 2 (over x), tile: 16 (over z, y, core).
Axes of the slice: x: 2, y: 2, z: 4, core: 2. Of those that a mesh axis runs over, the one named last changes fastest.
Arguments:
- object_field: float32 [4, 2, 2048, 2048], P('group', None, 'tile'), parts along dimension 0, may hold values from -6 to 6
- probe: float32 [2, 256, 256], replicated, may hold values from -6 to 6
- measured: bfloat16 [64, 256, 256], P(('group', 'tile')), parts along dimension 0, may hold values from 0.099609375 to 3
- frame_table: int32 [64, 3], P(('group', 'tile')), parts along dimension 0, may hold values from 0 to 1792, as said below
- frame_count: int32 [32], P(('group', 'tile')), parts along dimension 0, may hold values from 0 to 2, as said below
Outputs:
- updated_object: float32 [4, 2, 2048, 2048], P('group', None, 'tile'), parts along dimension 0
- phase_map: float32 [4, 2048, 2048], P('group', 'tile'), parts along dimension 0
The draws below stay inside these ranges and needn't reach their ends.
There are 2 independent parts, one for each index of `group`. The reference program is written for one: setup_inputs(seed, part) draws one part's arguments, and reference() takes and returns one part's arrays. A program takes and returns all parts, laid end to end along the dimension named above; an argument that names none is the same for every part. Nothing has to cross between parts.
Inputs may be any that keep to these rules, and one draw needn't show every extreme that they name: `frame_table`: per slot: the row offset is below 128, and the frame's rows d * 128 + offset to that plus 256 - 1 and columns lie inside the projection; the angle is below 2. Only the first frame_count[d] slots of device d are live. `frame_count`: exactly 2 on some device in every draw; zero on every device d with d * 128 > 1792.
All inputs are finite; a program needn't handle non-finite values.
Results may differ from the reference program's by a relative error of at most 0.0009.
Values may be sent and summed in bfloat16 or wider, within the bound.
A program may use at most 192 MiB of HBM per device.

```python
import math
import jax
import jax.numpy as jnp
from jax import lax

NP = 2048
FRAME = 256
ANGLES = 2
CAP = 2
SLOTS = 32
N_TILE = 16


def frame_layout(key):
    strip_rows = NP // N_TILE
    devices = jnp.arange(N_TILE, dtype=jnp.int32)
    spare_rows = jnp.clip(NP - FRAME - devices * strip_rows + 1, 0, strip_rows)
    subkeys = jax.random.split(jax.random.fold_in(key, 7), 6)
    first_draw = jax.random.randint(subkeys[0], (N_TILE,), 0, CAP, dtype=jnp.int32)
    second_draw = jax.random.randint(subkeys[1], (N_TILE,), 0, CAP, dtype=jnp.int32)
    counts = 1 + first_draw * second_draw // CAP
    busiest = jax.random.randint(subkeys[2], (), 0, N_TILE - FRAME // strip_rows + 1, dtype=jnp.int32)
    counts = jnp.where(devices == busiest, CAP, counts)
    counts = jnp.where(spare_rows > 0, counts, 0)
    offsets = jax.random.randint(subkeys[3], (N_TILE, CAP), 0, strip_rows, dtype=jnp.int32) % jnp.maximum(spare_rows, 1)[:, None]
    columns = jax.random.randint(subkeys[4], (N_TILE, CAP), 0, NP - FRAME + 1, dtype=jnp.int32)
    angle_ids = jax.random.randint(subkeys[5], (N_TILE, CAP), 0, ANGLES, dtype=jnp.int32)
    slot_table = jnp.stack([offsets, columns, angle_ids], -1).reshape(N_TILE * CAP, 3)
    return (slot_table.astype(jnp.int32), counts.astype(jnp.int32))


def draw_frame_table(key, part):
    return frame_layout(key)[0]


def draw_frame_count(key, part):
    return frame_layout(key)[1]


def block_levels(stream_key, dims, cuts, smallest, top_value):
    factor_of = 1.0
    for dim, parts in cuts:
        draws = jax.random.uniform(jax.random.fold_in(jax.random.fold_in(stream_key, 6), dim), (parts,), jnp.float32, smallest / len(cuts), top_value / len(cuts))
        factor_of = factor_of * jnp.repeat(jnp.exp(draws), dims[dim] // parts).reshape((-1,) + (1,) * (len(dims) - 1 - dim))
    return factor_of


def normal_values(own_key, shape, spread, most, pieces=(), kind=jnp.bfloat16):
    factor_of = block_levels(own_key, shape, pieces, -0.22, 0.18) if pieces else 1.0
    array = jax.random.normal(own_key, shape, jnp.float32) * spread * factor_of
    return jnp.minimum(jnp.maximum(array, -most), most).astype(kind)


def setup_inputs(seed: int = 0, part: int = 0) -> dict:
    arg_keys = jax.random.split(jax.random.key(seed), 6)
    part_splits = jax.random.split(jax.random.fold_in(arg_keys[5], part), 6)
    return {
        "object_field": normal_values(part_splits[0], (ANGLES, 2, NP, NP), 1.0, 6.0, ((2, 16),), jnp.float32),
        "probe": normal_values(arg_keys[1], (2, FRAME, FRAME), 1.0, 6.0, (), jnp.float32),
        "measured": jnp.clip(jnp.exp(math.log(3.0) - 3.4051113 * jax.random.uniform(part_splits[2], (SLOTS, FRAME, FRAME), jnp.float32) ** block_levels(part_splits[2], (SLOTS, FRAME, FRAME), ((0, 16),), -0.2, 0.2)), 0.099609375, 3.0).astype(jnp.bfloat16),
        "frame_table": draw_frame_table(jax.random.fold_in(jax.random.fold_in(arg_keys[5], part), 71), part),
        "frame_count": draw_frame_count(jax.random.fold_in(jax.random.fold_in(arg_keys[5], part), 71), part),
    }


magnitude_floor = 0.5
soften_term = 0.5
screen_term = 0.0001
epsilon_term = 1e-06

def fourier_tables(frame_side):
    indices = jnp.arange(frame_side, dtype=jnp.int32)
    products = indices[:, None] * indices[None, :] % frame_side
    phases = products.astype(jnp.float32) * (-2.0 * math.pi / frame_side)
    norm_scale = 1.0 / math.sqrt(frame_side)
    return ((jnp.cos(phases) * norm_scale).astype(jnp.bfloat16), (jnp.sin(phases) * norm_scale).astype(jnp.bfloat16))

def complex_left(table_re, table_im, operand):
    side = table_re.shape[0]
    stacked = jnp.concatenate([table_re, table_im], 0)
    joined = jnp.concatenate([operand[0], operand[1]], 1)
    products = jnp.dot(stacked, joined, preferred_element_type=jnp.float32)
    return jnp.stack([products[:side, :side] - products[side:, side:], products[:side, side:] + products[side:, :side]])

def complex_right(operand, table_re, table_im):
    side = table_re.shape[0]
    stacked = jnp.concatenate([operand[0], operand[1]], 0)
    joined = jnp.concatenate([table_re, table_im], 1)
    products = jnp.dot(stacked, joined, preferred_element_type=jnp.float32)
    return jnp.stack([products[:side, :side] - products[side:, side:], products[:side, side:] + products[side:, :side]])

def correct_frame(exit_field, magnitude, fourier):
    cos_part, sin_part = fourier
    half_spectrum = complex_left(cos_part, sin_part, exit_field).astype(jnp.bfloat16)
    spectrum = complex_right(half_spectrum, cos_part, sin_part)
    amplitude = jnp.sqrt(spectrum[0] * spectrum[0] + spectrum[1] * spectrum[1])
    factor = magnitude.astype(spectrum.dtype) / jnp.maximum(amplitude, magnitude_floor) - 1.0
    change = (spectrum * factor[None]).astype(jnp.bfloat16)
    half_back = complex_left(cos_part, -sin_part, change).astype(jnp.bfloat16)
    return complex_right(half_back, cos_part, -sin_part)

def exit_wave(probe, patch):
    object_part = patch.astype(probe.dtype)
    real_part = probe[0] * object_part[0] - probe[1] * object_part[1]
    imag_part = probe[0] * object_part[1] + probe[1] * object_part[0]
    return jnp.stack([real_part, imag_part]).astype(jnp.bfloat16)

def object_step(probe, correction, probe_peak):
    real_part = (probe[0] * correction[0] + probe[1] * correction[1]) / probe_peak
    imag_part = (probe[0] * correction[1] - probe[1] * correction[0]) / probe_peak
    return jnp.stack([real_part, imag_part])

def phase_bond(first_cell, second_cell):
    cross_term = first_cell[:, 0] * second_cell[:, 1] - first_cell[:, 1] * second_cell[:, 0]
    power_sum = first_cell[:, 0] ** 2 + first_cell[:, 1] ** 2 + second_cell[:, 0] ** 2 + second_cell[:, 1] ** 2 + soften_term
    return 2.0 * cross_term / power_sum

def cosine_last(values):
    length = values.shape[-1]
    mirrored = jnp.concatenate([values, jnp.flip(values, -1)], -1)
    spectrum = jnp.fft.fft(mirrored, axis=-1)[..., :length]
    freqs = jnp.arange(length, dtype=jnp.int32).astype(values.dtype)
    twisted = jnp.real(spectrum * jnp.exp(-1j * math.pi * freqs / (2 * length)))
    norm_scale = jnp.where(freqs == 0, math.sqrt(1.0 / length), math.sqrt(2.0 / length)) * 0.5
    return (twisted * norm_scale).astype(values.dtype)

def inverse_last(coeffs):
    length = coeffs.shape[-1]
    freqs = jnp.arange(length, dtype=jnp.int32).astype(coeffs.dtype)
    norm_scale = jnp.where(freqs == 0, math.sqrt(1.0 / length), math.sqrt(2.0 / length))
    weighted = coeffs * norm_scale * jnp.exp(1j * math.pi * freqs / (2 * length))
    padded = jnp.concatenate([weighted, jnp.zeros_like(weighted)], -1)
    values = jnp.real(jnp.fft.ifft(padded, axis=-1)[..., :length]) * (2 * length)
    return values.astype(coeffs.dtype)

def reference(object_field, probe, measured, frame_table, frame_count):
    window_object = object_field.astype(jnp.bfloat16)
    fourier = fourier_tables(FRAME)
    probe_peak = jnp.max(probe[0] * probe[0] + probe[1] * probe[1]) + epsilon_term
    strip_rows = NP // N_TILE
    anchor = jnp.zeros((), jnp.int32)

    def visit(slot_index, deposits):
        slot_index = jnp.asarray(slot_index).astype(jnp.int32)
        owner = slot_index // CAP
        live = slot_index % CAP < frame_count[owner]

        def apply(current_sum):
            record = frame_table[slot_index]
            corner = (record[2].astype(jnp.int32), anchor, (owner * strip_rows + record[0]).astype(jnp.int32), record[1].astype(jnp.int32))
            patch = lax.dynamic_slice(window_object, corner, (1, 2, FRAME, FRAME))[0]
            correction = correct_frame(exit_wave(probe, patch), measured[slot_index], fourier)
            update = object_step(probe, correction, probe_peak)
            current = lax.dynamic_slice(current_sum, corner, (1, 2, FRAME, FRAME))
            return lax.dynamic_update_slice(current_sum, current + update[None], corner)
        return lax.cond(live, apply, lambda current_sum: current_sum, deposits)
    deposits = lax.fori_loop(0, SLOTS, visit, jnp.zeros(object_field.shape, object_field.dtype))
    updated_object = object_field + deposits
    padded = jnp.pad(updated_object, ((0, 0), (0, 0), (1, 1), (1, 1)))
    row_grad = phase_bond(padded[:, :, :-1, 1:-1], padded[:, :, 1:, 1:-1])
    col_grad = phase_bond(padded[:, :, 1:-1, :-1], padded[:, :, 1:-1, 1:])
    source = -(row_grad[:, 1:] - row_grad[:, :-1] + col_grad[:, :, 1:] - col_grad[:, :, :-1])
    along_rows = jnp.swapaxes(cosine_last(jnp.swapaxes(source, 1, 2)), 1, 2)
    both_dims = cosine_last(along_rows)
    freqs = jnp.arange(NP, dtype=jnp.int32).astype(source.dtype)
    eigen = 2.0 - 2.0 * jnp.cos(freqs * (math.pi / NP))
    coefficients = both_dims / (screen_term + eigen[None, :, None] + eigen[None, None, :])
    back_rows = jnp.swapaxes(inverse_last(jnp.swapaxes(coefficients, 1, 2)), 1, 2)
    phase_map = inverse_last(back_rows)
    return (updated_object, phase_map)
```

```python
import functools
import math

import numpy as np
import jax
import jax.numpy as jnp
from jax import lax
from jax.experimental import pallas as pl
from jax.experimental.pallas import tpu as pltpu
from jax.sharding import PartitionSpec as P

magnitude_floor = 0.5
soften_term = 0.5
screen_term = 0.0001
epsilon_term = 1e-06
f32 = jnp.float32
bf16 = jnp.bfloat16
LANES = 128
GROUP = 8
TILE = 256
VMEM_BYTES = 30 * 1024 * 1024
MESH = pl.DeviceIdType.MESH
vmem = pl.BlockSpec(memory_space=pltpu.VMEM)
smem = pl.BlockSpec(memory_space=pltpu.SMEM)
hbm = pl.BlockSpec(memory_space=pltpu.HBM)


def cost(micros):
    return pl.CostEstimate(
        flops=0, bytes_accessed=int(micros * 3_000_000), transcendentals=0
    )


def params(**more):
    return pltpu.CompilerParams(vmem_limit_bytes=VMEM_BYTES, **more)


def join_kernel(ends, powers, extra, out, heard, told, up_sems, in_sems, down_sems, back_sems):
    count = lax.axis_size("tile")
    me = lax.axis_index("tile")
    blocks, lines = ends.shape[0], ends.shape[1]
    angles = lines // 2
    stride = count // blocks
    mine = me // stride
    joins = lax.rem(me, stride) == 0
    barrier = pltpu.get_barrier_semaphore()

    def greet(by, _):
        pl.semaphore_signal(
            barrier, inc=1, device_id={"tile": lax.rem(me + by, count)}, device_id_type=MESH
        )
        return 0

    lax.fori_loop(1, count, greet, 0)
    pl.semaphore_wait(barrier, count - 1)

    def up(by):
        block = lax.rem(mine + by, blocks)
        return pltpu.make_async_remote_copy(
            src_ref=ends.at[block],
            dst_ref=heard.at[me],
            send_sem=up_sems.at[block],
            recv_sem=in_sems.at[me],
            device_id={"tile": block * stride},
            device_id_type=MESH,
        )

    def came(other):
        return pltpu.make_async_remote_copy(
            src_ref=ends.at[0],
            dst_ref=heard.at[other],
            send_sem=up_sems.at[0],
            recv_sem=in_sems.at[other],
            device_id={"tile": other},
            device_id_type=MESH,
        )

    def down(other):
        return pltpu.make_async_remote_copy(
            src_ref=told.at[other],
            dst_ref=out.at[mine],
            send_sem=down_sems.at[other],
            recv_sem=back_sems.at[mine],
            device_id={"tile": other},
            device_id_type=MESH,
        )

    def answered(block):
        return pltpu.make_async_remote_copy(
            src_ref=told.at[0],
            dst_ref=out.at[block],
            send_sem=down_sems.at[0],
            recv_sem=back_sems.at[block],
            device_id={"tile": block * stride},
            device_id_type=MESH,
        )

    def each(limit, step):
        def run(index, _):
            step(index)
            return 0

        lax.fori_loop(0, limit, run, 0)

    for by in range(blocks):
        pl.when(lax.rem(mine + by, blocks) * stride != me)(lambda: up(by).start())

    @pl.when(joins)
    def _():
        heard[me] = ends[mine]
        for by in range(1, count):
            came(lax.rem(me + by, count)).wait_recv()
        step = powers[mine, 1:2]
        whole = powers[mine, count : count + 1]
        closing = extra[mine, 1:2]
        gain = extra[mine, 0:1]
        wall = heard[count - 1, angles:]
        floor = heard[0, :angles]
        for strip in range(1, count):
            floor = floor * step + heard[strip, :angles]
            wall = wall * step + heard[count - 1 - strip, angles:]
        enter = (wall + whole * floor) * closing
        leave = (floor + whole * wall) * closing
        for strip in range(count):
            told[strip, :angles] = enter * gain
            enter = enter * step + heard[strip, :angles]
            back = count - 1 - strip
            told[back, angles:] = leave * gain
            leave = leave * step + heard[back, angles:]
        for by in range(1, count):
            down(lax.rem(me + by, count)).start()
        out[mine] = told[me]

    for by in range(blocks):
        block = lax.rem(mine + by, blocks)
        pl.when(block * stride != me)(lambda: answered(block).wait_recv())
        pl.when(block * stride != me)(lambda: up(by).wait_send())

    @pl.when(joins)
    def _():
        for by in range(1, count):
            down(lax.rem(me + by, count)).wait_send()


def fourier_tables(side):
    indices = np.arange(side)
    products = indices[:, None] * indices[None, :] % side
    phases = products.astype(np.float64) * (-2.0 * math.pi / side)
    scale = 1.0 / math.sqrt(side)
    return (
        jnp.asarray(np.cos(phases) * scale, f32).astype(bf16),
        jnp.asarray(np.sin(phases) * scale, f32).astype(bf16),
    )


def cosine_factors(grid_side):
    half = grid_side // 2
    step = 32
    out = []
    for odd in (0, 1):
        freqs = 2 * np.arange(half) + odd
        scale = np.where(freqs == 0, math.sqrt(1.0 / grid_side), math.sqrt(2.0 / grid_side))
        coarse = (2 * step * np.arange(half // step)[:, None] * freqs[None, :]) % (4 * grid_side)
        fine = ((2 * np.arange(step)[:, None] + 1) * freqs[None, :]) % (4 * grid_side)
        unit = math.pi / (2 * grid_side)
        out.append(
            np.stack(
                [
                    np.cos(coarse * unit) * scale,
                    np.sin(coarse * unit) * scale,
                    np.cos(fine * unit),
                    np.sin(fine * unit),
                ]
            )
        )
    return jnp.asarray(np.stack(out), f32)


def decay_tables(grid_side, strip_rows):
    half = grid_side // 2
    freqs = np.concatenate([2 * np.arange(half), 2 * np.arange(half) + 1]).astype(np.float64)
    shift = screen_term + 2.0 - 2.0 * np.cos(freqs * math.pi / grid_side)
    rate = 2.0 * np.arcsinh(np.sqrt(shift) / 2.0)
    gain = 1.0 / (2.0 * np.sinh(rate))
    rows = np.arange(GROUP)[:, None]
    down = [np.where(rows >= s, np.exp(-s * rate), 0.0) for s in (1, 2, 4)]
    up = [np.where(rows < GROUP - s, np.exp(-s * rate), 0.0) for s in (1, 2, 4)]
    down.append(np.exp(-(rows + 1) * rate))
    up.append(np.exp(-(GROUP - rows) * rate))
    local = np.stack(down + up)
    strips = grid_side // strip_rows
    powers = np.exp(-strip_rows * np.arange(strips + 1)[:, None] * rate)
    extra = np.stack(
        [gain, 1.0 / (1.0 - np.exp(-2.0 * grid_side * rate)), np.exp(-GROUP * rate)]
        + [rate * 0.0] * 5
    )
    return local.astype(np.float32), powers.astype(np.float32), extra.astype(np.float32)


def table_rows(factors, part, high, low):
    step = factors.shape[2]

    def run(block, _):
        rows = pl.ds(pl.multiple_of(block * step, step), step)
        value = (
            factors[part, 0, pl.ds(block, 1)] * factors[part, 2]
            - factors[part, 1, pl.ds(block, 1)] * factors[part, 3]
        )
        rounded = value.astype(bf16)
        high[rows] = rounded
        low[rows] = (value - rounded.astype(f32)).astype(bf16)
        return 0

    lax.fori_loop(0, high.shape[0] // step, run, 0)


def window_start(column, width, span):
    return jnp.minimum(column // LANES, (width - span) // LANES) * LANES


def update_kernel(
    frame_table, frame_count, field, probe_in, measured, cos_in, sin_in, factors_in,
    held, halo, even_hi, even_lo, odd_hi, odd_lo,
    tables, counts, probe, cos_ref, sin_ref, factors, moved, cuts, arrived, away, landed,
    own, placed, window, edges,
    load_sems, tell_sems, count_sems, moved_sems, fetch_sems, give_sems, edge_sems,
):
    count = lax.axis_size("tile")
    me = lax.axis_index("tile")
    angles, _, strip, width = field.shape
    cap, side = measured.shape[0], measured.shape[1]
    span = side + LANES
    lanes = span // LANES
    blocks = width // LANES
    reach = tables.shape[0] - 1
    middle = reach // 2
    total = (reach + 1) * strip
    others = [j for j in range(reach + 1) if j != middle]

    def inside(place):
        return (place >= 0) & (place < count)

    def load(index, source, target):
        return pltpu.make_async_copy(source, target, load_sems.at[index])

    loads = [
        load(0, frame_table, tables.at[0]),
        load(1, factors_in, factors),
        load(2, probe_in, probe),
        load(3, cos_in, cos_ref),
        load(4, sin_in, sin_ref),
    ]
    strips = [
        load(5 + block, field.at[:, :, :, block * LANES : (block + 1) * LANES], held.at[:, :, block])
        for block in range(blocks)
    ]
    for item in loads[:2] + strips + loads[2:]:
        item.start()
    loads[0].wait()

    def send(source, target, sems, index, by):
        copy = pltpu.make_async_remote_copy(
            src_ref=source,
            dst_ref=target,
            send_sem=sems.at[0, index],
            recv_sem=sems.at[1, index],
            device_id={"tile": me + by},
            device_id_type=MESH,
        )
        return copy, inside(me + by), inside(me - by)

    barrier = pltpu.get_barrier_semaphore()
    met = jnp.zeros((), jnp.int32)
    for by in [sign * by for by in range(1, reach + 1) for sign in (1, -1)]:

        @pl.when(inside(me + by))
        def _():
            pl.semaphore_signal(
                barrier, inc=1, device_id={"tile": me + by}, device_id_type=MESH
            )

        met = met + jnp.where(inside(me + by), 1, 0)
    pl.semaphore_wait(barrier, met)

    tells = [
        send(tables.at[0], tables.at[j], tell_sems, j, j) for j in range(1, reach + 1)
    ]
    tells.append(send(frame_count, counts, count_sems, 0, middle))
    moves = [
        send(measured.at[s], moved.at[s], moved_sems, s, middle) for s in range(cap)
    ]
    fetches = [
        [send(cuts.at[j, s], arrived.at[j, s], fetch_sems, s * (reach + 1) + j, middle - j) for j in others]
        for s in range(cap)
    ]
    gives = [
        [send(away.at[j, s], landed.at[j, s], give_sems, s * (reach + 1) + j, j - middle) for j in others]
        for s in range(cap)
    ]
    borders = [
        send(edges.at[1], halo.at[0], edge_sems, 0, 1),
        send(edges.at[0], halo.at[1], edge_sems, 1, -1),
    ]
    started = []

    def start(items):
        for copy, sends, takes in items:
            pl.when(sends)(copy.start)
            started.append((copy, sends))

    def arrive(items):
        for copy, sends, takes in items:
            pl.when(takes)(copy.wait_recv)

    def blank(items, wipe):
        for index, (copy, sends, takes) in enumerate(items):

            @pl.when(jnp.logical_not(takes))
            def _():
                wipe(index)

    def wipe_table(index):
        if index == reach:
            counts[0] = 0
        else:
            for s in range(cap):
                for item in range(3):
                    tables[index + 1, s, item] = 0

    def wipe(ref, *first):
        ref[first] = jnp.zeros(ref.shape[len(first):], ref.dtype)

    start(tells)
    start(moves)
    blank(tells, wipe_table)
    blank(moves, lambda s: wipe(moved, s))
    for s in range(cap):
        blank(fetches[s], lambda index: wipe(arrived, others[index], s))
        blank(gives[s], lambda index: wipe(landed, others[index], s))
    blank(borders, lambda index: wipe(halo, index))
    for j in range(reach + 1):
        for s in range(cap):
            for part in range(2):
                placed[j, s, part, 0] = jnp.zeros((strip, LANES), f32)
    loads[1].wait()
    table_rows(factors, 0, even_hi, even_lo)
    for item in strips:
        item.wait()
    arrive(tells)

    def first_block(j, s):
        return jnp.minimum(tables[j, s, 1] // LANES, blocks - lanes)

    for s in range(cap):
        for j in others + [middle]:
            block = first_block(j, s)
            shift = tables[j, s, 1] - block * LANES
            angle = tables[j, s, 2]
            for part in range(2):
                piece = jnp.concatenate(
                    [held[angle, part, block + lane] for lane in range(lanes)], 1
                )
                turned = pltpu.roll(piece, lax.rem(span - shift, span), 1)
                target = arrived if j == middle else cuts
                target[j, s, part] = turned[:, :side].astype(bf16)
        start(fetches[s])

    table_rows(factors, 1, odd_hi, odd_lo)
    for item in loads[2:5]:
        item.wait()
    cos_part, sin_part = cos_ref[...], sin_ref[...]
    stacked = jnp.concatenate([cos_part, sin_part], 0)
    joined = jnp.concatenate([cos_part, sin_part], 1)
    probe_re, probe_im = probe[0], probe[1]
    peak = jnp.max(probe_re * probe_re + probe_im * probe_im) + epsilon_term

    def left(re, im, sign):
        products = jnp.dot(
            stacked, jnp.concatenate([re, im], 1), preferred_element_type=f32
        )
        cc, ci = products[:side, :side], products[:side, side:]
        sc, si = products[side:, :side], products[side:, side:]
        return (cc - si, ci + sc) if sign > 0 else (cc + si, ci - sc)

    def right(re, im, sign):
        products = jnp.dot(
            jnp.concatenate([re, im], 0), joined, preferred_element_type=f32
        )
        rc, rs = products[:side, :side], products[:side, side:]
        ic, js = products[side:, :side], products[side:, side:]
        return (rc - js, rs + ic) if sign > 0 else (rc + js, ic - rs)

    for s in range(cap):
        arrive(fetches[s])
        offset = tables[middle, s, 0]
        patch = []
        for part in range(2):
            for j in range(reach + 1):
                window[j * strip : (j + 1) * strip] = arrived[j, s, part].astype(f32)
            turned = pltpu.roll(window[...], lax.rem(total - offset, total), 0)
            patch.append(turned[:side])
        wave_re = (probe_re * patch[0] - probe_im * patch[1]).astype(bf16)
        wave_im = (probe_re * patch[1] + probe_im * patch[0]).astype(bf16)
        half_re, half_im = left(wave_re, wave_im, 1)
        spec_re, spec_im = right(half_re.astype(bf16), half_im.astype(bf16), 1)
        amplitude = jnp.sqrt(spec_re * spec_re + spec_im * spec_im)
        if s == 0:
            arrive(moves)
        factor = moved[s].astype(f32) / jnp.maximum(amplitude, magnitude_floor) - 1.0
        back_re, back_im = left(
            (spec_re * factor).astype(bf16), (spec_im * factor).astype(bf16), -1
        )
        corr_re, corr_im = right(back_re.astype(bf16), back_im.astype(bf16), -1)
        live = s < counts[0]
        updates = (
            (probe_re * corr_re + probe_im * corr_im) / peak,
            (probe_re * corr_im - probe_im * corr_re) / peak,
        )
        for part in range(2):
            window[:side] = jnp.where(live, updates[part], 0.0)
            window[side:] = jnp.zeros((total - side, side), f32)
            turned = pltpu.roll(window[...], offset, 0)
            for j in range(reach + 1):
                piece = turned[j * strip : (j + 1) * strip]
                if j == middle:
                    own[s, part] = piece
                else:
                    away[j, s, part] = piece.astype(bf16)
        start(gives[s])

    pad = jnp.zeros((strip, LANES), f32)

    def shifted(source, j, s):
        shift = tables[j, s, 1] - first_block(j, s) * LANES
        for part in range(2):
            value = jnp.concatenate([source[part].astype(f32), pad], 1)
            turned = pltpu.roll(value, shift, 1)
            for lane in range(lanes):
                placed[j, s, part, lane + 1] = turned[:, lane * LANES : (lane + 1) * LANES]

    def add(items, rows):
        def chunk(block, _):
            for angle in range(angles):
                found = []
                for j, s in items:
                    near = block - first_block(j, s)
                    hit = (tables[j, s, 2] == angle) & (near >= 0) & (near < lanes)
                    found.append(jnp.where(hit, near + 1, 0))
                for part in range(2):
                    for row in rows:
                        value = held[angle, part, block, row]
                        for (j, s), index in zip(items, found):
                            value = value + placed[j, s, part, index, row]
                        held[angle, part, block, row] = value
            return 0

        lax.fori_loop(0, blocks, chunk, 0)

    for s in range(cap):
        shifted(own.at[s], middle, s)
    early = [(middle, s) for s in range(cap)]
    for s in range(cap - 1):
        arrive(gives[s])
        for j in others:
            shifted(landed.at[j, s], j, s)
        early += [(j, s) for j in others]
    add(early, [slice(0, strip)])
    arrive(gives[cap - 1])
    for j in others:
        shifted(landed.at[j, cap - 1], j, cap - 1)
    late = [(j, cap - 1) for j in others]
    add(late, [slice(0, GROUP), slice(strip - GROUP, strip)])
    for angle in range(angles):
        for part in range(2):
            for block in range(blocks):
                where = slice(block * LANES, (block + 1) * LANES)
                edges[0, angle, part, :, where] = held[angle, part, block, :1]
                edges[1, angle, part, :, where] = held[angle, part, block, strip - 1 :]
    start(borders)
    add(late, [slice(GROUP, strip - GROUP)])
    arrive(borders)
    for copy, sends in started:
        pl.when(sends)(copy.wait_send)


def mirror(value):
    side = value.shape[1]
    rows = lax.broadcasted_iota(jnp.int32, (side, side), 0)
    columns = lax.broadcasted_iota(jnp.int32, (side, side), 1)
    swap = jnp.where(rows + columns == side - 1, 1.0, 0.0).astype(bf16)
    total = None
    for _ in range(3):
        piece = value.astype(bf16)
        value = value - piece.astype(f32)
        term = jnp.dot(piece, swap, preferred_element_type=f32)
        total = term if total is None else total + term
    return total


def split_store(value, high, low, columns):
    rounded = value.astype(bf16)
    high[:, columns] = rounded
    low[:, columns] = (value - rounded.astype(f32)).astype(bf16)


def bond(a_re, a_im, b_re, b_im):
    cross = a_re * b_im - a_im * b_re
    power = a_re * a_re + a_im * a_im + b_re * b_re + b_im * b_im + soften_term
    return 2.0 * cross / power


def forward_kernel(
    field, halo, even_hi, even_lo, odd_hi, odd_lo, local, extra,
    updated, out, ends, source, xeh, xel, xoh, xol, sems,
):
    angles, _, strip, width = updated.shape
    copies = [
        pltpu.make_async_copy(
            field.at[:, :, block],
            updated.at[:, :, :, block * LANES : (block + 1) * LANES],
            sems.at[block],
        )
        for block in range(width // LANES)
    ]
    for copy in copies:
        copy.start()

    def rows_of(angle, part, rows):
        return jnp.concatenate(
            [field[angle, part, block, rows] for block in range(width // LANES)], 1
        )

    half = width // 2
    block = GROUP * 2
    columns = lax.broadcasted_iota(jnp.int32, (block, width), 1)
    for angle in range(angles):
        for first in range(0, strip, block):
            here, up, down, left = [], [], [], []
            for part in range(2):
                body = rows_of(angle, part, slice(first, first + block))
                before = (
                    halo[0, angle, part]
                    if first == 0
                    else rows_of(angle, part, slice(first - 1, first))
                )
                after = (
                    halo[1, angle, part]
                    if first + block == strip
                    else rows_of(angle, part, slice(first + block, first + block + 1))
                )
                here.append(body)
                up.append(jnp.concatenate([before, body[:-1]], 0))
                down.append(jnp.concatenate([body[1:], after], 0))
                left.append(jnp.where(columns == 0, 0.0, pltpu.roll(body, 1, 1)))
            row_up = bond(*up, *here)
            row_down = bond(*here, *down)
            col_left = bond(*left, *here)
            col_right = jnp.where(
                columns == width - 1, 0.0, pltpu.roll(col_left, width - 1, 1)
            )
            source[angle * strip + first : angle * strip + first + block] = -(
                row_down - row_up + col_right - col_left
            )
    for first in range(0, half, TILE):
        near = source[:, first : first + TILE]
        far = mirror(source[:, width - first - TILE : width - first])
        where = slice(first, first + TILE)
        split_store(near + far, xeh, xel, where)
        split_store(near - far, xoh, xol, where)
    for base, high, low, table_hi, table_lo in (
        (0, xeh, xel, even_hi, even_lo),
        (half, xoh, xol, odd_hi, odd_lo),
    ):
        for first in range(0, half, TILE):
            where = slice(first, first + TILE)
            source[:, base + first : base + first + TILE] = (
                jnp.dot(high[...], table_hi[:, where], preferred_element_type=f32)
                + jnp.dot(low[...], table_hi[:, where], preferred_element_type=f32)
                + jnp.dot(high[...], table_lo[:, where], preferred_element_type=f32)
            )
    groups = strip // GROUP

    def scan(chunk, _):
        where = pl.ds(pl.multiple_of(chunk * LANES, LANES), LANES)
        gain = extra[0:1, where]
        for angle in range(angles):
            value = source[angle * strip : (angle + 1) * strip, where]
            value = value.reshape(groups, GROUP, LANES)
            fall, rise = value, value
            for index, by in enumerate((1, 2, 4)):
                fall = fall + local[index, :, where][None] * pltpu.roll(fall, by, 1)
                rise = rise + local[4 + index, :, where][None] * pltpu.roll(rise, GROUP - by, 1)
            falls, carry = [], None
            for group in range(groups):
                item = fall[group]
                if carry is not None:
                    item = item + local[3, :, where] * carry
                carry = item[GROUP - 1 :]
                falls.append(item)
            ends[chunk, angle : angle + 1] = carry
            rises, carry = [None] * groups, None
            for group in reversed(range(groups)):
                item = rise[group]
                if carry is not None:
                    item = item + local[7, :, where] * carry
                carry = item[:1]
                rises[group] = item
            ends[chunk, angles + angle : angles + angle + 1] = carry
            for group in range(groups):
                out[angle, group * GROUP : (group + 1) * GROUP, where] = gain * (
                    falls[group] + rises[group] - value[group]
                )
        return 0

    lax.fori_loop(0, width // LANES, scan, 0)
    for copy in copies:
        copy.wait()


def inverse_kernel(
    value, incoming, even_hi, even_lo, odd_hi, odd_lo, local, extra, out, xh, xl
):
    angles, strip, width = value.shape
    half = width // 2
    groups = strip // GROUP

    def enter(chunk, _):
        where = pl.ds(pl.multiple_of(chunk * LANES, LANES), LANES)
        for angle in range(angles):
            fall = incoming[chunk, angle : angle + 1]
            rise = incoming[chunk, angles + angle : angles + angle + 1]
            step = extra[2:3, where]
            falls, rises = [], []
            for group in range(groups):
                falls.append(fall)
                rises.append(rise)
                fall = fall * step
                rise = rise * step
            for pair in range(0, groups, 2):
                rows = []
                for group in (pair, pair + 1):
                    rows.append(
                        value[angle, group * GROUP : (group + 1) * GROUP, where]
                        + local[3, :, where] * falls[group]
                        + local[7, :, where] * rises[groups - 1 - group]
                    )
                item = jnp.concatenate(rows, 0)
                rounded = item.astype(bf16)
                start = angle * strip + pair * GROUP
                xh[start : start + 2 * GROUP, where] = rounded
                xl[start : start + 2 * GROUP, where] = (item - rounded.astype(f32)).astype(bf16)
        return 0

    lax.fori_loop(0, width // LANES, enter, 0)
    last = (((1,), (1,)), ((), ()))
    for first in range(0, half, TILE):
        where = slice(first, first + TILE)
        parts = []
        for base, table_hi, table_lo in ((0, even_hi, even_lo), (half, odd_hi, odd_lo)):
            high = xh[:, base : base + half]
            low = xl[:, base : base + half]
            parts.append(
                lax.dot_general(high, table_hi[where], last, preferred_element_type=f32)
                + lax.dot_general(low, table_hi[where], last, preferred_element_type=f32)
                + lax.dot_general(high, table_lo[where], last, preferred_element_type=f32)
            )
        near = parts[0] + parts[1]
        far = mirror(parts[0] - parts[1])
        for angle in range(angles):
            rows = slice(angle * strip, (angle + 1) * strip)
            out[angle, :, where] = near[rows]
            out[angle, :, width - first - TILE : width - first] = far[rows]


def body(object_field, probe, measured, frame_table, frame_count):
    angles, _, strip, width = object_field.shape
    side = probe.shape[1]
    cap = measured.shape[0]
    half = width // 2
    reach = side // strip
    rows = angles * strip
    strips = lax.axis_size("tile")
    blocks = width // LANES
    shape = jax.ShapeDtypeStruct

    pieces = (reach + 1) * cap
    local, powers, extra = decay_tables(width, strip)

    def by_block(table):
        return jnp.asarray(table.reshape(-1, blocks, LANES).transpose(1, 0, 2))

    factors = cosine_factors(width)
    table = (reach + 1, cap, 2, strip, side)
    held, halo, *half_tables = pl.pallas_call(
        update_kernel,
        out_shape=[
            shape((angles, 2, blocks, strip, LANES), f32),
            shape((2, angles, 2, 1, width), f32),
        ]
        + [shape((half, half), bf16)] * 4,
        in_specs=[smem] * 2 + [hbm] * 6,
        out_specs=[vmem] * 6,
        scratch_shapes=[
            pltpu.SMEM((reach + 1, cap, 3), jnp.int32),
            pltpu.SMEM((1,), jnp.int32),
            pltpu.VMEM(probe.shape, f32),
            pltpu.VMEM((side, side), bf16),
            pltpu.VMEM((side, side), bf16),
            pltpu.VMEM(factors.shape, f32),
            pltpu.VMEM(measured.shape, bf16),
            pltpu.VMEM(table, bf16),
            pltpu.VMEM(table, bf16),
            pltpu.VMEM(table, bf16),
            pltpu.VMEM(table, bf16),
            pltpu.VMEM((cap, 2, strip, side), f32),
            pltpu.VMEM((reach + 1, cap, 2, side // LANES + 2, strip, LANES), f32),
            pltpu.VMEM(((reach + 1) * strip, side), f32),
            pltpu.VMEM((2, angles, 2, 1, width), f32),
            pltpu.SemaphoreType.DMA((5 + blocks,)),
            pltpu.SemaphoreType.DMA((2, reach + 1)),
            pltpu.SemaphoreType.DMA((2, 1)),
            pltpu.SemaphoreType.DMA((2, cap)),
            pltpu.SemaphoreType.DMA((2, pieces)),
            pltpu.SemaphoreType.DMA((2, pieces)),
            pltpu.SemaphoreType.DMA((2, 2)),
        ],
        compiler_params=params(collective_id=0, has_side_effects=True),
        cost_estimate=cost(20),
        name="update",
    )(frame_table, frame_count, object_field, probe, measured, *fourier_tables(side), factors)

    updated, solved, ends = pl.pallas_call(
        forward_kernel,
        out_shape=[
            shape(object_field.shape, f32),
            shape((angles, strip, width), f32),
            shape((blocks, 2 * angles, LANES), f32),
        ],
        in_specs=[vmem] * 8,
        out_specs=[hbm, vmem, vmem],
        scratch_shapes=[pltpu.VMEM((rows, width), f32)]
        + [pltpu.VMEM((rows, half), bf16)] * 4
        + [pltpu.SemaphoreType.DMA((blocks,))],
        compiler_params=params(),
        cost_estimate=cost(9),
        name="forward",
    )(held, halo, *half_tables, local, extra)
    incoming = pl.pallas_call(
        join_kernel,
        out_shape=shape(ends.shape, f32),
        in_specs=[vmem] * 3,
        out_specs=vmem,
        scratch_shapes=[
            pltpu.VMEM((strips, 2 * angles, LANES), f32),
            pltpu.VMEM((strips, 2 * angles, LANES), f32),
            pltpu.SemaphoreType.DMA((blocks,)),
            pltpu.SemaphoreType.DMA((strips,)),
            pltpu.SemaphoreType.DMA((strips,)),
            pltpu.SemaphoreType.DMA((blocks,)),
        ],
        compiler_params=params(collective_id=4, has_side_effects=True),
        cost_estimate=cost(10),
        name="join",
    )(ends, by_block(powers), by_block(extra))
    phase_map = pl.pallas_call(
        inverse_kernel,
        out_shape=shape((angles, strip, width), f32),
        in_specs=[vmem] * 8,
        out_specs=vmem,
        scratch_shapes=[
            pltpu.VMEM((rows, width), bf16),
            pltpu.VMEM((rows, width), bf16),
        ],
        compiler_params=params(),
        cost_estimate=cost(6),
        name="inverse",
    )(solved, incoming, *half_tables, local, extra)
    return (updated, phase_map)


def solution(mesh):
    return jax.shard_map(
        body,
        mesh=mesh,
        in_specs=(
            P("group", None, "tile", None),
            P(),
            P(("group", "tile"), None, None),
            P(("group", "tile"), None),
            P(("group", "tile")),
        ),
        out_specs=(P("group", None, "tile", None), P("group", "tile", None)),
        check_vma=False,
    )
```

```python
import functools
import math

import numpy as np
import jax
import jax.numpy as jnp
from jax import lax
from jax.experimental import pallas as pl
from jax.experimental.pallas import tpu as pltpu
from jax.sharding import PartitionSpec as P

magnitude_floor = 0.5
soften_term = 0.5
screen_term = 0.0001
epsilon_term = 1e-06
f32 = jnp.float32
bf16 = jnp.bfloat16
LANES = 128
GROUP = 8
TILE = 256
VMEM_BYTES = 30 * 1024 * 1024
MESH = pl.DeviceIdType.MESH
vmem = pl.BlockSpec(memory_space=pltpu.VMEM)
smem = pl.BlockSpec(memory_space=pltpu.SMEM)
hbm = pl.BlockSpec(memory_space=pltpu.HBM)


def cost(micros):
    return pl.CostEstimate(
        flops=0, bytes_accessed=int(micros * 3_000_000), transcendentals=0
    )


def params(**more):
    return pltpu.CompilerParams(vmem_limit_bytes=VMEM_BYTES, **more)


def join_kernel(ends, powers, extra, out, heard, told, up_sems, in_sems, down_sems, back_sems):
    count = lax.axis_size("tile")
    me = lax.axis_index("tile")
    blocks, lines = ends.shape[0], ends.shape[1]
    angles = lines // 2
    stride = count // blocks
    mine = me // stride
    joins = lax.rem(me, stride) == 0
    barrier = pltpu.get_barrier_semaphore()

    def greet(by, _):
        pl.semaphore_signal(
            barrier, inc=1, device_id={"tile": lax.rem(me + by, count)}, device_id_type=MESH
        )
        return 0

    lax.fori_loop(1, count, greet, 0)
    pl.semaphore_wait(barrier, count - 1)

    def up(by):
        block = lax.rem(mine + by, blocks)
        return pltpu.make_async_remote_copy(
            src_ref=ends.at[block],
            dst_ref=heard.at[me],
            send_sem=up_sems.at[block],
            recv_sem=in_sems.at[me],
            device_id={"tile": block * stride},
            device_id_type=MESH,
        )

    def came(other):
        return pltpu.make_async_remote_copy(
            src_ref=ends.at[0],
            dst_ref=heard.at[other],
            send_sem=up_sems.at[0],
            recv_sem=in_sems.at[other],
            device_id={"tile": other},
            device_id_type=MESH,
        )

    def down(other):
        return pltpu.make_async_remote_copy(
            src_ref=told.at[other],
            dst_ref=out.at[mine],
            send_sem=down_sems.at[other],
            recv_sem=back_sems.at[mine],
            device_id={"tile": other},
            device_id_type=MESH,
        )

    def answered(block):
        return pltpu.make_async_remote_copy(
            src_ref=told.at[0],
            dst_ref=out.at[block],
            send_sem=down_sems.at[0],
            recv_sem=back_sems.at[block],
            device_id={"tile": block * stride},
            device_id_type=MESH,
        )

    def each(limit, step):
        def run(index, _):
            step(index)
            return 0

        lax.fori_loop(0, limit, run, 0)

    for by in range(blocks):
        pl.when(lax.rem(mine + by, blocks) * stride != me)(lambda: up(by).start())

    @pl.when(joins)
    def _():
        heard[me] = ends[mine]
        for by in range(1, count):
            came(lax.rem(me + by, count)).wait_recv()
        step = powers[mine, 1:2]
        whole = powers[mine, count : count + 1]
        closing = extra[mine, 1:2]
        gain = extra[mine, 0:1]
        wall = heard[count - 1, angles:]
        floor = heard[0, :angles]
        for strip in range(1, count):
            floor = floor * step + heard[strip, :angles]
            wall = wall * step + heard[count - 1 - strip, angles:]
        enter = (wall + whole * floor) * closing
        leave = (floor + whole * wall) * closing
        for strip in range(count):
            told[strip, :angles] = enter * gain
            enter = enter * step + heard[strip, :angles]
            back = count - 1 - strip
            told[back, angles:] = leave * gain
            leave = leave * step + heard[back, angles:]
        for by in range(1, count):
            down(lax.rem(me + by, count)).start()
        out[mine] = told[me]

    for by in range(blocks):
        block = lax.rem(mine + by, blocks)
        pl.when(block * stride != me)(lambda: answered(block).wait_recv())
        pl.when(block * stride != me)(lambda: up(by).wait_send())

    @pl.when(joins)
    def _():
        for by in range(1, count):
            down(lax.rem(me + by, count)).wait_send()


def fourier_tables(side):
    indices = np.arange(side)
    products = indices[:, None] * indices[None, :] % side
    phases = products.astype(np.float64) * (-2.0 * math.pi / side)
    scale = 1.0 / math.sqrt(side)
    return (
        jnp.asarray(np.cos(phases) * scale, f32).astype(bf16),
        jnp.asarray(np.sin(phases) * scale, f32).astype(bf16),
    )


def cosine_factors(grid_side):
    half = grid_side // 2
    step = 32
    out = []
    for odd in (0, 1):
        freqs = 2 * np.arange(half) + odd
        scale = np.where(freqs == 0, math.sqrt(1.0 / grid_side), math.sqrt(2.0 / grid_side))
        coarse = (2 * step * np.arange(half // step)[:, None] * freqs[None, :]) % (4 * grid_side)
        fine = ((2 * np.arange(step)[:, None] + 1) * freqs[None, :]) % (4 * grid_side)
        unit = math.pi / (2 * grid_side)
        out.append(
            np.stack(
                [
                    np.cos(coarse * unit) * scale,
                    np.sin(coarse * unit) * scale,
                    np.cos(fine * unit),
                    np.sin(fine * unit),
                ]
            )
        )
    return jnp.asarray(np.stack(out), f32)


def decay_tables(grid_side, strip_rows):
    half = grid_side // 2
    freqs = np.concatenate([2 * np.arange(half), 2 * np.arange(half) + 1]).astype(np.float64)
    shift = screen_term + 2.0 - 2.0 * np.cos(freqs * math.pi / grid_side)
    rate = 2.0 * np.arcsinh(np.sqrt(shift) / 2.0)
    gain = 1.0 / (2.0 * np.sinh(rate))
    rows = np.arange(GROUP)[:, None]
    down = [np.where(rows >= s, np.exp(-s * rate), 0.0) for s in (1, 2, 4)]
    up = [np.where(rows < GROUP - s, np.exp(-s * rate), 0.0) for s in (1, 2, 4)]
    down.append(np.exp(-(rows + 1) * rate))
    up.append(np.exp(-(GROUP - rows) * rate))
    local = np.stack(down + up)
    strips = grid_side // strip_rows
    powers = np.exp(-strip_rows * np.arange(strips + 1)[:, None] * rate)
    extra = np.stack(
        [gain, 1.0 / (1.0 - np.exp(-2.0 * grid_side * rate)), np.exp(-GROUP * rate)]
        + [rate * 0.0] * 5
    )
    return local.astype(np.float32), powers.astype(np.float32), extra.astype(np.float32)


def table_rows(factors, part, high, low):
    step = factors.shape[2]

    def run(block, _):
        rows = pl.ds(pl.multiple_of(block * step, step), step)
        value = (
            factors[part, 0, pl.ds(block, 1)] * factors[part, 2]
            - factors[part, 1, pl.ds(block, 1)] * factors[part, 3]
        )
        rounded = value.astype(bf16)
        high[rows] = rounded
        low[rows] = (value - rounded.astype(f32)).astype(bf16)
        return 0

    lax.fori_loop(0, high.shape[0] // step, run, 0)


def window_start(column, width, span):
    return jnp.minimum(column // LANES, (width - span) // LANES) * LANES


def update_kernel(
    frame_count, frame_table, field, probe_in, measured, cos_in, sin_in, factors_in,
    held, halo, even_hi, even_lo, odd_hi, odd_lo,
    tables, counts, probe, cos_ref, sin_ref, factors, moved, cuts, arrived, away, landed,
    own, placed, window, edges,
    load_sems, tell_sems, count_sems, moved_sems, fetch_sems, give_sems, edge_sems,
):
    count = lax.axis_size("tile")
    me = lax.axis_index("tile")
    angles, _, strip, width = field.shape
    cap, side = measured.shape[0], measured.shape[1]
    span = side + LANES
    lanes = span // LANES
    blocks = width // LANES
    reach = tables.shape[0] - 1
    middle = reach // 2
    total = (reach + 1) * strip
    others = [j for j in range(reach + 1) if j != middle]

    def inside(place):
        return (place >= 0) & (place < count)

    def load(index, source, target):
        return pltpu.make_async_copy(source, target, load_sems.at[index])

    loads = [
        load(0, frame_table, tables.at[0]),
        load(1, factors_in, factors),
        load(2, probe_in, probe),
        load(3, cos_in, cos_ref),
        load(4, sin_in, sin_ref),
    ]
    strips = [
        load(5 + block, field.at[:, :, :, block * LANES : (block + 1) * LANES], held.at[:, :, block])
        for block in range(blocks)
    ]
    for item in loads[:2] + strips + loads[2:5]:
        item.start()

    def send(source, target, sems, index, by):
        copy = pltpu.make_async_remote_copy(
            src_ref=source,
            dst_ref=target,
            send_sem=sems.at[0, index],
            recv_sem=sems.at[1, index],
            device_id={"tile": me + by},
            device_id_type=MESH,
        )
        return copy, inside(me + by), inside(me - by)

    barrier = pltpu.get_barrier_semaphore()
    met = jnp.zeros((), jnp.int32)
    for by in [sign * by for by in range(1, reach + 1) for sign in (1, -1)]:

        @pl.when(inside(me + by))
        def _():
            pl.semaphore_signal(
                barrier, inc=1, device_id={"tile": me + by}, device_id_type=MESH
            )

        met = met + jnp.where(inside(me + by), 1, 0)
    pl.semaphore_wait(barrier, met)

    tells = [
        send(tables.at[0], tables.at[j], tell_sems, j, j) for j in range(1, reach + 1)
    ]
    tells.append(send(frame_count, counts, count_sems, 0, middle))
    moves = [
        send(measured.at[s], moved.at[s], moved_sems, s, middle) for s in range(cap)
    ]
    fetches = [
        [send(cuts.at[j, s], arrived.at[j, s], fetch_sems, s * (reach + 1) + j, middle - j) for j in others]
        for s in range(cap)
    ]
    gives = [
        [send(away.at[j, s], landed.at[j, s], give_sems, s * (reach + 1) + j, j - middle) for j in others]
        for s in range(cap)
    ]
    borders = [
        send(edges.at[1], halo.at[0], edge_sems, 0, 1),
        send(edges.at[0], halo.at[1], edge_sems, 1, -1),
    ]
    started = []

    def start(items):
        for copy, sends, takes in items:
            pl.when(sends)(copy.start)
            started.append((copy, sends))

    def arrive(items):
        for copy, sends, takes in items:
            pl.when(takes)(copy.wait_recv)

    def blank(items, wipe):
        for index, (copy, sends, takes) in enumerate(items):

            @pl.when(jnp.logical_not(takes))
            def _():
                wipe(index)

    def wipe_table(index):
        if index == reach:
            counts[0] = 0
        else:
            for s in range(cap):
                for item in range(3):
                    tables[index + 1, s, item] = 0

    def wipe(ref, *first):
        ref[first] = jnp.zeros(ref.shape[len(first):], ref.dtype)

    loads[0].wait()
    start(tells)
    start(moves)
    blank(tells, wipe_table)
    blank(moves, lambda s: wipe(moved, s))
    for s in range(cap):
        blank(fetches[s], lambda index: wipe(arrived, others[index], s))
        blank(gives[s], lambda index: wipe(landed, others[index], s))
    blank(borders, lambda index: wipe(halo, index))
    for j in range(reach + 1):
        for s in range(cap):
            for part in range(2):
                placed[j, s, part, 0] = jnp.zeros((strip, LANES), f32)
    loads[1].wait()
    table_rows(factors, 0, even_hi, even_lo)
    for item in strips:
        item.wait()
    arrive(tells)

    def first_block(j, s):
        return jnp.minimum(tables[j, s, 1] // LANES, blocks - lanes)

    for s in range(cap):
        for j in others + [middle]:
            block = first_block(j, s)
            shift = tables[j, s, 1] - block * LANES
            angle = tables[j, s, 2]
            for part in range(2):
                piece = jnp.concatenate(
                    [held[angle, part, block + lane] for lane in range(lanes)], 1
                )
                turned = pltpu.roll(piece, lax.rem(span - shift, span), 1)
                target = arrived if j == middle else cuts
                target[j, s, part] = turned[:, :side].astype(bf16)
        start(fetches[s])

    table_rows(factors, 1, odd_hi, odd_lo)
    for item in loads[2:5]:
        item.wait()
    cos_part, sin_part = cos_ref[...], sin_ref[...]
    stacked = jnp.concatenate([cos_part, sin_part], 0)
    joined = jnp.concatenate([cos_part, sin_part], 1)
    probe_re, probe_im = probe[0], probe[1]
    peak = jnp.max(probe_re * probe_re + probe_im * probe_im) + epsilon_term

    def left(re, im, sign):
        products = jnp.dot(
            stacked, jnp.concatenate([re, im], 1), preferred_element_type=f32
        )
        cc, ci = products[:side, :side], products[:side, side:]
        sc, si = products[side:, :side], products[side:, side:]
        return (cc - si, ci + sc) if sign > 0 else (cc + si, ci - sc)

    def right(re, im, sign):
        products = jnp.dot(
            jnp.concatenate([re, im], 0), joined, preferred_element_type=f32
        )
        rc, rs = products[:side, :side], products[:side, side:]
        ic, js = products[side:, :side], products[side:, side:]
        return (rc - js, rs + ic) if sign > 0 else (rc + js, ic - rs)

    for s in range(cap):
        arrive(fetches[s])
        offset = tables[middle, s, 0]
        patch = []
        for part in range(2):
            for j in range(reach + 1):
                window[j * strip : (j + 1) * strip] = arrived[j, s, part].astype(f32)
            turned = pltpu.roll(window[...], lax.rem(total - offset, total), 0)
            patch.append(turned[:side])
        wave_re = (probe_re * patch[0] - probe_im * patch[1]).astype(bf16)
        wave_im = (probe_re * patch[1] + probe_im * patch[0]).astype(bf16)
        half_re, half_im = left(wave_re, wave_im, 1)
        spec_re, spec_im = right(half_re.astype(bf16), half_im.astype(bf16), 1)
        amplitude = jnp.sqrt(spec_re * spec_re + spec_im * spec_im)
        if s == 0:
            arrive(moves)
        factor = moved[s].astype(f32) / jnp.maximum(amplitude, magnitude_floor) - 1.0
        back_re, back_im = left(
            (spec_re * factor).astype(bf16), (spec_im * factor).astype(bf16), -1
        )
        corr_re, corr_im = right(back_re.astype(bf16), back_im.astype(bf16), -1)
        live = s < counts[0]
        updates = (
            (probe_re * corr_re + probe_im * corr_im) / peak,
            (probe_re * corr_im - probe_im * corr_re) / peak,
        )
        for part in range(2):
            window[:side] = jnp.where(live, updates[part], 0.0)
            window[side:] = jnp.zeros((total - side, side), f32)
            turned = pltpu.roll(window[...], offset, 0)
            for j in range(reach + 1):
                piece = turned[j * strip : (j + 1) * strip]
                if j == middle:
                    own[s, part] = piece
                else:
                    away[j, s, part] = piece.astype(bf16)
        start(gives[s])

    pad = jnp.zeros((strip, LANES), f32)

    def shifted(source, j, s):
        shift = tables[j, s, 1] - first_block(j, s) * LANES
        for part in range(2):
            value = jnp.concatenate([source[part].astype(f32), pad], 1)
            turned = pltpu.roll(value, shift, 1)
            for lane in range(lanes):
                placed[j, s, part, lane + 1] = turned[:, lane * LANES : (lane + 1) * LANES]

    def add(items, rows):
        def chunk(block, _):
            for angle in range(angles):
                found = []
                for j, s in items:
                    near = block - first_block(j, s)
                    hit = (tables[j, s, 2] == angle) & (near >= 0) & (near < lanes)
                    found.append(jnp.where(hit, near + 1, 0))
                for part in range(2):
                    for row in rows:
                        value = held[angle, part, block, row]
                        for (j, s), index in zip(items, found):
                            value = value + placed[j, s, part, index, row]
                        held[angle, part, block, row] = value
            return 0

        lax.fori_loop(0, blocks, chunk, 0)

    for s in range(cap):
        shifted(own.at[s], middle, s)
    early = [(middle, s) for s in range(cap)]
    for s in range(cap - 1):
        arrive(gives[s])
        for j in others:
            shifted(landed.at[j, s], j, s)
        early += [(j, s) for j in others]
    add(early, [slice(0, strip)])
    arrive(gives[cap - 1])
    for j in others:
        shifted(landed.at[j, cap - 1], j, cap - 1)
    late = [(j, cap - 1) for j in others]
    add(late, [slice(0, GROUP), slice(strip - GROUP, strip)])
    for angle in range(angles):
        for part in range(2):
            for block in range(blocks):
                where = slice(block * LANES, (block + 1) * LANES)
                edges[0, angle, part, :, where] = held[angle, part, block, :1]
                edges[1, angle, part, :, where] = held[angle, part, block, strip - 1 :]
    start(borders)
    add(late, [slice(GROUP, strip - GROUP)])
    arrive(borders)
    for copy, sends in started:
        pl.when(sends)(copy.wait_send)


def mirror(value):
    side = value.shape[1]
    rows = lax.broadcasted_iota(jnp.int32, (side, side), 0)
    columns = lax.broadcasted_iota(jnp.int32, (side, side), 1)
    swap = jnp.where(rows + columns == side - 1, 1.0, 0.0).astype(bf16)
    total = None
    for _ in range(3):
        piece = value.astype(bf16)
        value = value - piece.astype(f32)
        term = jnp.dot(piece, swap, preferred_element_type=f32)
        total = term if total is None else total + term
    return total


def split_store(value, high, low, columns):
    rounded = value.astype(bf16)
    high[:, columns] = rounded
    low[:, columns] = (value - rounded.astype(f32)).astype(bf16)


def bond(a_re, a_im, b_re, b_im):
    cross = a_re * b_im - a_im * b_re
    power = a_re * a_re + a_im * a_im + b_re * b_re + b_im * b_im + soften_term
    return 2.0 * cross / power


def forward_kernel(
    field, halo, even_hi, even_lo, odd_hi, odd_lo, local, extra,
    updated, out, ends, source, xeh, xel, xoh, xol, sems,
):
    angles, _, strip, width = updated.shape
    copies = [
        pltpu.make_async_copy(
            field.at[:, :, block],
            updated.at[:, :, :, block * LANES : (block + 1) * LANES],
            sems.at[block],
        )
        for block in range(width // LANES)
    ]
    for copy in copies:
        copy.start()

    def rows_of(angle, part, rows):
        return jnp.concatenate(
            [field[angle, part, block, rows] for block in range(width // LANES)], 1
        )

    half = width // 2
    block = GROUP * 2
    columns = lax.broadcasted_iota(jnp.int32, (block, width), 1)
    for angle in range(angles):
        for first in range(0, strip, block):
            here, up, down, left = [], [], [], []
            for part in range(2):
                body = rows_of(angle, part, slice(first, first + block))
                before = (
                    halo[0, angle, part]
                    if first == 0
                    else rows_of(angle, part, slice(first - 1, first))
                )
                after = (
                    halo[1, angle, part]
                    if first + block == strip
                    else rows_of(angle, part, slice(first + block, first + block + 1))
                )
                here.append(body)
                up.append(jnp.concatenate([before, body[:-1]], 0))
                down.append(jnp.concatenate([body[1:], after], 0))
                left.append(jnp.where(columns == 0, 0.0, pltpu.roll(body, 1, 1)))
            row_up = bond(*up, *here)
            row_down = bond(*here, *down)
            col_left = bond(*left, *here)
            col_right = jnp.where(
                columns == width - 1, 0.0, pltpu.roll(col_left, width - 1, 1)
            )
            source[angle * strip + first : angle * strip + first + block] = -(
                row_down - row_up + col_right - col_left
            )
    for first in range(0, half, TILE):
        near = source[:, first : first + TILE]
        far = mirror(source[:, width - first - TILE : width - first])
        where = slice(first, first + TILE)
        split_store(near + far, xeh, xel, where)
        split_store(near - far, xoh, xol, where)
    for base, high, low, table_hi, table_lo in (
        (0, xeh, xel, even_hi, even_lo),
        (half, xoh, xol, odd_hi, odd_lo),
    ):
        for first in range(0, half, TILE):
            where = slice(first, first + TILE)
            source[:, base + first : base + first + TILE] = (
                jnp.dot(high[...], table_hi[:, where], preferred_element_type=f32)
                + jnp.dot(low[...], table_hi[:, where], preferred_element_type=f32)
                + jnp.dot(high[...], table_lo[:, where], preferred_element_type=f32)
            )
    groups = strip // GROUP

    def scan(chunk, _):
        where = pl.ds(pl.multiple_of(chunk * LANES, LANES), LANES)
        gain = extra[0:1, where]
        for angle in range(angles):
            value = source[angle * strip : (angle + 1) * strip, where]
            value = value.reshape(groups, GROUP, LANES)
            fall, rise = value, value
            for index, by in enumerate((1, 2, 4)):
                fall = fall + local[index, :, where][None] * pltpu.roll(fall, by, 1)
                rise = rise + local[4 + index, :, where][None] * pltpu.roll(rise, GROUP - by, 1)
            falls, carry = [], None
            for group in range(groups):
                item = fall[group]
                if carry is not None:
                    item = item + local[3, :, where] * carry
                carry = item[GROUP - 1 :]
                falls.append(item)
            ends[chunk, angle : angle + 1] = carry
            rises, carry = [None] * groups, None
            for group in reversed(range(groups)):
                item = rise[group]
                if carry is not None:
                    item = item + local[7, :, where] * carry
                carry = item[:1]
                rises[group] = item
            ends[chunk, angles + angle : angles + angle + 1] = carry
            for group in range(groups):
                out[angle, group * GROUP : (group + 1) * GROUP, where] = gain * (
                    falls[group] + rises[group] - value[group]
                )
        return 0

    lax.fori_loop(0, width // LANES, scan, 0)
    for copy in copies:
        copy.wait()


def inverse_kernel(
    value, incoming, even_hi, even_lo, odd_hi, odd_lo, local, extra, out, xh, xl
):
    angles, strip, width = value.shape
    half = width // 2
    groups = strip // GROUP

    def enter(chunk, _):
        where = pl.ds(pl.multiple_of(chunk * LANES, LANES), LANES)
        for angle in range(angles):
            fall = incoming[chunk, angle : angle + 1]
            rise = incoming[chunk, angles + angle : angles + angle + 1]
            step = extra[2:3, where]
            falls, rises = [], []
            for group in range(groups):
                falls.append(fall)
                rises.append(rise)
                fall = fall * step
                rise = rise * step
            for pair in range(0, groups, 2):
                rows = []
                for group in (pair, pair + 1):
                    rows.append(
                        value[angle, group * GROUP : (group + 1) * GROUP, where]
                        + local[3, :, where] * falls[group]
                        + local[7, :, where] * rises[groups - 1 - group]
                    )
                item = jnp.concatenate(rows, 0)
                rounded = item.astype(bf16)
                start = angle * strip + pair * GROUP
                xh[start : start + 2 * GROUP, where] = rounded
                xl[start : start + 2 * GROUP, where] = (item - rounded.astype(f32)).astype(bf16)
        return 0

    lax.fori_loop(0, width // LANES, enter, 0)
    last = (((1,), (1,)), ((), ()))
    for first in range(0, half, TILE):
        where = slice(first, first + TILE)
        parts = []
        for base, table_hi, table_lo in ((0, even_hi, even_lo), (half, odd_hi, odd_lo)):
            high = xh[:, base : base + half]
            low = xl[:, base : base + half]
            parts.append(
                lax.dot_general(high, table_hi[where], last, preferred_element_type=f32)
                + lax.dot_general(low, table_hi[where], last, preferred_element_type=f32)
                + lax.dot_general(high, table_lo[where], last, preferred_element_type=f32)
            )
        near = parts[0] + parts[1]
        far = mirror(parts[0] - parts[1])
        for angle in range(angles):
            rows = slice(angle * strip, (angle + 1) * strip)
            out[angle, :, where] = near[rows]
            out[angle, :, width - first - TILE : width - first] = far[rows]


def body(object_field, probe, measured, frame_table, frame_count):
    angles, _, strip, width = object_field.shape
    side = probe.shape[1]
    cap = measured.shape[0]
    half = width // 2
    reach = side // strip
    rows = angles * strip
    strips = lax.axis_size("tile")
    blocks = width // LANES
    shape = jax.ShapeDtypeStruct

    pieces = (reach + 1) * cap
    local, powers, extra = decay_tables(width, strip)

    def by_block(table):
        return jnp.asarray(table.reshape(-1, blocks, LANES).transpose(1, 0, 2))

    factors = cosine_factors(width)
    table = (reach + 1, cap, 2, strip, side)
    held, halo, *half_tables = pl.pallas_call(
        update_kernel,
        out_shape=[
            shape((angles, 2, blocks, strip, LANES), f32),
            shape((2, angles, 2, 1, width), f32),
        ]
        + [shape((half, half), bf16)] * 4,
        in_specs=[smem] + [hbm] * 7,
        out_specs=[vmem] * 6,
        scratch_shapes=[
            pltpu.SMEM((reach + 1, cap, 3), jnp.int32),
            pltpu.SMEM((1,), jnp.int32),
            pltpu.VMEM(probe.shape, f32),
            pltpu.VMEM((side, side), bf16),
            pltpu.VMEM((side, side), bf16),
            pltpu.VMEM(factors.shape, f32),
            pltpu.VMEM(measured.shape, bf16),
            pltpu.VMEM(table, bf16),
            pltpu.VMEM(table, bf16),
            pltpu.VMEM(table, bf16),
            pltpu.VMEM(table, bf16),
            pltpu.VMEM((cap, 2, strip, side), f32),
            pltpu.VMEM((reach + 1, cap, 2, side // LANES + 2, strip, LANES), f32),
            pltpu.VMEM(((reach + 1) * strip, side), f32),
            pltpu.VMEM((2, angles, 2, 1, width), f32),
            pltpu.SemaphoreType.DMA((5 + blocks,)),
            pltpu.SemaphoreType.DMA((2, reach + 1)),
            pltpu.SemaphoreType.DMA((2, 1)),
            pltpu.SemaphoreType.DMA((2, cap)),
            pltpu.SemaphoreType.DMA((2, pieces)),
            pltpu.SemaphoreType.DMA((2, pieces)),
            pltpu.SemaphoreType.DMA((2, 2)),
        ],
        compiler_params=params(collective_id=0, has_side_effects=True),
        cost_estimate=cost(20),
        name="update",
    )(
        frame_count,
        *[
            pltpu.with_memory_space_constraint(item, pltpu.HBM)
            for item in (
                frame_table,
                object_field,
                probe,
                measured,
                *fourier_tables(side),
                factors,
            )
        ],
    )

    updated, solved, ends = pl.pallas_call(
        forward_kernel,
        out_shape=[
            shape(object_field.shape, f32),
            shape((angles, strip, width), f32),
            shape((blocks, 2 * angles, LANES), f32),
        ],
        in_specs=[vmem] * 8,
        out_specs=[hbm, vmem, vmem],
        scratch_shapes=[pltpu.VMEM((rows, width), f32)]
        + [pltpu.VMEM((rows, half), bf16)] * 4
        + [pltpu.SemaphoreType.DMA((blocks,))],
        compiler_params=params(),
        cost_estimate=cost(9),
        name="forward",
    )(held, halo, *half_tables, local, extra)
    incoming = pl.pallas_call(
        join_kernel,
        out_shape=shape(ends.shape, f32),
        in_specs=[vmem] * 3,
        out_specs=vmem,
        scratch_shapes=[
            pltpu.VMEM((strips, 2 * angles, LANES), f32),
            pltpu.VMEM((strips, 2 * angles, LANES), f32),
            pltpu.SemaphoreType.DMA((blocks,)),
            pltpu.SemaphoreType.DMA((strips,)),
            pltpu.SemaphoreType.DMA((strips,)),
            pltpu.SemaphoreType.DMA((blocks,)),
        ],
        compiler_params=params(collective_id=4, has_side_effects=True),
        cost_estimate=cost(10),
        name="join",
    )(ends, by_block(powers), by_block(extra))
    phase_map = pl.pallas_call(
        inverse_kernel,
        out_shape=shape((angles, strip, width), f32),
        in_specs=[vmem] * 8,
        out_specs=vmem,
        scratch_shapes=[
            pltpu.VMEM((rows, width), bf16),
            pltpu.VMEM((rows, width), bf16),
        ],
        compiler_params=params(),
        cost_estimate=cost(6),
        name="inverse",
    )(solved, incoming, *half_tables, local, extra)
    return (updated, phase_map)


def solution(mesh):
    return jax.shard_map(
        body,
        mesh=mesh,
        in_specs=(
            P("group", None, "tile", None),
            P(),
            P(("group", "tile"), None, None),
            P(("group", "tile"), None),
            P(("group", "tile")),
        ),
        out_specs=(P("group", None, "tile", None), P("group", "tile", None)),
        check_vma=False,
    )
```

```python
import functools
import math

import numpy as np
import jax
import jax.numpy as jnp
from jax import lax
from jax.experimental import pallas as pl
from jax.experimental.pallas import tpu as pltpu
from jax.sharding import PartitionSpec as P

magnitude_floor = 0.5
soften_term = 0.5
screen_term = 0.0001
epsilon_term = 1e-06
f32 = jnp.float32
bf16 = jnp.bfloat16
LANES = 128
GROUP = 8
TILE = 256
VMEM_BYTES = 30 * 1024 * 1024
MESH = pl.DeviceIdType.MESH
vmem = pl.BlockSpec(memory_space=pltpu.VMEM)
smem = pl.BlockSpec(memory_space=pltpu.SMEM)
hbm = pl.BlockSpec(memory_space=pltpu.HBM)


def cost(micros):
    return pl.CostEstimate(
        flops=0, bytes_accessed=int(micros * 3_000_000), transcendentals=0
    )


def params(**more):
    return pltpu.CompilerParams(vmem_limit_bytes=VMEM_BYTES, **more)


def join_kernel(ends, powers, extra, out, heard, told, up_sems, in_sems, down_sems, back_sems):
    count = lax.axis_size("tile")
    me = lax.axis_index("tile")
    blocks, lines = ends.shape[0], ends.shape[1]
    angles = lines // 2
    stride = count // blocks
    mine = me // stride
    joins = lax.rem(me, stride) == 0
    barrier = pltpu.get_barrier_semaphore()

    def greet(by, _):
        pl.semaphore_signal(
            barrier, inc=1, device_id={"tile": lax.rem(me + by, count)}, device_id_type=MESH
        )
        return 0

    lax.fori_loop(1, count, greet, 0)
    pl.semaphore_wait(barrier, count - 1)

    def up(by):
        block = lax.rem(mine + by, blocks)
        return pltpu.make_async_remote_copy(
            src_ref=ends.at[block],
            dst_ref=heard.at[me],
            send_sem=up_sems.at[block],
            recv_sem=in_sems.at[me],
            device_id={"tile": block * stride},
            device_id_type=MESH,
        )

    def came(other):
        return pltpu.make_async_remote_copy(
            src_ref=ends.at[0],
            dst_ref=heard.at[other],
            send_sem=up_sems.at[0],
            recv_sem=in_sems.at[other],
            device_id={"tile": other},
            device_id_type=MESH,
        )

    def down(other):
        return pltpu.make_async_remote_copy(
            src_ref=told.at[other],
            dst_ref=out.at[mine],
            send_sem=down_sems.at[other],
            recv_sem=back_sems.at[mine],
            device_id={"tile": other},
            device_id_type=MESH,
        )

    def answered(block):
        return pltpu.make_async_remote_copy(
            src_ref=told.at[0],
            dst_ref=out.at[block],
            send_sem=down_sems.at[0],
            recv_sem=back_sems.at[block],
            device_id={"tile": block * stride},
            device_id_type=MESH,
        )

    def each(limit, step):
        def run(index, _):
            step(index)
            return 0

        lax.fori_loop(0, limit, run, 0)

    for by in range(blocks):
        pl.when(lax.rem(mine + by, blocks) * stride != me)(lambda: up(by).start())

    @pl.when(joins)
    def _():
        heard[me] = ends[mine]
        for by in range(1, count):
            came(lax.rem(me + by, count)).wait_recv()
        step = powers[mine, 1:2]
        whole = powers[mine, count : count + 1]
        closing = extra[mine, 1:2]
        gain = extra[mine, 0:1]
        wall = heard[count - 1, angles:]
        floor = heard[0, :angles]
        for strip in range(1, count):
            floor = floor * step + heard[strip, :angles]
            wall = wall * step + heard[count - 1 - strip, angles:]
        enter = (wall + whole * floor) * closing
        leave = (floor + whole * wall) * closing
        for strip in range(count):
            told[strip, :angles] = enter * gain
            enter = enter * step + heard[strip, :angles]
            back = count - 1 - strip
            told[back, angles:] = leave * gain
            leave = leave * step + heard[back, angles:]
        for by in range(1, count):
            down(lax.rem(me + by, count)).start()
        out[mine] = told[me]

    for by in range(blocks):
        block = lax.rem(mine + by, blocks)
        pl.when(block * stride != me)(lambda: answered(block).wait_recv())
        pl.when(block * stride != me)(lambda: up(by).wait_send())

    @pl.when(joins)
    def _():
        for by in range(1, count):
            down(lax.rem(me + by, count)).wait_send()


def fourier_tables(side):
    indices = np.arange(side)
    products = indices[:, None] * indices[None, :] % side
    phases = products.astype(np.float64) * (-2.0 * math.pi / side)
    scale = 1.0 / math.sqrt(side)
    return (
        jnp.asarray(np.cos(phases) * scale, f32).astype(bf16),
        jnp.asarray(np.sin(phases) * scale, f32).astype(bf16),
    )


def cosine_factors(grid_side):
    half = grid_side // 2
    step = 32
    out = []
    for odd in (0, 1):
        freqs = 2 * np.arange(half) + odd
        scale = np.where(freqs == 0, math.sqrt(1.0 / grid_side), math.sqrt(2.0 / grid_side))
        coarse = (2 * step * np.arange(half // step)[:, None] * freqs[None, :]) % (4 * grid_side)
        fine = ((2 * np.arange(step)[:, None] + 1) * freqs[None, :]) % (4 * grid_side)
        unit = math.pi / (2 * grid_side)
        out.append(
            np.stack(
                [
                    np.cos(coarse * unit) * scale,
                    np.sin(coarse * unit) * scale,
                    np.cos(fine * unit),
                    np.sin(fine * unit),
                ]
            )
        )
    return jnp.asarray(np.stack(out), f32)


def decay_tables(grid_side, strip_rows):
    half = grid_side // 2
    freqs = np.concatenate([2 * np.arange(half), 2 * np.arange(half) + 1]).astype(np.float64)
    shift = screen_term + 2.0 - 2.0 * np.cos(freqs * math.pi / grid_side)
    rate = 2.0 * np.arcsinh(np.sqrt(shift) / 2.0)
    gain = 2.0 / (2.0 * np.sinh(rate))
    groups = strip_rows // GROUP
    segments = np.exp(-groups * np.arange(GROUP)[:, None] * rate)
    steps = np.exp(-(np.arange(groups)[:, None] + 1) * rate)
    jumps = np.exp(-groups * np.array([[1], [2], [4]]) * rate)
    decays = np.concatenate([segments, segments[::-1], gain[None], jumps, steps])
    strips = grid_side // strip_rows
    powers = np.exp(-strip_rows * np.arange(strips + 1)[:, None] * rate)
    extra = np.stack([gain, 1.0 / (1.0 - np.exp(-2.0 * grid_side * rate))])
    return decays.astype(np.float32), powers.astype(np.float32), extra.astype(np.float32)


def table_rows(factors, part, high, low):
    step = factors.shape[2]

    def run(block, _):
        rows = pl.ds(pl.multiple_of(block * step, step), step)
        value = (
            factors[part, 0, pl.ds(block, 1)] * factors[part, 2]
            - factors[part, 1, pl.ds(block, 1)] * factors[part, 3]
        )
        rounded = value.astype(bf16)
        high[rows] = rounded
        low[rows] = (value - rounded.astype(f32)).astype(bf16)
        return 0

    lax.fori_loop(0, high.shape[0] // step, run, 0)


def window_start(column, width, span):
    return jnp.minimum(column // LANES, (width - span) // LANES) * LANES


def update_kernel(
    frame_count, frame_table, field, probe_in, measured, cos_in, sin_in, factors_in,
    held, halo, even_hi, even_lo, odd_hi, odd_lo,
    tables, counts, probe, cos_ref, sin_ref, factors, moved, cuts, arrived, away, landed,
    own, placed, window, edges,
    load_sems, tell_sems, count_sems, moved_sems, fetch_sems, give_sems, edge_sems,
):
    count = lax.axis_size("tile")
    me = lax.axis_index("tile")
    angles, _, strip, width = field.shape
    cap, side = measured.shape[0], measured.shape[1]
    span = side + LANES
    lanes = span // LANES
    blocks = width // LANES
    reach = tables.shape[0] - 1
    middle = reach // 2
    total = (reach + 1) * strip
    others = [j for j in range(reach + 1) if j != middle]

    def inside(place):
        return (place >= 0) & (place < count)

    def load(index, source, target):
        return pltpu.make_async_copy(source, target, load_sems.at[index])

    loads = [
        load(0, frame_table, tables.at[0]),
        load(1, factors_in, factors),
        load(2, probe_in, probe),
        load(3, cos_in, cos_ref),
        load(4, sin_in, sin_ref),
    ]
    strips = [
        load(5 + block, field.at[:, :, :, block * LANES : (block + 1) * LANES], held.at[:, :, block])
        for block in range(blocks)
    ]
    for item in loads[:2] + strips + loads[2:5]:
        item.start()

    def send(source, target, sems, index, by):
        copy = pltpu.make_async_remote_copy(
            src_ref=source,
            dst_ref=target,
            send_sem=sems.at[0, index],
            recv_sem=sems.at[1, index],
            device_id={"tile": me + by},
            device_id_type=MESH,
        )
        return copy, inside(me + by), inside(me - by)

    barrier = pltpu.get_barrier_semaphore()
    met = jnp.zeros((), jnp.int32)
    for by in [sign * by for by in range(1, reach + 1) for sign in (1, -1)]:

        @pl.when(inside(me + by))
        def _():
            pl.semaphore_signal(
                barrier, inc=1, device_id={"tile": me + by}, device_id_type=MESH
            )

        met = met + jnp.where(inside(me + by), 1, 0)
    pl.semaphore_wait(barrier, met)

    tells = [
        send(tables.at[0], tables.at[j], tell_sems, j, j) for j in range(1, reach + 1)
    ]
    tells.append(send(frame_count, counts, count_sems, 0, middle))
    moves = [
        send(measured.at[s], moved.at[s], moved_sems, s, middle) for s in range(cap)
    ]
    fetches = [
        [send(cuts.at[j, s], arrived.at[j, s], fetch_sems, s * (reach + 1) + j, middle - j) for j in others]
        for s in range(cap)
    ]
    gives = [
        [send(away.at[j, s], landed.at[j, s], give_sems, s * (reach + 1) + j, j - middle) for j in others]
        for s in range(cap)
    ]
    borders = [
        send(edges.at[1], halo.at[0], edge_sems, 0, 1),
        send(edges.at[0], halo.at[1], edge_sems, 1, -1),
    ]
    started = []

    def start(items):
        for copy, sends, takes in items:
            pl.when(sends)(copy.start)
            started.append((copy, sends))

    def arrive(items):
        for copy, sends, takes in items:
            pl.when(takes)(copy.wait_recv)

    def blank(items, wipe):
        for index, (copy, sends, takes) in enumerate(items):

            @pl.when(jnp.logical_not(takes))
            def _():
                wipe(index)

    def wipe_table(index):
        if index == reach:
            counts[0] = 0
        else:
            for s in range(cap):
                for item in range(3):
                    tables[index + 1, s, item] = 0

    def wipe(ref, *first):
        ref[first] = jnp.zeros(ref.shape[len(first):], ref.dtype)

    loads[0].wait()
    start(tells)
    start(moves)
    blank(tells, wipe_table)
    blank(moves, lambda s: wipe(moved, s))
    for s in range(cap):
        blank(fetches[s], lambda index: wipe(arrived, others[index], s))
        blank(gives[s], lambda index: wipe(landed, others[index], s))
    blank(borders, lambda index: wipe(halo, index))
    for j in range(reach + 1):
        for s in range(cap):
            for part in range(2):
                placed[j, s, part, 0] = jnp.zeros((strip, LANES), f32)
    loads[1].wait()
    table_rows(factors, 0, even_hi, even_lo)
    for item in strips:
        item.wait()
    arrive(tells)

    def first_block(j, s):
        return jnp.minimum(tables[j, s, 1] // LANES, blocks - lanes)

    for s in range(cap):
        for j in others + [middle]:
            block = first_block(j, s)
            shift = tables[j, s, 1] - block * LANES
            angle = tables[j, s, 2]
            for part in range(2):
                piece = jnp.concatenate(
                    [held[angle, part, block + lane] for lane in range(lanes)], 1
                )
                turned = pltpu.roll(piece, lax.rem(span - shift, span), 1)
                target = arrived if j == middle else cuts
                target[j, s, part] = turned[:, :side].astype(bf16)
        start(fetches[s])

    table_rows(factors, 1, odd_hi, odd_lo)
    for item in loads[2:5]:
        item.wait()
    cos_part, sin_part = cos_ref[...], sin_ref[...]
    stacked = jnp.concatenate([cos_part, sin_part], 0)
    joined = jnp.concatenate([cos_part, sin_part], 1)
    probe_re, probe_im = probe[0], probe[1]
    peak = jnp.max(probe_re * probe_re + probe_im * probe_im) + epsilon_term

    def left(re, im, sign):
        products = jnp.dot(
            stacked, jnp.concatenate([re, im], 1), preferred_element_type=f32
        )
        cc, ci = products[:side, :side], products[:side, side:]
        sc, si = products[side:, :side], products[side:, side:]
        return (cc - si, ci + sc) if sign > 0 else (cc + si, ci - sc)

    def right(re, im, sign):
        products = jnp.dot(
            jnp.concatenate([re, im], 0), joined, preferred_element_type=f32
        )
        rc, rs = products[:side, :side], products[:side, side:]
        ic, js = products[side:, :side], products[side:, side:]
        return (rc - js, rs + ic) if sign > 0 else (rc + js, ic - rs)

    for s in range(cap):
        arrive(fetches[s])
        offset = tables[middle, s, 0]
        patch = []
        for part in range(2):
            for j in range(reach + 1):
                window[j * strip : (j + 1) * strip] = arrived[j, s, part].astype(f32)
            turned = pltpu.roll(window[...], lax.rem(total - offset, total), 0)
            patch.append(turned[:side])
        wave_re = (probe_re * patch[0] - probe_im * patch[1]).astype(bf16)
        wave_im = (probe_re * patch[1] + probe_im * patch[0]).astype(bf16)
        half_re, half_im = left(wave_re, wave_im, 1)
        spec_re, spec_im = right(half_re.astype(bf16), half_im.astype(bf16), 1)
        amplitude = jnp.sqrt(spec_re * spec_re + spec_im * spec_im)
        if s == 0:
            arrive(moves)
        factor = moved[s].astype(f32) / jnp.maximum(amplitude, magnitude_floor) - 1.0
        back_re, back_im = left(
            (spec_re * factor).astype(bf16), (spec_im * factor).astype(bf16), -1
        )
        corr_re, corr_im = right(back_re.astype(bf16), back_im.astype(bf16), -1)
        live = s < counts[0]
        updates = (
            (probe_re * corr_re + probe_im * corr_im) / peak,
            (probe_re * corr_im - probe_im * corr_re) / peak,
        )
        for part in range(2):
            window[:side] = jnp.where(live, updates[part], 0.0)
            window[side:] = jnp.zeros((total - side, side), f32)
            turned = pltpu.roll(window[...], offset, 0)
            for j in range(reach + 1):
                piece = turned[j * strip : (j + 1) * strip]
                if j == middle:
                    own[s, part] = piece
                else:
                    away[j, s, part] = piece.astype(bf16)
        start(gives[s])

    pad = jnp.zeros((strip, LANES), f32)

    def shifted(source, j, s):
        shift = tables[j, s, 1] - first_block(j, s) * LANES
        for part in range(2):
            value = jnp.concatenate([source[part].astype(f32), pad], 1)
            turned = pltpu.roll(value, shift, 1)
            for lane in range(lanes):
                placed[j, s, part, lane + 1] = turned[:, lane * LANES : (lane + 1) * LANES]

    def add(items, rows):
        def chunk(block, _):
            for angle in range(angles):
                found = []
                for j, s in items:
                    near = block - first_block(j, s)
                    hit = (tables[j, s, 2] == angle) & (near >= 0) & (near < lanes)
                    found.append(jnp.where(hit, near + 1, 0))
                for part in range(2):
                    for row in rows:
                        value = held[angle, part, block, row]
                        for (j, s), index in zip(items, found):
                            value = value + placed[j, s, part, index, row]
                        held[angle, part, block, row] = value
            return 0

        lax.fori_loop(0, blocks, chunk, 0)

    for s in range(cap):
        shifted(own.at[s], middle, s)
    early = [(middle, s) for s in range(cap)]
    for s in range(cap - 1):
        arrive(gives[s])
        for j in others:
            shifted(landed.at[j, s], j, s)
        early += [(j, s) for j in others]
    add(early, [slice(0, strip)])
    arrive(gives[cap - 1])
    for j in others:
        shifted(landed.at[j, cap - 1], j, cap - 1)
    late = [(j, cap - 1) for j in others]
    add(late, [slice(0, GROUP), slice(strip - GROUP, strip)])
    for angle in range(angles):
        for part in range(2):
            for block in range(blocks):
                where = slice(block * LANES, (block + 1) * LANES)
                edges[0, angle, part, :, where] = held[angle, part, block, :1]
                edges[1, angle, part, :, where] = held[angle, part, block, strip - 1 :]
    start(borders)
    add(late, [slice(GROUP, strip - GROUP)])
    arrive(borders)
    for copy, sends in started:
        pl.when(sends)(copy.wait_send)


def mirror(value):
    side = value.shape[1]
    rows = lax.broadcasted_iota(jnp.int32, (side, side), 0)
    columns = lax.broadcasted_iota(jnp.int32, (side, side), 1)
    swap = jnp.where(rows + columns == side - 1, 1.0, 0.0).astype(bf16)
    high = value.astype(bf16)
    low = (value - high.astype(f32)).astype(bf16)
    return jnp.dot(high, swap, preferred_element_type=f32) + jnp.dot(
        low, swap, preferred_element_type=f32
    )


def split_store(value, high, low, columns):
    rounded = value.astype(bf16)
    high[:, columns] = rounded
    low[:, columns] = (value - rounded.astype(f32)).astype(bf16)


def power_of(re, im):
    return re * re + im * im + 0.5 * soften_term


def half_bond(first, second):
    cross = first[0] * second[1] - first[1] * second[0]
    return cross / (first[2] + second[2])


def forward_kernel(
    field, halo, even_hi, even_lo, odd_hi, odd_lo, decays,
    updated, out, carries, ends, source, xeh, xel, xoh, xol, coefs, power, drops, shifts, bonds, partial, afters, sems,
):
    angles, _, blocks, strip, _ = field.shape
    width = blocks * LANES
    groups = strip // GROUP
    copies = [
        pltpu.make_async_copy(
            field.at[:, :, block],
            updated.at[:, :, :, block * LANES : (block + 1) * LANES],
            sems.at[block],
        )
        for block in range(blocks)
    ]
    for copy in copies:
        copy.start()
    lane = lax.broadcasted_iota(jnp.int32, (GROUP, LANES), 1)
    segment = lax.broadcasted_iota(jnp.int32, (GROUP, LANES), 0)

    for angle in range(angles):

        def rows_of(group):
            return slice(group * GROUP, (group + 1) * GROUP)

        def prepare(block, slot):
            for group in range(groups):
                pair = [field[angle, part, block, rows_of(group)] for part in range(2)]
                power[slot, rows_of(group)] = power_of(*pair)
                for part, value in enumerate(pair):
                    shifts[slot, part, group] = pltpu.roll(value, 1, 1)

        def combine(block, slot):
            where = pl.ds(pl.multiple_of(block * LANES, LANES), LANES)

            def beyond(upper):
                edge, by, border = (0, 1, 0) if upper else (GROUP - 1, GROUP - 1, 1)
                pair = [
                    jnp.where(
                        segment == edge,
                        halo[border, angle, part, :, where],
                        pltpu.roll(field[angle, part, block, rows_of(0 if upper else groups - 1)], by, 0),
                    )
                    for part in range(2)
                ]
                return pair + [power_of(*pair)]

            for group in range(groups):
                here = [field[angle, part, block, rows_of(group)] for part in range(2)]
                here.append(power[slot, rows_of(group)])
                if group == 0:
                    drops[GROUP - 1 : 2 * GROUP - 1] = half_bond(beyond(True), here)
                if group == groups - 1:
                    below = beyond(False)
                else:
                    lower = slice(group * GROUP + 1, (group + 1) * GROUP + 1)
                    below = [field[angle, part, block, lower] for part in range(2)]
                    below.append(power[slot, lower])
                down = half_bond(here, below)
                first = (group + 1) * GROUP
                drops[first : first + GROUP] = down
                up = drops[first - 1 : first - 1 + GROUP]
                left = [
                    jnp.where(lane == 0, shifts[1 - slot, part, group], shifts[slot, part, group])
                    for part in range(2)
                ]
                bond = half_bond(left + [power_of(*left)], here)
                bonds[slot, group] = bond
                partial[slot, group] = up - down + bond

        def finish(block, slot):
            behind = pl.ds(pl.multiple_of(jnp.maximum(block - 1, 0) * LANES, LANES), LANES)
            for group in range(groups):
                after = pltpu.roll(bonds[slot, group], LANES - 1, 1)
                first = angle * strip + group * GROUP
                source[first : first + GROUP, behind] = partial[1 - slot, group] - jnp.where(
                    lane == LANES - 1, after, afters[group]
                )
                afters[group] = after

        def step(pair, _):
            block = 2 * pair
            finish(block - 1, 1)
            combine(block, 0)
            prepare(block + 1, 1)
            finish(block, 0)
            combine(block + 1, 1)
            prepare(jnp.minimum(block + 2, blocks - 1), 0)
            return 0

        for group in range(groups):
            for part in range(2):
                shifts[1, part, group] = jnp.zeros((GROUP, LANES), f32)
        prepare(0, 0)
        lax.fori_loop(0, blocks // 2, step, 0)
        finish(blocks - 1, 1)
        for group in range(groups):
            first = angle * strip + group * GROUP
            source[first : first + GROUP, width - LANES :] = partial[1, group] - jnp.where(
                lane == LANES - 1, 0.0, afters[group]
            )

    half = width // 2

    def tile(index):
        return pl.ds(pl.multiple_of(index * TILE, TILE), TILE)

    def fold(index, _):
        where = tile(index)
        near = source[:, where]
        far = mirror(source[:, tile(width // TILE - 1 - index)])
        split_store(near + far, xeh, xel, where)
        split_store(near - far, xoh, xol, where)
        return 0

    lax.fori_loop(0, half // TILE, fold, 0)
    for base, high, low, table_hi, table_lo in (
        (0, xeh, xel, even_hi, even_lo),
        (half, xoh, xol, odd_hi, odd_lo),
    ):

        def transform(index, _):
            where = tile(index)
            value = (
                jnp.dot(high[...], table_hi[:, where], preferred_element_type=f32)
                + jnp.dot(low[...], table_hi[:, where], preferred_element_type=f32)
                + jnp.dot(high[...], table_lo[:, where], preferred_element_type=f32)
            )
            for column in range(TILE // LANES):
                block = (base + index * TILE) // LANES + column
                coefs[block] = value[:, column * LANES : (column + 1) * LANES]
            return 0

        lax.fori_loop(0, half // TILE, transform, 0)

    def scan(chunk, _):
        where = pl.ds(pl.multiple_of(chunk * LANES, LANES), LANES)
        gain = decays[2 * GROUP : 2 * GROUP + 1, where]
        step = decays[2 * GROUP + 4 : 2 * GROUP + 5, where]
        for angle in range(angles):
            values = [
                coefs[chunk, pl.ds(angle * strip + group, GROUP, stride=groups)]
                for group in range(groups)
            ]
            fall, falls = values[0], [values[0]]
            for group in range(1, groups):
                fall = values[group] + step * fall
                falls.append(fall)
            rise = values[-1]
            for group in reversed(range(groups)):
                total = falls[group]
                if group < groups - 1:
                    later = step * rise
                    total = total + later
                    rise = values[group] + later
                out[angle, group * GROUP : (group + 1) * GROUP, where] = gain * total
            for index, by in enumerate((1, 2, 4)):
                jump = decays[2 * GROUP + 1 + index : 2 * GROUP + 2 + index, where]
                fall = fall + jnp.where(segment >= by, pltpu.roll(fall, by, 0), 0.0) * jump
                rise = rise + jnp.where(segment < GROUP - by, pltpu.roll(rise, GROUP - by, 0), 0.0) * jump
            ends[chunk, angle : angle + 1] = fall[GROUP - 1 :]
            ends[chunk, angles + angle : angles + angle + 1] = rise[:1]
            carries[chunk, angle] = gain * jnp.where(segment >= 1, pltpu.roll(fall, 1, 0), 0.0)
            carries[chunk, angles + angle] = gain * jnp.where(
                segment < GROUP - 1, pltpu.roll(rise, GROUP - 1, 0), 0.0
            )
        return 0

    lax.fori_loop(0, blocks, scan, 0, unroll=2)
    for copy in copies:
        copy.wait()


def inverse_kernel(
    value, carries, incoming, even_hi, even_lo, odd_hi, odd_lo, decays, out, xh, xl, parted, sems
):
    angles, strip, width = value.shape
    half = width // 2
    groups = strip // GROUP
    blocks = width // LANES

    def enter(chunk, _):
        where = pl.ds(pl.multiple_of(chunk * LANES, LANES), LANES)
        for angle in range(angles):
            fall = (
                carries[chunk, angle]
                + decays[:GROUP, where] * incoming[chunk, angle : angle + 1]
            )
            rise = (
                carries[chunk, angles + angle]
                + decays[GROUP : 2 * GROUP, where]
                * incoming[chunk, angles + angle : angles + angle + 1]
            )
            for pair in range(0, groups, 2):
                rows = []
                for group in (pair, pair + 1):
                    ahead = 2 * GROUP + 4 + group
                    behind = 2 * GROUP + 4 + groups - 1 - group
                    rows.append(
                        value[angle, group * GROUP : (group + 1) * GROUP, where]
                        + decays[ahead : ahead + 1, where] * fall
                        + decays[behind : behind + 1, where] * rise
                    )
                item = jnp.concatenate(rows, 0)
                rounded = item.astype(bf16)
                start = angle * strip + pair * GROUP
                xh[start : start + 2 * GROUP, where] = rounded
                xl[start : start + 2 * GROUP, where] = (item - rounded.astype(f32)).astype(bf16)
        return 0

    lax.fori_loop(0, blocks, enter, 0)
    last = (((1,), (1,)), ((), ()))
    copies = []
    for first in range(0, half, TILE):
        where = slice(first, first + TILE)
        parts = []
        for base, table_hi, table_lo in ((0, even_hi, even_lo), (half, odd_hi, odd_lo)):
            high = xh[:, base : base + half]
            low = xl[:, base : base + half]
            parts.append(
                lax.dot_general(high, table_hi[where], last, preferred_element_type=f32)
                + lax.dot_general(low, table_hi[where], last, preferred_element_type=f32)
                + lax.dot_general(high, table_lo[where], last, preferred_element_type=f32)
            )
        near = parts[0] + parts[1]
        far = mirror(parts[0] - parts[1])
        for item, start in ((near, first), (far, width - first - TILE)):
            for column in range(0, TILE, LANES):
                block = (start + column) // LANES
                for angle in range(angles):
                    for group in range(groups):
                        row = angle * strip + group * GROUP
                        parted[angle, block, pl.ds(group, GROUP, stride=groups)] = item[
                            row : row + GROUP, column : column + LANES
                        ]
                copy = pltpu.make_async_copy(
                    parted.at[:, block],
                    out.at[:, :, block * LANES : (block + 1) * LANES],
                    sems.at[block],
                )
                copy.start()
                copies.append(copy)
    for copy in copies:
        copy.wait()


def body(object_field, probe, measured, frame_table, frame_count):
    angles, _, strip, width = object_field.shape
    side = probe.shape[1]
    cap = measured.shape[0]
    half = width // 2
    reach = side // strip
    rows = angles * strip
    strips = lax.axis_size("tile")
    blocks = width // LANES
    shape = jax.ShapeDtypeStruct

    pieces = (reach + 1) * cap
    decays, powers, extra = decay_tables(width, strip)

    def by_block(table):
        return jnp.asarray(table.reshape(-1, blocks, LANES).transpose(1, 0, 2))

    factors = cosine_factors(width)
    table = (reach + 1, cap, 2, strip, side)
    held, halo, *half_tables = pl.pallas_call(
        update_kernel,
        out_shape=[
            shape((angles, 2, blocks, strip, LANES), f32),
            shape((2, angles, 2, 1, width), f32),
        ]
        + [shape((half, half), bf16)] * 4,
        in_specs=[smem] + [hbm] * 7,
        out_specs=[vmem] * 6,
        scratch_shapes=[
            pltpu.SMEM((reach + 1, cap, 3), jnp.int32),
            pltpu.SMEM((1,), jnp.int32),
            pltpu.VMEM(probe.shape, f32),
            pltpu.VMEM((side, side), bf16),
            pltpu.VMEM((side, side), bf16),
            pltpu.VMEM(factors.shape, f32),
            pltpu.VMEM(measured.shape, bf16),
            pltpu.VMEM(table, bf16),
            pltpu.VMEM(table, bf16),
            pltpu.VMEM(table, bf16),
            pltpu.VMEM(table, bf16),
            pltpu.VMEM((cap, 2, strip, side), f32),
            pltpu.VMEM((reach + 1, cap, 2, side // LANES + 2, strip, LANES), f32),
            pltpu.VMEM(((reach + 1) * strip, side), f32),
            pltpu.VMEM((2, angles, 2, 1, width), f32),
            pltpu.SemaphoreType.DMA((5 + blocks,)),
            pltpu.SemaphoreType.DMA((2, reach + 1)),
            pltpu.SemaphoreType.DMA((2, 1)),
            pltpu.SemaphoreType.DMA((2, cap)),
            pltpu.SemaphoreType.DMA((2, pieces)),
            pltpu.SemaphoreType.DMA((2, pieces)),
            pltpu.SemaphoreType.DMA((2, 2)),
        ],
        compiler_params=params(collective_id=0, has_side_effects=True),
        cost_estimate=cost(20),
        name="update",
    )(
        frame_count,
        *[
            pltpu.with_memory_space_constraint(item, pltpu.HBM)
            for item in (
                frame_table,
                object_field,
                probe,
                measured,
                *fourier_tables(side),
                factors,
            )
        ],
    )

    updated, solved, carries, ends = pl.pallas_call(
        forward_kernel,
        out_shape=[
            shape(object_field.shape, f32),
            shape((angles, strip, width), f32),
            shape((blocks, 2 * angles, GROUP, LANES), f32),
            shape((blocks, 2 * angles, LANES), f32),
        ],
        in_specs=[vmem] * 7,
        out_specs=[hbm, vmem, vmem, vmem],
        scratch_shapes=[pltpu.VMEM((rows, width), f32)]
        + [pltpu.VMEM((rows, half), bf16)] * 4
        + [
            pltpu.VMEM((blocks, rows, LANES), f32),
            pltpu.VMEM((2, strip, LANES), f32),
            pltpu.VMEM((strip + GROUP, LANES), f32),
            pltpu.VMEM((2, 2, strip // GROUP, GROUP, LANES), f32),
            pltpu.VMEM((2, strip // GROUP, GROUP, LANES), f32),
            pltpu.VMEM((2, strip // GROUP, GROUP, LANES), f32),
            pltpu.VMEM((strip // GROUP, GROUP, LANES), f32),
        ]
        + [pltpu.SemaphoreType.DMA((blocks,))],
        compiler_params=params(),
        cost_estimate=cost(9),
        name="forward",
    )(held, halo, *half_tables, decays)
    incoming = pl.pallas_call(
        join_kernel,
        out_shape=shape(ends.shape, f32),
        in_specs=[vmem] * 3,
        out_specs=vmem,
        scratch_shapes=[
            pltpu.VMEM((strips, 2 * angles, LANES), f32),
            pltpu.VMEM((strips, 2 * angles, LANES), f32),
            pltpu.SemaphoreType.DMA((blocks,)),
            pltpu.SemaphoreType.DMA((strips,)),
            pltpu.SemaphoreType.DMA((strips,)),
            pltpu.SemaphoreType.DMA((blocks,)),
        ],
        compiler_params=params(collective_id=4, has_side_effects=True),
        cost_estimate=cost(10),
        name="join",
    )(ends, by_block(powers), by_block(extra))
    phase_map = pl.pallas_call(
        inverse_kernel,
        out_shape=shape((angles, strip, width), f32),
        in_specs=[vmem] * 8,
        out_specs=hbm,
        scratch_shapes=[
            pltpu.VMEM((rows, width), bf16),
            pltpu.VMEM((rows, width), bf16),
            pltpu.VMEM((angles, blocks, strip, LANES), f32),
            pltpu.SemaphoreType.DMA((blocks,)),
        ],
        compiler_params=params(),
        cost_estimate=cost(6),
        name="inverse",
    )(solved, carries, incoming, *half_tables, decays)
    return (updated, phase_map)


def solution(mesh):
    return jax.shard_map(
        body,
        mesh=mesh,
        in_specs=(
            P("group", None, "tile", None),
            P(),
            P(("group", "tile"), None, None),
            P(("group", "tile"), None),
            P(("group", "tile")),
        ),
        out_specs=(P("group", None, "tile", None), P("group", "tile", None)),
        check_vma=False,
    )
```

```python
import functools
import math

import numpy as np
import jax
import jax.numpy as jnp
from jax import lax
from jax.experimental import pallas as pl
from jax.experimental.pallas import tpu as pltpu
from jax.sharding import PartitionSpec as P

magnitude_floor = 0.5
soften_term = 0.5
screen_term = 0.0001
epsilon_term = 1e-06
f32 = jnp.float32
bf16 = jnp.bfloat16
LANES = 128
GROUP = 8
TILE = 256
VMEM_BYTES = 30 * 1024 * 1024
MESH = pl.DeviceIdType.MESH
vmem = pl.BlockSpec(memory_space=pltpu.VMEM)
smem = pl.BlockSpec(memory_space=pltpu.SMEM)
hbm = pl.BlockSpec(memory_space=pltpu.HBM)


def cost(micros):
    return pl.CostEstimate(
        flops=0, bytes_accessed=int(micros * 3_000_000), transcendentals=0
    )


def params(**more):
    return pltpu.CompilerParams(vmem_limit_bytes=VMEM_BYTES, **more)


def fourier_tables(side):
    indices = np.arange(side)
    products = indices[:, None] * indices[None, :] % side
    phases = products.astype(np.float64) * (-2.0 * math.pi / side)
    scale = 1.0 / math.sqrt(side)
    return (
        jnp.asarray(np.cos(phases) * scale, f32).astype(bf16),
        jnp.asarray(np.sin(phases) * scale, f32).astype(bf16),
    )


def cosine_factors(grid_side):
    half = grid_side // 2
    step = 32
    out = []
    for odd in (0, 1):
        freqs = 2 * np.arange(half) + odd
        scale = np.where(freqs == 0, math.sqrt(1.0 / grid_side), math.sqrt(2.0 / grid_side))
        coarse = (2 * step * np.arange(half // step)[:, None] * freqs[None, :]) % (4 * grid_side)
        fine = ((2 * np.arange(step)[:, None] + 1) * freqs[None, :]) % (4 * grid_side)
        unit = math.pi / (2 * grid_side)
        out.append(
            np.stack(
                [
                    np.cos(coarse * unit) * scale,
                    np.sin(coarse * unit) * scale,
                    np.cos(fine * unit),
                    np.sin(fine * unit),
                ]
            )
        )
    return jnp.asarray(np.stack(out), f32)


def decay_tables(grid_side, strip_rows, plane):
    half = grid_side // 2
    freqs = np.concatenate([2 * np.arange(half), 2 * np.arange(half) + 1]).astype(np.float64)
    shift = screen_term + 2.0 - 2.0 * np.cos(freqs * math.pi / grid_side)
    rate = 2.0 * np.arcsinh(np.sqrt(shift) / 2.0)
    gain = 2.0 / (2.0 * np.sinh(rate))
    groups = strip_rows // GROUP
    segments = np.exp(-groups * np.arange(GROUP)[:, None] * rate)
    steps = np.exp(-(np.arange(groups)[:, None] + 1) * rate)
    jumps = np.exp(-groups * np.array([[1], [2], [4]]) * rate)
    decays = np.concatenate([segments, segments[::-1], gain[None], jumps, steps])
    spans = strip_rows * np.array([[1], [plane], [grid_side // strip_rows]])
    closing = 1.0 / (1.0 - np.exp(-2.0 * grid_side * rate))
    joins = np.concatenate([np.exp(-spans * rate), closing[None], gain[None]])
    return decays.astype(np.float32), joins.astype(np.float32)


def table_rows(factors, part, high, low):
    step = factors.shape[2]

    def run(block, _):
        rows = pl.ds(pl.multiple_of(block * step, step), step)
        value = (
            factors[part, 0, pl.ds(block, 1)] * factors[part, 2]
            - factors[part, 1, pl.ds(block, 1)] * factors[part, 3]
        )
        rounded = value.astype(bf16)
        high[rows] = rounded
        low[rows] = (value - rounded.astype(f32)).astype(bf16)
        return 0

    lax.fori_loop(0, high.shape[0] // step, run, 0)


def window_start(column, width, span):
    return jnp.minimum(column // LANES, (width - span) // LANES) * LANES


def update_kernel(
    frame_count, frame_table, field, probe_in, measured, cos_in, sin_in, factors_in,
    held, halo, even_hi, even_lo, odd_hi, odd_lo,
    tables, counts, probe, cos_ref, sin_ref, factors, moved, cuts, arrived, away, landed,
    own, placed, window, edges,
    load_sems, tell_sems, count_sems, moved_sems, fetch_sems, give_sems, edge_sems,
):
    count = lax.axis_size("tile")
    me = lax.axis_index("tile")
    angles, _, strip, width = field.shape
    cap, side = measured.shape[0], measured.shape[1]
    span = side + LANES
    lanes = span // LANES
    blocks = width // LANES
    reach = tables.shape[0] - 1
    middle = reach // 2
    total = (reach + 1) * strip
    others = [j for j in range(reach + 1) if j != middle]

    def inside(place):
        return (place >= 0) & (place < count)

    def load(index, source, target):
        return pltpu.make_async_copy(source, target, load_sems.at[index])

    loads = [
        load(0, frame_table, tables.at[0]),
        load(1, factors_in, factors),
        load(2, probe_in, probe),
        load(3, cos_in, cos_ref),
        load(4, sin_in, sin_ref),
    ]
    strips = [
        load(5 + block, field.at[:, :, :, block * LANES : (block + 1) * LANES], held.at[:, :, block])
        for block in range(blocks)
    ]
    for item in loads[:2] + strips + loads[2:5]:
        item.start()

    def send(source, target, sems, index, by):
        copy = pltpu.make_async_remote_copy(
            src_ref=source,
            dst_ref=target,
            send_sem=sems.at[0, index],
            recv_sem=sems.at[1, index],
            device_id={"tile": me + by},
            device_id_type=MESH,
        )
        return copy, inside(me + by), inside(me - by)

    barrier = pltpu.get_barrier_semaphore()
    met = jnp.zeros((), jnp.int32)
    for by in [sign * by for by in range(1, reach + 1) for sign in (1, -1)]:

        @pl.when(inside(me + by))
        def _():
            pl.semaphore_signal(
                barrier, inc=1, device_id={"tile": me + by}, device_id_type=MESH
            )

        met = met + jnp.where(inside(me + by), 1, 0)
    pl.semaphore_wait(barrier, met)

    tells = [
        send(tables.at[0], tables.at[j], tell_sems, j, j) for j in range(1, reach + 1)
    ]
    tells.append(send(frame_count, counts, count_sems, 0, middle))
    moves = [
        send(measured.at[s], moved.at[s], moved_sems, s, middle) for s in range(cap)
    ]
    fetches = [
        [send(cuts.at[j, s], arrived.at[j, s], fetch_sems, s * (reach + 1) + j, middle - j) for j in others]
        for s in range(cap)
    ]
    gives = [
        [send(away.at[j, s], landed.at[j, s], give_sems, s * (reach + 1) + j, j - middle) for j in others]
        for s in range(cap)
    ]
    borders = [
        send(edges.at[1], halo.at[0], edge_sems, 0, 1),
        send(edges.at[0], halo.at[1], edge_sems, 1, -1),
    ]
    started = []

    def start(items):
        for copy, sends, takes in items:
            pl.when(sends)(copy.start)
            started.append((copy, sends))

    def arrive(items):
        for copy, sends, takes in items:
            pl.when(takes)(copy.wait_recv)

    def blank(items, wipe):
        for index, (copy, sends, takes) in enumerate(items):

            @pl.when(jnp.logical_not(takes))
            def _():
                wipe(index)

    def wipe_table(index):
        if index == reach:
            counts[0] = 0
        else:
            for s in range(cap):
                for item in range(3):
                    tables[index + 1, s, item] = 0

    def wipe(ref, *first):
        ref[first] = jnp.zeros(ref.shape[len(first):], ref.dtype)

    loads[0].wait()
    start(tells)
    start(moves)
    blank(tells, wipe_table)
    blank(moves, lambda s: wipe(moved, s))
    for s in range(cap):
        blank(fetches[s], lambda index: wipe(arrived, others[index], s))
        blank(gives[s], lambda index: wipe(landed, others[index], s))
    blank(borders, lambda index: wipe(halo, index))
    for j in range(reach + 1):
        for s in range(cap):
            for part in range(2):
                placed[j, s, part, 0] = jnp.zeros((strip, LANES), f32)
    loads[1].wait()
    table_rows(factors, 0, even_hi, even_lo)
    for item in strips:
        item.wait()
    arrive(tells)

    def first_block(j, s):
        return jnp.minimum(tables[j, s, 1] // LANES, blocks - lanes)

    for s in range(cap):
        for j in others + [middle]:
            block = first_block(j, s)
            shift = tables[j, s, 1] - block * LANES
            angle = tables[j, s, 2]
            for part in range(2):
                piece = jnp.concatenate(
                    [held[angle, part, block + lane] for lane in range(lanes)], 1
                )
                turned = pltpu.roll(piece, lax.rem(span - shift, span), 1)
                target = arrived if j == middle else cuts
                target[j, s, part] = turned[:, :side].astype(bf16)
        start(fetches[s])

    table_rows(factors, 1, odd_hi, odd_lo)
    for item in loads[2:5]:
        item.wait()
    cos_part, sin_part = cos_ref[...], sin_ref[...]
    stacked = jnp.concatenate([cos_part, sin_part], 0)
    joined = jnp.concatenate([cos_part, sin_part], 1)
    probe_re, probe_im = probe[0], probe[1]
    peak = jnp.max(probe_re * probe_re + probe_im * probe_im) + epsilon_term

    def left(re, im, sign):
        products = jnp.dot(
            stacked, jnp.concatenate([re, im], 1), preferred_element_type=f32
        )
        cc, ci = products[:side, :side], products[:side, side:]
        sc, si = products[side:, :side], products[side:, side:]
        return (cc - si, ci + sc) if sign > 0 else (cc + si, ci - sc)

    def right(re, im, sign):
        products = jnp.dot(
            jnp.concatenate([re, im], 0), joined, preferred_element_type=f32
        )
        rc, rs = products[:side, :side], products[:side, side:]
        ic, js = products[side:, :side], products[side:, side:]
        return (rc - js, rs + ic) if sign > 0 else (rc + js, ic - rs)

    for s in range(cap):
        arrive(fetches[s])
        offset = tables[middle, s, 0]
        patch = []
        for part in range(2):
            for j in range(reach + 1):
                window[j * strip : (j + 1) * strip] = arrived[j, s, part].astype(f32)
            turned = pltpu.roll(window[...], lax.rem(total - offset, total), 0)
            patch.append(turned[:side])
        wave_re = (probe_re * patch[0] - probe_im * patch[1]).astype(bf16)
        wave_im = (probe_re * patch[1] + probe_im * patch[0]).astype(bf16)
        half_re, half_im = left(wave_re, wave_im, 1)
        spec_re, spec_im = right(half_re.astype(bf16), half_im.astype(bf16), 1)
        amplitude = jnp.sqrt(spec_re * spec_re + spec_im * spec_im)
        if s == 0:
            arrive(moves)
        factor = moved[s].astype(f32) / jnp.maximum(amplitude, magnitude_floor) - 1.0
        back_re, back_im = left(
            (spec_re * factor).astype(bf16), (spec_im * factor).astype(bf16), -1
        )
        corr_re, corr_im = right(back_re.astype(bf16), back_im.astype(bf16), -1)
        live = s < counts[0]
        updates = (
            (probe_re * corr_re + probe_im * corr_im) / peak,
            (probe_re * corr_im - probe_im * corr_re) / peak,
        )
        for part in range(2):
            window[:side] = jnp.where(live, updates[part], 0.0)
            window[side:] = jnp.zeros((total - side, side), f32)
            turned = pltpu.roll(window[...], offset, 0)
            for j in range(reach + 1):
                piece = turned[j * strip : (j + 1) * strip]
                if j == middle:
                    own[s, part] = piece
                else:
                    away[j, s, part] = piece.astype(bf16)
        start(gives[s])

    pad = jnp.zeros((strip, LANES), f32)

    def shifted(source, j, s):
        shift = tables[j, s, 1] - first_block(j, s) * LANES
        for part in range(2):
            value = jnp.concatenate([source[part].astype(f32), pad], 1)
            turned = pltpu.roll(value, shift, 1)
            for lane in range(lanes):
                placed[j, s, part, lane + 1] = turned[:, lane * LANES : (lane + 1) * LANES]

    def add(items, rows):
        def chunk(block, _):
            for angle in range(angles):
                found = []
                for j, s in items:
                    near = block - first_block(j, s)
                    hit = (tables[j, s, 2] == angle) & (near >= 0) & (near < lanes)
                    found.append(jnp.where(hit, near + 1, 0))
                for part in range(2):
                    for row in rows:
                        value = held[angle, part, block, row]
                        for (j, s), index in zip(items, found):
                            value = value + placed[j, s, part, index, row]
                        held[angle, part, block, row] = value
            return 0

        lax.fori_loop(0, blocks, chunk, 0)

    for s in range(cap):
        shifted(own.at[s], middle, s)
    early = [(middle, s) for s in range(cap)]
    for s in range(cap - 1):
        arrive(gives[s])
        for j in others:
            shifted(landed.at[j, s], j, s)
        early += [(j, s) for j in others]
    add(early, [slice(0, strip)])
    arrive(gives[cap - 1])
    for j in others:
        shifted(landed.at[j, cap - 1], j, cap - 1)
    late = [(j, cap - 1) for j in others]
    add(late, [slice(0, GROUP), slice(strip - GROUP, strip)])
    for angle in range(angles):
        for part in range(2):
            for block in range(blocks):
                where = slice(block * LANES, (block + 1) * LANES)
                edges[0, angle, part, :, where] = held[angle, part, block, :1]
                edges[1, angle, part, :, where] = held[angle, part, block, strip - 1 :]
    start(borders)
    add(late, [slice(GROUP, strip - GROUP)])
    arrive(borders)
    for copy, sends in started:
        pl.when(sends)(copy.wait_send)


def mirror(value):
    side = value.shape[1]
    rows = lax.broadcasted_iota(jnp.int32, (side, side), 0)
    columns = lax.broadcasted_iota(jnp.int32, (side, side), 1)
    swap = jnp.where(rows + columns == side - 1, 1.0, 0.0).astype(bf16)
    high = value.astype(bf16)
    low = (value - high.astype(f32)).astype(bf16)
    return jnp.dot(high, swap, preferred_element_type=f32) + jnp.dot(
        low, swap, preferred_element_type=f32
    )


def split_store(value, high, low, columns):
    rounded = value.astype(bf16)
    high[:, columns] = rounded
    low[:, columns] = (value - rounded.astype(f32)).astype(bf16)


def power_of(re, im):
    return re * re + im * im + 0.5 * soften_term


def half_bond(first, second):
    cross = first[0] * second[1] - first[1] * second[0]
    return cross / (first[2] + second[2])


def forward_kernel(
    field, halo, even_hi, even_lo, odd_hi, odd_lo, decays, joins,
    solved, carried, incoming, evens,
    source, xeh, xel, xoh, xol, coefs, power, drops, shifts, bonds, partial, afters,
    out, carries, ends, heard, sums, totals, told,
    up_sems, in_sems, over_sems, across_sems, down_sems, back_sems,
):
    angles, _, blocks, strip, _ = field.shape
    width = blocks * LANES
    groups = strip // GROUP
    plane, share = ends.shape[1], ends.shape[2]
    planes = totals.shape[1]
    me = lax.axis_index("tile")
    floor_at, seat = me // plane, lax.rem(me, plane)
    beside = [lax.rem(seat + by, plane) for by in range(1, plane)]
    beyond_planes = [lax.rem(floor_at + by, planes) for by in range(1, planes)]
    barrier = pltpu.get_barrier_semaphore()
    for peer in [floor_at * plane + other for other in beside] + [
        other * plane + seat for other in beyond_planes
    ]:
        pl.semaphore_signal(barrier, inc=1, device_id={"tile": peer}, device_id_type=MESH)

    def hop(source_ref, target_ref, send_sem, recv_sem, peer):
        return pltpu.make_async_remote_copy(
            src_ref=source_ref,
            dst_ref=target_ref,
            send_sem=send_sem,
            recv_sem=recv_sem,
            device_id={"tile": peer},
            device_id_type=MESH,
        )

    def up(part, other, slot):
        return hop(
            ends.at[part, other], heard.at[part, slot], up_sems.at[part, other],
            in_sems.at[part, slot], floor_at * plane + other,
        )

    def over(part, other, slot):
        return hop(
            sums.at[part], totals.at[part, slot], over_sems.at[part, other],
            across_sems.at[part, slot], other * plane + seat,
        )

    def down(part, other, slot):
        return hop(
            told.at[part, other], incoming.at[part, slot], down_sems.at[part, other],
            back_sems.at[part, slot], floor_at * plane + other,
        )

    def gather(part):
        for other in beside:
            up(part, other, seat).start()
        heard[part, seat] = ends[part, seat]

    def spread(part):
        for other in beside:
            up(part, other, other).wait_recv()
        step = joins[part, seat, 0][:, None]
        fall = heard[part, 0, :, :angles]
        rise = heard[part, plane - 1, :, angles:]
        for item in range(1, plane):
            fall = fall * step + heard[part, item, :, :angles]
            rise = rise * step + heard[part, plane - 1 - item, :, angles:]
        sums[part, :, :angles] = fall
        sums[part, :, angles:] = rise
        for other in beyond_planes:
            over(part, other, floor_at).start()
        totals[part, floor_at] = sums[part]

    def answer(part):
        for other in beyond_planes:
            over(part, other, other).wait_recv()
        step, leap, whole, closing, gain = [joins[part, seat, item][:, None] for item in range(5)]
        bottom = totals[part, 0, :, :angles]
        top = totals[part, planes - 1, :, angles:]
        for item in range(1, planes):
            bottom = bottom * leap + totals[part, item, :, :angles]
            top = top * leap + totals[part, planes - 1 - item, :, angles:]
        fall = (top + whole * bottom) * closing
        rise = (bottom + whole * top) * closing
        fall_here, rise_here = fall, rise
        for item in range(planes):
            fall_here = jnp.where(floor_at == item, fall, fall_here)
            fall = fall * leap + totals[part, item, :, :angles]
            back = planes - 1 - item
            rise_here = jnp.where(floor_at == back, rise, rise_here)
            rise = rise * leap + totals[part, back, :, angles:]
        for item in range(plane):
            told[part, item, :, :angles] = fall_here * gain
            fall_here = fall_here * step + heard[part, item, :, :angles]
            back = plane - 1 - item
            told[part, back, :, angles:] = rise_here * gain
            rise_here = rise_here * step + heard[part, back, :, angles:]
        for other in beside:
            down(part, other, seat).start()
        incoming[part, seat] = told[part, seat]

    def learn(part):
        for other in beside:
            down(part, other, other).wait_recv()

    lane = lax.broadcasted_iota(jnp.int32, (GROUP, LANES), 1)
    segment = lax.broadcasted_iota(jnp.int32, (GROUP, LANES), 0)

    for angle in range(angles):

        def rows_of(group):
            return slice(group * GROUP, (group + 1) * GROUP)

        def prepare(block, slot):
            for group in range(groups):
                pair = [field[angle, part, block, rows_of(group)] for part in range(2)]
                power[slot, rows_of(group)] = power_of(*pair)
                for part, value in enumerate(pair):
                    shifts[slot, part, group] = pltpu.roll(value, 1, 1)

        def combine(block, slot):
            where = pl.ds(pl.multiple_of(block * LANES, LANES), LANES)

            def beyond(upper):
                edge, by, border = (0, 1, 0) if upper else (GROUP - 1, GROUP - 1, 1)
                pair = [
                    jnp.where(
                        segment == edge,
                        halo[border, angle, part, :, where],
                        pltpu.roll(field[angle, part, block, rows_of(0 if upper else groups - 1)], by, 0),
                    )
                    for part in range(2)
                ]
                return pair + [power_of(*pair)]

            for group in range(groups):
                here = [field[angle, part, block, rows_of(group)] for part in range(2)]
                here.append(power[slot, rows_of(group)])
                if group == 0:
                    drops[GROUP - 1 : 2 * GROUP - 1] = half_bond(beyond(True), here)
                if group == groups - 1:
                    below = beyond(False)
                else:
                    lower = slice(group * GROUP + 1, (group + 1) * GROUP + 1)
                    below = [field[angle, part, block, lower] for part in range(2)]
                    below.append(power[slot, lower])
                down = half_bond(here, below)
                first = (group + 1) * GROUP
                drops[first : first + GROUP] = down
                up = drops[first - 1 : first - 1 + GROUP]
                left = [
                    jnp.where(lane == 0, shifts[1 - slot, part, group], shifts[slot, part, group])
                    for part in range(2)
                ]
                bond = half_bond(left + [power_of(*left)], here)
                bonds[slot, group] = bond
                partial[slot, group] = up - down + bond

        def finish(block, slot):
            behind = pl.ds(pl.multiple_of(jnp.maximum(block - 1, 0) * LANES, LANES), LANES)
            for group in range(groups):
                after = pltpu.roll(bonds[slot, group], LANES - 1, 1)
                first = angle * strip + group * GROUP
                source[first : first + GROUP, behind] = partial[1 - slot, group] - jnp.where(
                    lane == LANES - 1, after, afters[group]
                )
                afters[group] = after

        def step(pair, _):
            block = 2 * pair
            finish(block - 1, 1)
            combine(block, 0)
            prepare(block + 1, 1)
            finish(block, 0)
            combine(block + 1, 1)
            prepare(jnp.minimum(block + 2, blocks - 1), 0)
            return 0

        for group in range(groups):
            for part in range(2):
                shifts[1, part, group] = jnp.zeros((GROUP, LANES), f32)
        prepare(0, 0)
        lax.fori_loop(0, blocks // 2, step, 0)
        finish(blocks - 1, 1)
        for group in range(groups):
            first = angle * strip + group * GROUP
            source[first : first + GROUP, width - LANES :] = partial[1, group] - jnp.where(
                lane == LANES - 1, 0.0, afters[group]
            )

    half = width // 2

    def tile(index):
        return slice(index * TILE, (index + 1) * TILE)

    def fold(index):
        where = tile(index)
        near = source[:, where]
        far = mirror(source[:, tile(width // TILE - 1 - index)])
        split_store(near + far, xeh, xel, where)
        split_store(near - far, xoh, xol, where)

    for index in range(half // TILE):
        fold(index)
    def transform(part, index):
        high, low, table_hi, table_lo = (
            (xeh, xel, even_hi, even_lo),
            (xoh, xol, odd_hi, odd_lo),
        )[part]
        where = tile(index)
        value = (
            jnp.dot(high[...], table_hi[:, where], preferred_element_type=f32)
            + jnp.dot(low[...], table_hi[:, where], preferred_element_type=f32)
            + jnp.dot(high[...], table_lo[:, where], preferred_element_type=f32)
        )
        for column in range(TILE // LANES):
            block = index * TILE // LANES + column
            coefs[part, block] = value[:, column * LANES : (column + 1) * LANES]

    def scan(part):
        result, carry_ref = ((out, carries), (solved, carried))[part]

        def run(chunk, _):
            where = pl.ds(pl.multiple_of(chunk * LANES, LANES), LANES)
            table = pl.ds(pl.multiple_of(part * half + chunk * LANES, LANES), LANES)
            owner, place = chunk // share, lax.rem(chunk, share)
            gain = decays[2 * GROUP : 2 * GROUP + 1, table]
            step = decays[2 * GROUP + 4 : 2 * GROUP + 5, table]
            for angle in range(angles):
                values = [
                    coefs[part, chunk, pl.ds(angle * strip + group, GROUP, stride=groups)]
                    for group in range(groups)
                ]
                fall, falls = values[0], [values[0]]
                for group in range(1, groups):
                    fall = values[group] + step * fall
                    falls.append(fall)
                rise = values[-1]
                for group in reversed(range(groups)):
                    total = falls[group]
                    if group < groups - 1:
                        later = step * rise
                        total = total + later
                        rise = values[group] + later
                    result[angle, group * GROUP : (group + 1) * GROUP, where] = gain * total
                for index, by in enumerate((1, 2, 4)):
                    jump = decays[2 * GROUP + 1 + index : 2 * GROUP + 2 + index, table]
                    fall = fall + jnp.where(segment >= by, pltpu.roll(fall, by, 0), 0.0) * jump
                    rise = (
                        rise
                        + jnp.where(segment < GROUP - by, pltpu.roll(rise, GROUP - by, 0), 0.0)
                        * jump
                    )
                ends[part, owner, place, angle : angle + 1] = fall[GROUP - 1 :]
                ends[part, owner, place, angles + angle : angles + angle + 1] = rise[:1]
                carry_ref[chunk, angle] = gain * jnp.where(
                    segment >= 1, pltpu.roll(fall, 1, 0), 0.0
                )
                carry_ref[chunk, angles + angle] = gain * jnp.where(
                    segment < GROUP - 1, pltpu.roll(rise, GROUP - 1, 0), 0.0
                )
            return 0

        lax.fori_loop(0, blocks // 2, run, 0, unroll=2)

    tiles = half // TILE
    for index in range(tiles):
        transform(0, index)
    scan(0)
    pl.semaphore_wait(barrier, plane + planes - 2)
    gather(0)
    for index in range(tiles):
        transform(1, index)
    spread(0)
    scan(1)
    gather(1)
    spread(1)
    answer(0)
    learn(0)
    enter(0, out, carries, incoming, decays, xeh, xel)
    for index in range(tiles):
        if index == 1 or tiles == 1:
            answer(1)
        evens[:, tile(index)] = restored(xeh, xel, even_hi, even_lo, tile(index))
    learn(1)
    for part in range(2):
        for other in beside:
            up(part, other, seat).wait_send()
            down(part, other, seat).wait_send()
        for other in beyond_planes:
            over(part, other, floor_at).wait_send()


def enter(part, value, carries, incoming, decays, high, low):
    angles, strip, half = value.shape
    groups = strip // GROUP
    share = incoming.shape[2]

    def run(chunk, _):
        where = pl.ds(pl.multiple_of(chunk * LANES, LANES), LANES)
        table = pl.ds(pl.multiple_of(part * half + chunk * LANES, LANES), LANES)
        owner, place = chunk // share, lax.rem(chunk, share)
        for angle in range(angles):
            fall = (
                carries[chunk, angle]
                + decays[:GROUP, table] * incoming[part, owner, place, angle : angle + 1]
            )
            rise = (
                carries[chunk, angles + angle]
                + decays[GROUP : 2 * GROUP, table]
                * incoming[part, owner, place, angles + angle : angles + angle + 1]
            )
            for pair in range(0, groups, 2):
                rows = []
                for group in (pair, pair + 1):
                    ahead = 2 * GROUP + 4 + group
                    behind = 2 * GROUP + 4 + groups - 1 - group
                    rows.append(
                        value[angle, group * GROUP : (group + 1) * GROUP, where]
                        + decays[ahead : ahead + 1, table] * fall
                        + decays[behind : behind + 1, table] * rise
                    )
                item = jnp.concatenate(rows, 0)
                rounded = item.astype(bf16)
                start = angle * strip + pair * GROUP
                high[start : start + 2 * GROUP, where] = rounded
                low[start : start + 2 * GROUP, where] = (item - rounded.astype(f32)).astype(bf16)
        return 0

    lax.fori_loop(0, half // LANES, run, 0)


def restored(high, low, table_hi, table_lo, where):
    last = (((1,), (1,)), ((), ()))
    return (
        lax.dot_general(high[...], table_hi[where], last, preferred_element_type=f32)
        + lax.dot_general(low[...], table_hi[where], last, preferred_element_type=f32)
        + lax.dot_general(high[...], table_lo[where], last, preferred_element_type=f32)
    )


def inverse_kernel(
    field, value, carries, incoming, evens, odd_hi, odd_lo, decays,
    updated, out, xh, xl, parted, sems, field_sems,
):
    angles, strip, half = value.shape
    width = 2 * half
    groups = strip // GROUP
    blocks = width // LANES
    copies = []
    for block in range(blocks):
        copy = pltpu.make_async_copy(
            field.at[:, :, block],
            updated.at[:, :, :, block * LANES : (block + 1) * LANES],
            field_sems.at[block],
        )
        copy.start()
        copies.append(copy)
    enter(1, value, carries, incoming, decays, xh, xl)
    for first in range(0, half, TILE):
        where = slice(first, first + TILE)
        even = evens[:, where]
        odd = restored(xh, xl, odd_hi, odd_lo, where)
        near = even + odd
        far = mirror(even - odd)
        for item, start in ((near, first), (far, width - first - TILE)):
            for column in range(0, TILE, LANES):
                block = (start + column) // LANES
                for angle in range(angles):
                    for group in range(groups):
                        row = angle * strip + group * GROUP
                        parted[angle, block, pl.ds(group, GROUP, stride=groups)] = item[
                            row : row + GROUP, column : column + LANES
                        ]
                copy = pltpu.make_async_copy(
                    parted.at[:, block],
                    out.at[:, :, block * LANES : (block + 1) * LANES],
                    sems.at[block],
                )
                copy.start()
                copies.append(copy)
    for copy in copies:
        copy.wait()


def body(object_field, probe, measured, frame_table, frame_count):
    angles, _, strip, width = object_field.shape
    side = probe.shape[1]
    cap = measured.shape[0]
    half = width // 2
    reach = side // strip
    rows = angles * strip
    strips = lax.axis_size("tile")
    blocks = width // LANES
    shape = jax.ShapeDtypeStruct

    pieces = (reach + 1) * cap
    plane = 2 ** (int(math.log2(strips)) // 2)
    share = blocks // (2 * plane)
    decays, joins = decay_tables(width, strip, plane)
    joins = jnp.asarray(joins.reshape(-1, 2, plane, share, LANES).transpose(1, 2, 0, 3, 4))

    factors = cosine_factors(width)
    table = (reach + 1, cap, 2, strip, side)
    held, halo, *half_tables = pl.pallas_call(
        update_kernel,
        out_shape=[
            shape((angles, 2, blocks, strip, LANES), f32),
            shape((2, angles, 2, 1, width), f32),
        ]
        + [shape((half, half), bf16)] * 4,
        in_specs=[smem] + [hbm] * 7,
        out_specs=[vmem] * 6,
        scratch_shapes=[
            pltpu.SMEM((reach + 1, cap, 3), jnp.int32),
            pltpu.SMEM((1,), jnp.int32),
            pltpu.VMEM(probe.shape, f32),
            pltpu.VMEM((side, side), bf16),
            pltpu.VMEM((side, side), bf16),
            pltpu.VMEM(factors.shape, f32),
            pltpu.VMEM(measured.shape, bf16),
            pltpu.VMEM(table, bf16),
            pltpu.VMEM(table, bf16),
            pltpu.VMEM(table, bf16),
            pltpu.VMEM(table, bf16),
            pltpu.VMEM((cap, 2, strip, side), f32),
            pltpu.VMEM((reach + 1, cap, 2, side // LANES + 2, strip, LANES), f32),
            pltpu.VMEM(((reach + 1) * strip, side), f32),
            pltpu.VMEM((2, angles, 2, 1, width), f32),
            pltpu.SemaphoreType.DMA((5 + blocks,)),
            pltpu.SemaphoreType.DMA((2, reach + 1)),
            pltpu.SemaphoreType.DMA((2, 1)),
            pltpu.SemaphoreType.DMA((2, cap)),
            pltpu.SemaphoreType.DMA((2, pieces)),
            pltpu.SemaphoreType.DMA((2, pieces)),
            pltpu.SemaphoreType.DMA((2, 2)),
        ],
        compiler_params=params(collective_id=0, has_side_effects=True),
        cost_estimate=cost(20),
        name="update",
    )(
        frame_count,
        *[
            pltpu.with_memory_space_constraint(item, pltpu.HBM)
            for item in (
                frame_table,
                object_field,
                probe,
                measured,
                *fourier_tables(side),
                factors,
            )
        ],
    )

    planes = strips // plane
    lines = (share, 2 * angles, LANES)
    solved, carried, incoming, evens = pl.pallas_call(
        forward_kernel,
        out_shape=[
            shape((angles, strip, half), f32),
            shape((blocks // 2, 2 * angles, GROUP, LANES), f32),
            shape((2, plane) + lines, f32),
            shape((rows, half), f32),
        ],
        in_specs=[vmem] * 8,
        out_specs=[vmem] * 4,
        scratch_shapes=[pltpu.VMEM((rows, width), f32)]
        + [pltpu.VMEM((rows, half), bf16)] * 4
        + [
            pltpu.VMEM((2, blocks // 2, rows, LANES), f32),
            pltpu.VMEM((2, strip, LANES), f32),
            pltpu.VMEM((strip + GROUP, LANES), f32),
            pltpu.VMEM((2, 2, strip // GROUP, GROUP, LANES), f32),
            pltpu.VMEM((2, strip // GROUP, GROUP, LANES), f32),
            pltpu.VMEM((2, strip // GROUP, GROUP, LANES), f32),
            pltpu.VMEM((strip // GROUP, GROUP, LANES), f32),
            pltpu.VMEM((angles, strip, half), f32),
            pltpu.VMEM((blocks // 2, 2 * angles, GROUP, LANES), f32),
            pltpu.VMEM((2, plane) + lines, f32),
            pltpu.VMEM((2, plane) + lines, f32),
            pltpu.VMEM((2,) + lines, f32),
            pltpu.VMEM((2, planes) + lines, f32),
            pltpu.VMEM((2, plane) + lines, f32),
            pltpu.SemaphoreType.DMA((2, plane)),
            pltpu.SemaphoreType.DMA((2, plane)),
            pltpu.SemaphoreType.DMA((2, planes)),
            pltpu.SemaphoreType.DMA((2, planes)),
            pltpu.SemaphoreType.DMA((2, plane)),
            pltpu.SemaphoreType.DMA((2, plane)),
        ],
        compiler_params=params(collective_id=1, has_side_effects=True),
        cost_estimate=cost(15),
        name="forward",
    )(held, halo, *half_tables, decays, joins)
    updated, phase_map = pl.pallas_call(
        inverse_kernel,
        out_shape=[shape(object_field.shape, f32), shape((angles, strip, width), f32)],
        in_specs=[vmem] * 8,
        out_specs=[hbm, hbm],
        scratch_shapes=[
            pltpu.VMEM((rows, half), bf16),
            pltpu.VMEM((rows, half), bf16),
            pltpu.VMEM((angles, blocks, strip, LANES), f32),
            pltpu.SemaphoreType.DMA((blocks,)),
            pltpu.SemaphoreType.DMA((blocks,)),
        ],
        compiler_params=params(),
        cost_estimate=cost(6),
        name="inverse",
    )(held, solved, carried, incoming, evens, *half_tables[2:], decays)
    return (updated, phase_map)


def solution(mesh):
    return jax.shard_map(
        body,
        mesh=mesh,
        in_specs=(
            P("group", None, "tile", None),
            P(),
            P(("group", "tile"), None, None),
            P(("group", "tile"), None),
            P(("group", "tile")),
        ),
        out_specs=(P("group", None, "tile", None), P("group", "tile", None)),
        check_vma=False,
    )
```

```python
import functools
import math

import numpy as np
import jax
import jax.numpy as jnp
from jax import lax
from jax.experimental import pallas as pl
from jax.experimental.pallas import tpu as pltpu
from jax.sharding import PartitionSpec as P

magnitude_floor = 0.5
soften_term = 0.5
screen_term = 0.0001
epsilon_term = 1e-06
f32 = jnp.float32
bf16 = jnp.bfloat16
LANES = 128
GROUP = 8
TILE = 256
VMEM_BYTES = 30 * 1024 * 1024
MESH = pl.DeviceIdType.MESH
vmem = pl.BlockSpec(memory_space=pltpu.VMEM)
smem = pl.BlockSpec(memory_space=pltpu.SMEM)
hbm = pl.BlockSpec(memory_space=pltpu.HBM)


def cost(micros):
    return pl.CostEstimate(
        flops=0, bytes_accessed=int(micros * 3_000_000), transcendentals=0
    )


def params(**more):
    return pltpu.CompilerParams(vmem_limit_bytes=VMEM_BYTES, **more)


def fourier_tables(side):
    indices = np.arange(side)
    products = indices[:, None] * indices[None, :] % side
    phases = products.astype(np.float64) * (-2.0 * math.pi / side)
    scale = 1.0 / math.sqrt(side)
    return (
        jnp.asarray(np.cos(phases) * scale, f32).astype(bf16),
        jnp.asarray(np.sin(phases) * scale, f32).astype(bf16),
    )


def cosine_factors(grid_side):
    half = grid_side // 2
    step = 32
    out = []
    for odd in (0, 1):
        freqs = 2 * np.arange(half) + odd
        scale = np.where(freqs == 0, math.sqrt(1.0 / grid_side), math.sqrt(2.0 / grid_side))
        coarse = (2 * step * np.arange(half // step)[:, None] * freqs[None, :]) % (4 * grid_side)
        fine = ((2 * np.arange(step)[:, None] + 1) * freqs[None, :]) % (4 * grid_side)
        unit = math.pi / (2 * grid_side)
        out.append(
            np.stack(
                [
                    np.cos(coarse * unit) * scale,
                    np.sin(coarse * unit) * scale,
                    np.cos(fine * unit),
                    np.sin(fine * unit),
                ]
            )
        )
    return jnp.asarray(np.stack(out), f32)


def decay_tables(grid_side, strip_rows, plane):
    half = grid_side // 2
    freqs = np.concatenate([2 * np.arange(half), 2 * np.arange(half) + 1]).astype(np.float64)
    shift = screen_term + 2.0 - 2.0 * np.cos(freqs * math.pi / grid_side)
    rate = 2.0 * np.arcsinh(np.sqrt(shift) / 2.0)
    gain = 2.0 / (2.0 * np.sinh(rate))
    groups = strip_rows // GROUP
    segments = np.exp(-groups * np.arange(GROUP)[:, None] * rate)
    steps = np.exp(-(np.arange(groups)[:, None] + 1) * rate)
    jumps = np.exp(-groups * np.array([[1], [2], [4]]) * rate)
    spare = np.zeros((GROUP - 4,) + gain.shape)
    decays = np.concatenate(
        [segments, segments[::-1], gain[None], jumps, spare, steps, steps[::-1]]
    )
    spans = strip_rows * np.array([[1], [plane], [grid_side // strip_rows]])
    closing = 1.0 / (1.0 - np.exp(-2.0 * grid_side * rate))
    joins = np.concatenate([np.exp(-spans * rate), closing[None], gain[None]])
    return decays.astype(np.float32), joins.astype(np.float32)


def table_rows(factors, part, high, low):
    step = factors.shape[2]

    def run(block, _):
        rows = pl.ds(pl.multiple_of(block * step, step), step)
        value = (
            factors[part, 0, pl.ds(block, 1)] * factors[part, 2]
            - factors[part, 1, pl.ds(block, 1)] * factors[part, 3]
        )
        rounded = value.astype(bf16)
        high[rows] = rounded
        low[rows] = (value - rounded.astype(f32)).astype(bf16)
        return 0

    lax.fori_loop(0, high.shape[0] // step, run, 0)


def window_start(column, width, span):
    return jnp.minimum(column // LANES, (width - span) // LANES) * LANES


def update_kernel(
    frame_count, frame_table, field, probe_in, measured, cos_in, sin_in, factors_in,
    held, halo, even_hi, even_lo, odd_hi, odd_lo,
    tables, counts, probe, cos_ref, sin_ref, factors, moved, cuts, arrived, away, landed,
    own, placed, window, edges,
    load_sems, tell_sems, count_sems, moved_sems, fetch_sems, give_sems, edge_sems,
):
    count = lax.axis_size("tile")
    me = lax.axis_index("tile")
    angles, _, strip, width = field.shape
    cap, side = measured.shape[0], measured.shape[1]
    span = side + LANES
    lanes = span // LANES
    blocks = width // LANES
    reach = tables.shape[0] - 1
    middle = reach // 2
    total = (reach + 1) * strip
    others = [j for j in range(reach + 1) if j != middle]

    def inside(place):
        return (place >= 0) & (place < count)

    def load(index, source, target):
        return pltpu.make_async_copy(source, target, load_sems.at[index])

    loads = [
        load(0, frame_table, tables.at[0]),
        load(1, factors_in, factors),
        load(2, probe_in, probe),
        load(3, cos_in, cos_ref),
        load(4, sin_in, sin_ref),
    ]
    strips = [
        load(5 + block, field.at[:, :, :, block * LANES : (block + 1) * LANES], held.at[:, :, block])
        for block in range(blocks)
    ]
    for item in loads[:2] + strips + loads[2:5]:
        item.start()

    def send(source, target, sems, index, by):
        copy = pltpu.make_async_remote_copy(
            src_ref=source,
            dst_ref=target,
            send_sem=sems.at[0, index],
            recv_sem=sems.at[1, index],
            device_id={"tile": me + by},
            device_id_type=MESH,
        )
        return copy, inside(me + by), inside(me - by)

    barrier = pltpu.get_barrier_semaphore()
    met = jnp.zeros((), jnp.int32)
    for by in [sign * by for by in range(1, reach + 1) for sign in (1, -1)]:

        @pl.when(inside(me + by))
        def _():
            pl.semaphore_signal(
                barrier, inc=1, device_id={"tile": me + by}, device_id_type=MESH
            )

        met = met + jnp.where(inside(me + by), 1, 0)
    pl.semaphore_wait(barrier, met)

    tells = [
        send(tables.at[0], tables.at[j], tell_sems, j, j) for j in range(1, reach + 1)
    ]
    tells.append(send(frame_count, counts, count_sems, 0, middle))
    moves = [
        send(measured.at[s], moved.at[s], moved_sems, s, middle) for s in range(cap)
    ]
    fetches = [
        [send(cuts.at[j, s], arrived.at[j, s], fetch_sems, s * (reach + 1) + j, middle - j) for j in others]
        for s in range(cap)
    ]
    gives = [
        [send(away.at[j, s], landed.at[j, s], give_sems, s * (reach + 1) + j, j - middle) for j in others]
        for s in range(cap)
    ]
    borders = [
        send(edges.at[1], halo.at[0], edge_sems, 0, 1),
        send(edges.at[0], halo.at[1], edge_sems, 1, -1),
    ]
    started = []

    def start(items):
        for copy, sends, takes in items:
            pl.when(sends)(copy.start)
            started.append((copy, sends))

    def arrive(items):
        for copy, sends, takes in items:
            pl.when(takes)(copy.wait_recv)

    def blank(items, wipe):
        for index, (copy, sends, takes) in enumerate(items):

            @pl.when(jnp.logical_not(takes))
            def _():
                wipe(index)

    def wipe_table(index):
        if index == reach:
            counts[0] = 0
        else:
            for s in range(cap):
                for item in range(3):
                    tables[index + 1, s, item] = 0

    def wipe(ref, *first):
        ref[first] = jnp.zeros(ref.shape[len(first):], ref.dtype)

    loads[0].wait()
    start(tells)
    start(moves)
    blank(tells, wipe_table)
    blank(moves, lambda s: wipe(moved, s))
    for s in range(cap):
        blank(fetches[s], lambda index: wipe(arrived, others[index], s))
        blank(gives[s], lambda index: wipe(landed, others[index], s))
    blank(borders, lambda index: wipe(halo, index))
    for j in range(reach + 1):
        for s in range(cap):
            for part in range(2):
                placed[j, s, part, 0] = jnp.zeros((strip, LANES), f32)
    loads[1].wait()
    table_rows(factors, 0, even_hi, even_lo)
    for item in strips:
        item.wait()
    arrive(tells)

    def first_block(j, s):
        return jnp.minimum(tables[j, s, 1] // LANES, blocks - lanes)

    for s in range(cap):
        for j in others + [middle]:
            block = first_block(j, s)
            shift = tables[j, s, 1] - block * LANES
            angle = tables[j, s, 2]
            for part in range(2):
                piece = jnp.concatenate(
                    [held[angle, part, block + lane] for lane in range(lanes)], 1
                )
                turned = pltpu.roll(piece, lax.rem(span - shift, span), 1)
                target = arrived if j == middle else cuts
                target[j, s, part] = turned[:, :side].astype(bf16)
        start(fetches[s])

    table_rows(factors, 1, odd_hi, odd_lo)
    for item in loads[2:5]:
        item.wait()
    cos_part, sin_part = cos_ref[...], sin_ref[...]
    stacked = jnp.concatenate([cos_part, sin_part], 0)
    joined = jnp.concatenate([cos_part, sin_part], 1)
    probe_re, probe_im = probe[0], probe[1]
    peak = jnp.max(probe_re * probe_re + probe_im * probe_im) + epsilon_term

    def left(re, im, sign):
        products = jnp.dot(
            stacked, jnp.concatenate([re, im], 1), preferred_element_type=f32
        )
        cc, ci = products[:side, :side], products[:side, side:]
        sc, si = products[side:, :side], products[side:, side:]
        return (cc - si, ci + sc) if sign > 0 else (cc + si, ci - sc)

    def right(re, im, sign):
        products = jnp.dot(
            jnp.concatenate([re, im], 0), joined, preferred_element_type=f32
        )
        rc, rs = products[:side, :side], products[:side, side:]
        ic, js = products[side:, :side], products[side:, side:]
        return (rc - js, rs + ic) if sign > 0 else (rc + js, ic - rs)

    for s in range(cap):
        arrive(fetches[s])
        offset = tables[middle, s, 0]
        patch = []
        for part in range(2):
            for j in range(reach + 1):
                window[j * strip : (j + 1) * strip] = arrived[j, s, part].astype(f32)
            turned = pltpu.roll(window[...], lax.rem(total - offset, total), 0)
            patch.append(turned[:side])
        wave_re = (probe_re * patch[0] - probe_im * patch[1]).astype(bf16)
        wave_im = (probe_re * patch[1] + probe_im * patch[0]).astype(bf16)
        half_re, half_im = left(wave_re, wave_im, 1)
        spec_re, spec_im = right(half_re.astype(bf16), half_im.astype(bf16), 1)
        amplitude = jnp.sqrt(spec_re * spec_re + spec_im * spec_im)
        if s == 0:
            arrive(moves)
        factor = moved[s].astype(f32) / jnp.maximum(amplitude, magnitude_floor) - 1.0
        back_re, back_im = left(
            (spec_re * factor).astype(bf16), (spec_im * factor).astype(bf16), -1
        )
        corr_re, corr_im = right(back_re.astype(bf16), back_im.astype(bf16), -1)
        live = s < counts[0]
        updates = (
            (probe_re * corr_re + probe_im * corr_im) / peak,
            (probe_re * corr_im - probe_im * corr_re) / peak,
        )
        for part in range(2):
            window[:side] = jnp.where(live, updates[part], 0.0)
            window[side:] = jnp.zeros((total - side, side), f32)
            turned = pltpu.roll(window[...], offset, 0)
            for j in range(reach + 1):
                piece = turned[j * strip : (j + 1) * strip]
                if j == middle:
                    own[s, part] = piece
                else:
                    away[j, s, part] = piece.astype(bf16)
        start(gives[s])

    pad = jnp.zeros((strip, LANES), f32)

    def shifted(source, j, s):
        shift = tables[j, s, 1] - first_block(j, s) * LANES
        for part in range(2):
            value = jnp.concatenate([source[part].astype(f32), pad], 1)
            turned = pltpu.roll(value, shift, 1)
            for lane in range(lanes):
                placed[j, s, part, lane + 1] = turned[:, lane * LANES : (lane + 1) * LANES]

    def add(items, rows):
        def chunk(block, _):
            for angle in range(angles):
                found = []
                for j, s in items:
                    near = block - first_block(j, s)
                    hit = (tables[j, s, 2] == angle) & (near >= 0) & (near < lanes)
                    found.append(jnp.where(hit, near + 1, 0))
                for part in range(2):
                    for row in rows:
                        value = held[angle, part, block, row]
                        for (j, s), index in zip(items, found):
                            value = value + placed[j, s, part, index, row]
                        held[angle, part, block, row] = value
            return 0

        lax.fori_loop(0, blocks, chunk, 0)

    for s in range(cap):
        shifted(own.at[s], middle, s)
    early = [(middle, s) for s in range(cap)]
    for s in range(cap - 1):
        arrive(gives[s])
        for j in others:
            shifted(landed.at[j, s], j, s)
        early += [(j, s) for j in others]
    add(early, [slice(0, strip)])
    arrive(gives[cap - 1])
    for j in others:
        shifted(landed.at[j, cap - 1], j, cap - 1)
    late = [(j, cap - 1) for j in others]
    add(late, [slice(0, GROUP), slice(strip - GROUP, strip)])
    for angle in range(angles):
        for part in range(2):
            for block in range(blocks):
                where = slice(block * LANES, (block + 1) * LANES)
                edges[0, angle, part, :, where] = held[angle, part, block, :1]
                edges[1, angle, part, :, where] = held[angle, part, block, strip - 1 :]
    start(borders)
    add(late, [slice(GROUP, strip - GROUP)])
    arrive(borders)
    for copy, sends in started:
        pl.when(sends)(copy.wait_send)


def mirror(value):
    side = value.shape[1]
    rows = lax.broadcasted_iota(jnp.int32, (side, side), 0)
    columns = lax.broadcasted_iota(jnp.int32, (side, side), 1)
    swap = jnp.where(rows + columns == side - 1, 1.0, 0.0).astype(bf16)
    high = value.astype(bf16)
    low = (value - high.astype(f32)).astype(bf16)
    return jnp.dot(high, swap, preferred_element_type=f32) + jnp.dot(
        low, swap, preferred_element_type=f32
    )


def split_store(value, high, low, columns):
    rounded = value.astype(bf16)
    high[:, columns] = rounded
    low[:, columns] = (value - rounded.astype(f32)).astype(bf16)


def power_of(re, im):
    return re * re + im * im + 0.5 * soften_term


def half_bond(first, second):
    cross = first[0] * second[1] - first[1] * second[0]
    return cross / (first[2] + second[2])


def forward_kernel(
    field, halo, even_hi, even_lo, odd_hi, odd_lo, decays, joins,
    solved, carried, incoming, evens,
    source, xeh, xel, xoh, xol, coefs, power, drops, shifts, bonds, partial, afters,
    out, carries, ends, heard, sums, totals, told,
    up_sems, in_sems, over_sems, across_sems, down_sems, back_sems,
):
    angles, _, blocks, strip, _ = field.shape
    width = blocks * LANES
    groups = strip // GROUP
    plane, share = ends.shape[1], ends.shape[2]
    planes = totals.shape[1]
    me = lax.axis_index("tile")
    floor_at, seat = me // plane, lax.rem(me, plane)
    beside = [lax.rem(seat + by, plane) for by in range(1, plane)]
    beyond_planes = [lax.rem(floor_at + by, planes) for by in range(1, planes)]
    barrier = pltpu.get_barrier_semaphore()
    for peer in [floor_at * plane + other for other in beside] + [
        other * plane + seat for other in beyond_planes
    ]:
        pl.semaphore_signal(barrier, inc=1, device_id={"tile": peer}, device_id_type=MESH)

    def hop(source_ref, target_ref, send_sem, recv_sem, peer):
        return pltpu.make_async_remote_copy(
            src_ref=source_ref,
            dst_ref=target_ref,
            send_sem=send_sem,
            recv_sem=recv_sem,
            device_id={"tile": peer},
            device_id_type=MESH,
        )

    def up(part, other, slot):
        return hop(
            ends.at[part, other], heard.at[part, slot], up_sems.at[part, other],
            in_sems.at[part, slot], floor_at * plane + other,
        )

    def over(part, other, slot):
        return hop(
            sums.at[part], totals.at[part, slot], over_sems.at[part, other],
            across_sems.at[part, slot], other * plane + seat,
        )

    def down(part, other, slot):
        return hop(
            told.at[part, other], incoming.at[part, slot], down_sems.at[part, other],
            back_sems.at[part, slot], floor_at * plane + other,
        )

    def gather(part):
        for other in beside:
            up(part, other, seat).start()
        heard[part, seat] = ends[part, seat]

    def spread(part):
        for other in beside:
            up(part, other, other).wait_recv()
        step = joins[part, seat, 0][:, None]
        fall = heard[part, 0, :, :angles]
        rise = heard[part, plane - 1, :, angles:]
        for item in range(1, plane):
            fall = fall * step + heard[part, item, :, :angles]
            rise = rise * step + heard[part, plane - 1 - item, :, angles:]
        sums[part, :, :angles] = fall
        sums[part, :, angles:] = rise
        for other in beyond_planes:
            over(part, other, floor_at).start()
        totals[part, floor_at] = sums[part]

    def answer(part):
        for other in beyond_planes:
            over(part, other, other).wait_recv()
        step, leap, whole, closing, gain = [joins[part, seat, item][:, None] for item in range(5)]
        bottom = totals[part, 0, :, :angles]
        top = totals[part, planes - 1, :, angles:]
        for item in range(1, planes):
            bottom = bottom * leap + totals[part, item, :, :angles]
            top = top * leap + totals[part, planes - 1 - item, :, angles:]
        fall = (top + whole * bottom) * closing
        rise = (bottom + whole * top) * closing
        fall_here, rise_here = fall, rise
        for item in range(planes):
            fall_here = jnp.where(floor_at == item, fall, fall_here)
            fall = fall * leap + totals[part, item, :, :angles]
            back = planes - 1 - item
            rise_here = jnp.where(floor_at == back, rise, rise_here)
            rise = rise * leap + totals[part, back, :, angles:]
        for item in range(plane):
            told[part, item, :, :angles] = fall_here * gain
            fall_here = fall_here * step + heard[part, item, :, :angles]
            back = plane - 1 - item
            told[part, back, :, angles:] = rise_here * gain
            rise_here = rise_here * step + heard[part, back, :, angles:]
        for other in beside:
            down(part, other, seat).start()
        incoming[part, seat] = told[part, seat]

    def learn(part):
        for other in beside:
            down(part, other, other).wait_recv()

    lane = lax.broadcasted_iota(jnp.int32, (GROUP, LANES), 1)
    segment = lax.broadcasted_iota(jnp.int32, (GROUP, LANES), 0)

    for angle in range(angles):

        def rows_of(group):
            return slice(group * GROUP, (group + 1) * GROUP)

        def prepare(block, slot):
            for group in range(groups):
                pair = [field[angle, part, block, rows_of(group)] for part in range(2)]
                power[slot, rows_of(group)] = power_of(*pair)
                for part, value in enumerate(pair):
                    shifts[slot, part, group] = pltpu.roll(value, 1, 1)

        def combine(block, slot):
            where = pl.ds(pl.multiple_of(block * LANES, LANES), LANES)

            def beyond(upper):
                edge, by, border = (0, 1, 0) if upper else (GROUP - 1, GROUP - 1, 1)
                pair = [
                    jnp.where(
                        segment == edge,
                        halo[border, angle, part, :, where],
                        pltpu.roll(field[angle, part, block, rows_of(0 if upper else groups - 1)], by, 0),
                    )
                    for part in range(2)
                ]
                return pair + [power_of(*pair)]

            for group in range(groups):
                here = [field[angle, part, block, rows_of(group)] for part in range(2)]
                here.append(power[slot, rows_of(group)])
                if group == 0:
                    drops[GROUP - 1 : 2 * GROUP - 1] = half_bond(beyond(True), here)
                if group == groups - 1:
                    below = beyond(False)
                else:
                    lower = slice(group * GROUP + 1, (group + 1) * GROUP + 1)
                    below = [field[angle, part, block, lower] for part in range(2)]
                    below.append(power[slot, lower])
                down = half_bond(here, below)
                first = (group + 1) * GROUP
                drops[first : first + GROUP] = down
                up = drops[first - 1 : first - 1 + GROUP]
                left = [
                    jnp.where(lane == 0, shifts[1 - slot, part, group], shifts[slot, part, group])
                    for part in range(2)
                ]
                bond = half_bond(left + [power_of(*left)], here)
                bonds[slot, group] = bond
                partial[slot, group] = up - down + bond

        def finish(block, slot):
            behind = pl.ds(pl.multiple_of(jnp.maximum(block - 1, 0) * LANES, LANES), LANES)
            for group in range(groups):
                after = pltpu.roll(bonds[slot, group], LANES - 1, 1)
                first = angle * strip + group * GROUP
                source[first : first + GROUP, behind] = partial[1 - slot, group] - jnp.where(
                    lane == LANES - 1, after, afters[group]
                )
                afters[group] = after

        def step(pair, _):
            block = 2 * pair
            finish(block - 1, 1)
            combine(block, 0)
            prepare(block + 1, 1)
            finish(block, 0)
            combine(block + 1, 1)
            prepare(jnp.minimum(block + 2, blocks - 1), 0)
            return 0

        for group in range(groups):
            for part in range(2):
                shifts[1, part, group] = jnp.zeros((GROUP, LANES), f32)
        prepare(0, 0)
        lax.fori_loop(0, blocks // 2, step, 0)
        finish(blocks - 1, 1)
        for group in range(groups):
            first = angle * strip + group * GROUP
            source[first : first + GROUP, width - LANES :] = partial[1, group] - jnp.where(
                lane == LANES - 1, 0.0, afters[group]
            )

    half = width // 2

    def tile(index):
        return slice(index * TILE, (index + 1) * TILE)

    def fold(index):
        where = tile(index)
        near = source[:, where]
        far = mirror(source[:, tile(width // TILE - 1 - index)])
        split_store(near + far, xeh, xel, where)
        split_store(near - far, xoh, xol, where)

    for index in range(half // TILE):
        fold(index)
    def transform(part, index):
        high, low, table_hi, table_lo = (
            (xeh, xel, even_hi, even_lo),
            (xoh, xol, odd_hi, odd_lo),
        )[part]
        where = tile(index)
        value = (
            jnp.dot(high[...], table_hi[:, where], preferred_element_type=f32)
            + jnp.dot(low[...], table_hi[:, where], preferred_element_type=f32)
            + jnp.dot(high[...], table_lo[:, where], preferred_element_type=f32)
        )
        for column in range(TILE // LANES):
            block = index * TILE // LANES + column
            coefs[part, block] = value[:, column * LANES : (column + 1) * LANES]

    def scan(part):
        result, carry_ref = ((out, carries), (solved, carried))[part]

        def run(chunk, _):
            table = pl.ds(pl.multiple_of(part * half + chunk * LANES, LANES), LANES)
            owner, place = chunk // share, lax.rem(chunk, share)
            gain = decays[2 * GROUP : 2 * GROUP + 1, table]
            step = decays[3 * GROUP : 3 * GROUP + 1, table]
            for angle in range(angles):
                values = [
                    coefs[part, chunk, pl.ds(angle * strip + group, GROUP, stride=groups)]
                    for group in range(groups)
                ]
                fall, falls = values[0], [values[0]]
                for group in range(1, groups):
                    fall = values[group] + step * fall
                    falls.append(fall)
                rise = values[-1]
                for group in reversed(range(groups)):
                    total = falls[group]
                    if group < groups - 1:
                        later = step * rise
                        total = total + later
                        rise = values[group] + later
                    first = angle * strip + group * GROUP
                    result[chunk, first : first + GROUP] = gain * total
                for index, by in enumerate((1, 2, 4)):
                    jump = decays[2 * GROUP + 1 + index : 2 * GROUP + 2 + index, table]
                    fall = fall + jnp.where(segment >= by, pltpu.roll(fall, by, 0), 0.0) * jump
                    rise = (
                        rise
                        + jnp.where(segment < GROUP - by, pltpu.roll(rise, GROUP - by, 0), 0.0)
                        * jump
                    )
                ends[part, owner, place, angle : angle + 1] = fall[GROUP - 1 :]
                ends[part, owner, place, angles + angle : angles + angle + 1] = rise[:1]
                carry_ref[chunk, angle] = gain * jnp.where(
                    segment >= 1, pltpu.roll(fall, 1, 0), 0.0
                )
                carry_ref[chunk, angles + angle] = gain * jnp.where(
                    segment < GROUP - 1, pltpu.roll(rise, GROUP - 1, 0), 0.0
                )
            return 0

        lax.fori_loop(0, blocks // 2, run, 0, unroll=2)

    tiles = half // TILE
    for index in range(tiles):
        transform(0, index)
    scan(0)
    pl.semaphore_wait(barrier, plane + planes - 2)
    gather(0)
    for index in range(tiles):
        transform(1, index)
    spread(0)
    scan(1)
    gather(1)
    spread(1)
    answer(0)
    learn(0)
    enter(0, out, carries, incoming, decays, xeh, xel)
    for index in range(tiles):
        if index == 1 or tiles == 1:
            answer(1)
        evens[:, tile(index)] = restored(xeh, xel, even_hi, even_lo, tile(index))
    learn(1)
    for part in range(2):
        for other in beside:
            up(part, other, seat).wait_send()
            down(part, other, seat).wait_send()
        for other in beyond_planes:
            over(part, other, floor_at).wait_send()


def enter(part, value, carries, incoming, decays, high, low):
    angles = incoming.shape[3] // 2
    strip = value.shape[1] // angles
    half = value.shape[0] * LANES
    groups = strip // GROUP
    length = min(groups, GROUP)
    share = incoming.shape[2]

    def run(chunk, _):
        where = pl.ds(pl.multiple_of(chunk * LANES, LANES), LANES)
        table = pl.ds(pl.multiple_of(part * half + chunk * LANES, LANES), LANES)
        owner, place = chunk // share, lax.rem(chunk, share)
        for angle in range(angles):
            fall = (
                carries[chunk, angle]
                + decays[:GROUP, table] * incoming[part, owner, place, angle : angle + 1]
            )
            rise = (
                carries[chunk, angles + angle]
                + decays[GROUP : 2 * GROUP, table]
                * incoming[part, owner, place, angles + angle : angles + angle + 1]
            )
            for pair in range(0, strip, 2 * GROUP):
                rows = []
                for row in range(pair, pair + 2 * GROUP, length):
                    owner_row, group = row // groups, row % groups
                    ahead = 3 * GROUP + group
                    behind = ahead + groups
                    rows.append(
                        value[
                            chunk,
                            pl.ds(angle * strip + group * GROUP + owner_row, length, stride=GROUP),
                        ]
                        + decays[ahead : ahead + length, table] * fall[owner_row : owner_row + 1]
                        + decays[behind : behind + length, table] * rise[owner_row : owner_row + 1]
                    )
                item = jnp.concatenate(rows, 0)
                rounded = item.astype(bf16)
                start = angle * strip + pair
                high[start : start + 2 * GROUP, where] = rounded
                low[start : start + 2 * GROUP, where] = (item - rounded.astype(f32)).astype(bf16)
        return 0

    lax.fori_loop(0, half // LANES, run, 0)


def restored(high, low, table_hi, table_lo, where):
    last = (((1,), (1,)), ((), ()))
    return (
        lax.dot_general(high[...], table_hi[where], last, preferred_element_type=f32)
        + lax.dot_general(low[...], table_hi[where], last, preferred_element_type=f32)
        + lax.dot_general(high[...], table_lo[where], last, preferred_element_type=f32)
    )


def inverse_kernel(
    field, value, carries, incoming, evens, odd_hi, odd_lo, decays,
    updated, out, xh, xl, parted, sems, field_sems,
):
    angles, strip, width = out.shape
    half = width // 2
    blocks = width // LANES
    copies = []
    for block in range(blocks):
        copy = pltpu.make_async_copy(
            field.at[:, :, block],
            updated.at[:, :, :, block * LANES : (block + 1) * LANES],
            field_sems.at[block],
        )
        copy.start()
        copies.append(copy)
    enter(1, value, carries, incoming, decays, xh, xl)
    tiles = [slice(first, first + TILE) for first in range(0, half, TILE)]
    later = restored(xh, xl, odd_hi, odd_lo, tiles[0])
    for index, where in enumerate(tiles):
        first, odd, even = where.start, later, evens[:, where]
        if index + 1 < len(tiles):
            later = restored(xh, xl, odd_hi, odd_lo, tiles[index + 1])
        near = even + odd
        far = mirror(even - odd)
        for item, start in ((near, first), (far, width - first - TILE)):
            where = slice(start, start + TILE)
            for angle in range(angles):
                parted[angle, :, where] = item[angle * strip : (angle + 1) * strip]
            copy = pltpu.make_async_copy(
                parted.at[:, :, where], out.at[:, :, where], sems.at[start // TILE]
            )
            copy.start()
            copies.append(copy)
    for copy in copies:
        copy.wait()


def body(object_field, probe, measured, frame_table, frame_count):
    angles, _, strip, width = object_field.shape
    side = probe.shape[1]
    cap = measured.shape[0]
    half = width // 2
    reach = side // strip
    rows = angles * strip
    strips = lax.axis_size("tile")
    blocks = width // LANES
    shape = jax.ShapeDtypeStruct

    pieces = (reach + 1) * cap
    plane = 2 ** (int(math.log2(strips)) // 2)
    share = blocks // (2 * plane)
    decays, joins = decay_tables(width, strip, plane)
    joins = jnp.asarray(joins.reshape(-1, 2, plane, share, LANES).transpose(1, 2, 0, 3, 4))

    factors = cosine_factors(width)
    table = (reach + 1, cap, 2, strip, side)
    held, halo, *half_tables = pl.pallas_call(
        update_kernel,
        out_shape=[
            shape((angles, 2, blocks, strip, LANES), f32),
            shape((2, angles, 2, 1, width), f32),
        ]
        + [shape((half, half), bf16)] * 4,
        in_specs=[smem] + [hbm] * 7,
        out_specs=[vmem] * 6,
        scratch_shapes=[
            pltpu.SMEM((reach + 1, cap, 3), jnp.int32),
            pltpu.SMEM((1,), jnp.int32),
            pltpu.VMEM(probe.shape, f32),
            pltpu.VMEM((side, side), bf16),
            pltpu.VMEM((side, side), bf16),
            pltpu.VMEM(factors.shape, f32),
            pltpu.VMEM(measured.shape, bf16),
            pltpu.VMEM(table, bf16),
            pltpu.VMEM(table, bf16),
            pltpu.VMEM(table, bf16),
            pltpu.VMEM(table, bf16),
            pltpu.VMEM((cap, 2, strip, side), f32),
            pltpu.VMEM((reach + 1, cap, 2, side // LANES + 2, strip, LANES), f32),
            pltpu.VMEM(((reach + 1) * strip, side), f32),
            pltpu.VMEM((2, angles, 2, 1, width), f32),
            pltpu.SemaphoreType.DMA((5 + blocks,)),
            pltpu.SemaphoreType.DMA((2, reach + 1)),
            pltpu.SemaphoreType.DMA((2, 1)),
            pltpu.SemaphoreType.DMA((2, cap)),
            pltpu.SemaphoreType.DMA((2, pieces)),
            pltpu.SemaphoreType.DMA((2, pieces)),
            pltpu.SemaphoreType.DMA((2, 2)),
        ],
        compiler_params=params(collective_id=0, has_side_effects=True),
        cost_estimate=cost(20),
        name="update",
    )(
        frame_count,
        *[
            pltpu.with_memory_space_constraint(item, pltpu.HBM)
            for item in (
                frame_table,
                object_field,
                probe,
                measured,
                *fourier_tables(side),
                factors,
            )
        ],
    )

    planes = strips // plane
    lines = (share, 2 * angles, LANES)
    solved, carried, incoming, evens = pl.pallas_call(
        forward_kernel,
        out_shape=[
            shape((blocks // 2, rows, LANES), f32),
            shape((blocks // 2, 2 * angles, GROUP, LANES), f32),
            shape((2, plane) + lines, f32),
            shape((rows, half), f32),
        ],
        in_specs=[vmem] * 8,
        out_specs=[vmem] * 4,
        scratch_shapes=[pltpu.VMEM((rows, width), f32)]
        + [pltpu.VMEM((rows, half), bf16)] * 4
        + [
            pltpu.VMEM((2, blocks // 2, rows, LANES), f32),
            pltpu.VMEM((2, strip, LANES), f32),
            pltpu.VMEM((strip + GROUP, LANES), f32),
            pltpu.VMEM((2, 2, strip // GROUP, GROUP, LANES), f32),
            pltpu.VMEM((2, strip // GROUP, GROUP, LANES), f32),
            pltpu.VMEM((2, strip // GROUP, GROUP, LANES), f32),
            pltpu.VMEM((strip // GROUP, GROUP, LANES), f32),
            pltpu.VMEM((blocks // 2, rows, LANES), f32),
            pltpu.VMEM((blocks // 2, 2 * angles, GROUP, LANES), f32),
            pltpu.VMEM((2, plane) + lines, f32),
            pltpu.VMEM((2, plane) + lines, f32),
            pltpu.VMEM((2,) + lines, f32),
            pltpu.VMEM((2, planes) + lines, f32),
            pltpu.VMEM((2, plane) + lines, f32),
            pltpu.SemaphoreType.DMA((2, plane)),
            pltpu.SemaphoreType.DMA((2, plane)),
            pltpu.SemaphoreType.DMA((2, planes)),
            pltpu.SemaphoreType.DMA((2, planes)),
            pltpu.SemaphoreType.DMA((2, plane)),
            pltpu.SemaphoreType.DMA((2, plane)),
        ],
        compiler_params=params(collective_id=1, has_side_effects=True),
        cost_estimate=cost(15),
        name="forward",
    )(held, halo, *half_tables, decays, joins)
    updated, phase_map = pl.pallas_call(
        inverse_kernel,
        out_shape=[shape(object_field.shape, f32), shape((angles, strip, width), f32)],
        in_specs=[vmem] * 8,
        out_specs=[hbm, hbm],
        scratch_shapes=[
            pltpu.VMEM((rows, half), bf16),
            pltpu.VMEM((rows, half), bf16),
            pltpu.VMEM((angles, strip, width), f32),
            pltpu.SemaphoreType.DMA((width // TILE,)),
            pltpu.SemaphoreType.DMA((blocks,)),
        ],
        compiler_params=params(),
        cost_estimate=cost(6),
        name="inverse",
    )(held, solved, carried, incoming, evens, *half_tables[2:], decays)
    return (updated, phase_map)


def solution(mesh):
    return jax.shard_map(
        body,
        mesh=mesh,
        in_specs=(
            P("group", None, "tile", None),
            P(),
            P(("group", "tile"), None, None),
            P(("group", "tile"), None),
            P(("group", "tile")),
        ),
        out_specs=(P("group", None, "tile", None), P("group", "tile", None)),
        check_vma=False,
    )
```

```python
import functools
import math

import numpy as np
import jax
import jax.numpy as jnp
from jax import lax
from jax.experimental import pallas as pl
from jax.experimental.pallas import tpu as pltpu
from jax.sharding import PartitionSpec as P

magnitude_floor = 0.5
soften_term = 0.5
screen_term = 0.0001
epsilon_term = 1e-06
f32 = jnp.float32
bf16 = jnp.bfloat16
LANES = 128
GROUP = 8
TILE = 256
VMEM_BYTES = 30 * 1024 * 1024
MESH = pl.DeviceIdType.MESH
vmem = pl.BlockSpec(memory_space=pltpu.VMEM)
smem = pl.BlockSpec(memory_space=pltpu.SMEM)
hbm = pl.BlockSpec(memory_space=pltpu.HBM)


def cost(micros):
    return pl.CostEstimate(
        flops=0, bytes_accessed=int(micros * 3_000_000), transcendentals=0
    )


def params(**more):
    return pltpu.CompilerParams(vmem_limit_bytes=VMEM_BYTES, **more)


def fourier_tables(side):
    indices = np.arange(side)
    products = indices[:, None] * indices[None, :] % side
    phases = products.astype(np.float64) * (-2.0 * math.pi / side)
    scale = 1.0 / math.sqrt(side)
    return (
        jnp.asarray(np.cos(phases) * scale, f32).astype(bf16),
        jnp.asarray(np.sin(phases) * scale, f32).astype(bf16),
    )


def cosine_factors(grid_side):
    half = grid_side // 2
    step = 32
    out = []
    for odd in (0, 1):
        freqs = 2 * np.arange(half) + odd
        scale = np.where(freqs == 0, math.sqrt(1.0 / grid_side), math.sqrt(2.0 / grid_side))
        coarse = (2 * step * np.arange(half // step)[:, None] * freqs[None, :]) % (4 * grid_side)
        fine = ((2 * np.arange(step)[:, None] + 1) * freqs[None, :]) % (4 * grid_side)
        unit = math.pi / (2 * grid_side)
        out.append(
            np.stack(
                [
                    np.cos(coarse * unit) * scale,
                    np.sin(coarse * unit) * scale,
                    np.cos(fine * unit),
                    np.sin(fine * unit),
                ]
            )
        )
    return jnp.asarray(np.stack(out), f32)


def decay_tables(grid_side, strip_rows, plane):
    half = grid_side // 2
    freqs = np.concatenate([2 * np.arange(half), 2 * np.arange(half) + 1]).astype(np.float64)
    shift = screen_term + 2.0 - 2.0 * np.cos(freqs * math.pi / grid_side)
    rate = 2.0 * np.arcsinh(np.sqrt(shift) / 2.0)
    gain = 2.0 / (2.0 * np.sinh(rate))
    groups = strip_rows // GROUP
    segments = np.exp(-groups * np.arange(GROUP)[:, None] * rate)
    steps = np.exp(-(np.arange(groups)[:, None] + 1) * rate)
    jumps = np.exp(-groups * np.array([[1], [2], [4]]) * rate)
    spare = np.zeros((GROUP - 4,) + gain.shape)
    decays = np.concatenate(
        [segments, segments[::-1], gain[None], jumps, spare, steps, steps[::-1]]
    )
    spans = strip_rows * np.array([[1], [plane], [grid_side // strip_rows]])
    closing = 1.0 / (1.0 - np.exp(-2.0 * grid_side * rate))
    joins = np.concatenate([np.exp(-spans * rate), closing[None], gain[None]])
    return decays.astype(np.float32), joins.astype(np.float32)


def table_rows(factors, part, high, low):
    step = factors.shape[2]

    def run(block, _):
        rows = pl.ds(pl.multiple_of(block * step, step), step)
        value = (
            factors[part, 0, pl.ds(block, 1)] * factors[part, 2]
            - factors[part, 1, pl.ds(block, 1)] * factors[part, 3]
        )
        rounded = value.astype(bf16)
        high[rows] = rounded
        low[rows] = (value - rounded.astype(f32)).astype(bf16)
        return 0

    lax.fori_loop(0, high.shape[0] // step, run, 0)


def window_start(column, width, span):
    return jnp.minimum(column // LANES, (width - span) // LANES) * LANES


def power_of(re, im):
    return re * re + im * im + 0.5 * soften_term


def half_bond(first, second):
    cross = first[0] * second[1] - first[1] * second[0]
    return cross / (first[2] + second[2])


def update_kernel(
    frame_count, frame_table, field, probe_in, measured, cos_in, sin_in, factors_in,
    held, source, even_hi, even_lo, odd_hi, odd_lo,
    halo, power, drops, shifts, bonds, partial, afters, tables, counts, probe, cos_ref, sin_ref, factors, moved, cuts, arrived, away, landed,
    own, placed, window, edges,
    load_sems, tell_sems, count_sems, moved_sems, fetch_sems, give_sems, edge_sems,
):
    count = lax.axis_size("tile")
    me = lax.axis_index("tile")
    angles, _, strip, width = field.shape
    cap, side = measured.shape[0], measured.shape[1]
    span = side + LANES
    lanes = span // LANES
    blocks = width // LANES
    reach = tables.shape[0] - 1
    middle = reach // 2
    total = (reach + 1) * strip
    others = [j for j in range(reach + 1) if j != middle]

    def inside(place):
        return (place >= 0) & (place < count)

    def load(index, source, target):
        return pltpu.make_async_copy(source, target, load_sems.at[index])

    loads = [
        load(0, frame_table, tables.at[0]),
        load(1, factors_in, factors),
        load(2, probe_in, probe),
        load(3, cos_in, cos_ref),
        load(4, sin_in, sin_ref),
    ]
    strips = [
        load(5 + block, field.at[:, :, :, block * LANES : (block + 1) * LANES], held.at[:, :, block])
        for block in range(blocks)
    ]
    for item in loads[:2] + strips + loads[2:5]:
        item.start()

    def send(source, target, sems, index, by):
        copy = pltpu.make_async_remote_copy(
            src_ref=source,
            dst_ref=target,
            send_sem=sems.at[0, index],
            recv_sem=sems.at[1, index],
            device_id={"tile": me + by},
            device_id_type=MESH,
        )
        return copy, inside(me + by), inside(me - by)

    barrier = pltpu.get_barrier_semaphore()
    met = jnp.zeros((), jnp.int32)
    for by in [sign * by for by in range(1, reach + 1) for sign in (1, -1)]:

        @pl.when(inside(me + by))
        def _():
            pl.semaphore_signal(
                barrier, inc=1, device_id={"tile": me + by}, device_id_type=MESH
            )

        met = met + jnp.where(inside(me + by), 1, 0)
    pl.semaphore_wait(barrier, met)

    tells = [
        send(tables.at[0], tables.at[j], tell_sems, j, j) for j in range(1, reach + 1)
    ]
    tells.append(send(frame_count, counts, count_sems, 0, middle))
    moves = [
        send(measured.at[s], moved.at[s], moved_sems, s, middle) for s in range(cap)
    ]
    fetches = [
        [send(cuts.at[j, s], arrived.at[j, s], fetch_sems, s * (reach + 1) + j, middle - j) for j in others]
        for s in range(cap)
    ]
    gives = [
        [send(away.at[j, s], landed.at[j, s], give_sems, s * (reach + 1) + j, j - middle) for j in others]
        for s in range(cap)
    ]
    borders = [
        send(edges.at[1], halo.at[0], edge_sems, 0, 1),
        send(edges.at[0], halo.at[1], edge_sems, 1, -1),
    ]
    started = []

    def start(items):
        for copy, sends, takes in items:
            pl.when(sends)(copy.start)
            started.append((copy, sends))

    def arrive(items):
        for copy, sends, takes in items:
            pl.when(takes)(copy.wait_recv)

    def blank(items, wipe):
        for index, (copy, sends, takes) in enumerate(items):

            @pl.when(jnp.logical_not(takes))
            def _():
                wipe(index)

    def wipe_table(index):
        if index == reach:
            counts[0] = 0
        else:
            for s in range(cap):
                for item in range(3):
                    tables[index + 1, s, item] = 0

    def wipe(ref, *first):
        ref[first] = jnp.zeros(ref.shape[len(first):], ref.dtype)

    loads[0].wait()
    start(tells)
    start(moves)
    blank(tells, wipe_table)
    blank(moves, lambda s: wipe(moved, s))
    for s in range(cap):
        blank(fetches[s], lambda index: wipe(arrived, others[index], s))
        blank(gives[s], lambda index: wipe(landed, others[index], s))
    blank(borders, lambda index: wipe(halo, index))
    for j in range(reach + 1):
        for s in range(cap):
            for part in range(2):
                placed[j, s, part, 0] = jnp.zeros((strip, LANES), f32)
    loads[1].wait()
    table_rows(factors, 0, even_hi, even_lo)
    for item in strips:
        item.wait()
    arrive(tells)

    def first_block(j, s):
        return jnp.minimum(tables[j, s, 1] // LANES, blocks - lanes)

    for s in range(cap):
        for j in others + [middle]:
            block = first_block(j, s)
            shift = tables[j, s, 1] - block * LANES
            angle = tables[j, s, 2]
            for part in range(2):
                piece = jnp.concatenate(
                    [held[angle, part, block + lane] for lane in range(lanes)], 1
                )
                turned = pltpu.roll(piece, lax.rem(span - shift, span), 1)
                target = arrived if j == middle else cuts
                target[j, s, part] = turned[:, :side].astype(bf16)
        start(fetches[s])

    table_rows(factors, 1, odd_hi, odd_lo)
    for item in loads[2:5]:
        item.wait()
    cos_part, sin_part = cos_ref[...], sin_ref[...]
    stacked = jnp.concatenate([cos_part, sin_part], 0)
    joined = jnp.concatenate([cos_part, sin_part], 1)
    probe_re, probe_im = probe[0], probe[1]
    peak = jnp.max(probe_re * probe_re + probe_im * probe_im) + epsilon_term

    def left(re, im, sign):
        products = jnp.dot(
            stacked, jnp.concatenate([re, im], 1), preferred_element_type=f32
        )
        cc, ci = products[:side, :side], products[:side, side:]
        sc, si = products[side:, :side], products[side:, side:]
        return (cc - si, ci + sc) if sign > 0 else (cc + si, ci - sc)

    def right(re, im, sign):
        products = jnp.dot(
            jnp.concatenate([re, im], 0), joined, preferred_element_type=f32
        )
        rc, rs = products[:side, :side], products[:side, side:]
        ic, js = products[side:, :side], products[side:, side:]
        return (rc - js, rs + ic) if sign > 0 else (rc + js, ic - rs)

    for s in range(cap):
        arrive(fetches[s])
        offset = tables[middle, s, 0]
        patch = []
        for part in range(2):
            for j in range(reach + 1):
                window[j * strip : (j + 1) * strip] = arrived[j, s, part].astype(f32)
            turned = pltpu.roll(window[...], lax.rem(total - offset, total), 0)
            patch.append(turned[:side])
        wave_re = (probe_re * patch[0] - probe_im * patch[1]).astype(bf16)
        wave_im = (probe_re * patch[1] + probe_im * patch[0]).astype(bf16)
        half_re, half_im = left(wave_re, wave_im, 1)
        spec_re, spec_im = right(half_re.astype(bf16), half_im.astype(bf16), 1)
        amplitude = jnp.sqrt(spec_re * spec_re + spec_im * spec_im)
        if s == 0:
            arrive(moves)
        factor = moved[s].astype(f32) / jnp.maximum(amplitude, magnitude_floor) - 1.0
        back_re, back_im = left(
            (spec_re * factor).astype(bf16), (spec_im * factor).astype(bf16), -1
        )
        corr_re, corr_im = right(back_re.astype(bf16), back_im.astype(bf16), -1)
        live = s < counts[0]
        updates = (
            (probe_re * corr_re + probe_im * corr_im) / peak,
            (probe_re * corr_im - probe_im * corr_re) / peak,
        )
        for part in range(2):
            window[:side] = jnp.where(live, updates[part], 0.0)
            window[side:] = jnp.zeros((total - side, side), f32)
            turned = pltpu.roll(window[...], offset, 0)
            for j in range(reach + 1):
                piece = turned[j * strip : (j + 1) * strip]
                if j == middle:
                    own[s, part] = piece
                else:
                    away[j, s, part] = piece.astype(bf16)
        start(gives[s])

    pad = jnp.zeros((strip, LANES), f32)

    def shifted(source, j, s):
        shift = tables[j, s, 1] - first_block(j, s) * LANES
        for part in range(2):
            value = jnp.concatenate([source[part].astype(f32), pad], 1)
            turned = pltpu.roll(value, shift, 1)
            for lane in range(lanes):
                placed[j, s, part, lane + 1] = turned[:, lane * LANES : (lane + 1) * LANES]

    def add(items, rows):
        def chunk(block, _):
            for angle in range(angles):
                found = []
                for j, s in items:
                    near = block - first_block(j, s)
                    hit = (tables[j, s, 2] == angle) & (near >= 0) & (near < lanes)
                    found.append(jnp.where(hit, near + 1, 0))
                for part in range(2):
                    for row in rows:
                        value = held[angle, part, block, row]
                        for (j, s), index in zip(items, found):
                            value = value + placed[j, s, part, index, row]
                        held[angle, part, block, row] = value
            return 0

        lax.fori_loop(0, blocks, chunk, 0)

    for s in range(cap):
        shifted(own.at[s], middle, s)
    early = [(middle, s) for s in range(cap)]
    for s in range(cap - 1):
        arrive(gives[s])
        for j in others:
            shifted(landed.at[j, s], j, s)
        early += [(j, s) for j in others]
    add(early, [slice(0, strip)])
    arrive(gives[cap - 1])
    for j in others:
        shifted(landed.at[j, cap - 1], j, cap - 1)
    late = [(j, cap - 1) for j in others]
    add(late, [slice(0, GROUP), slice(strip - GROUP, strip)])
    for angle in range(angles):
        for part in range(2):
            for block in range(blocks):
                where = slice(block * LANES, (block + 1) * LANES)
                edges[0, angle, part, :, where] = held[angle, part, block, :1]
                edges[1, angle, part, :, where] = held[angle, part, block, strip - 1 :]
    start(borders)
    add(late, [slice(GROUP, strip - GROUP)])

    groups = strip // GROUP
    lane = lax.broadcasted_iota(jnp.int32, (GROUP, LANES), 1)
    segment = lax.broadcasted_iota(jnp.int32, (GROUP, LANES), 0)
    drops[:GROUP] = jnp.zeros((GROUP, LANES), f32)
    for angle in range(angles):

        def rows_of(group):
            return slice(group * GROUP, (group + 1) * GROUP)

        def prepare(block, slot):
            for group in range(groups):
                pair = [held[angle, part, block, rows_of(group)] for part in range(2)]
                power[slot, rows_of(group)] = power_of(*pair)
                for part, value in enumerate(pair):
                    shifts[slot, part, group] = pltpu.roll(value, 1, 1)

        def combine(block, slot):
            for group in range(groups):
                here = [held[angle, part, block, rows_of(group)] for part in range(2)]
                here.append(power[slot, rows_of(group)])
                if group == groups - 1:
                    below = [
                        jnp.where(segment == GROUP - 1, 0.0, pltpu.roll(value, GROUP - 1, 0))
                        for value in here[:2]
                    ]
                    below.append(power_of(*below))
                else:
                    lower = slice(group * GROUP + 1, (group + 1) * GROUP + 1)
                    below = [held[angle, part, block, lower] for part in range(2)]
                    below.append(power[slot, lower])
                down = half_bond(here, below)
                first = (group + 1) * GROUP
                drops[first : first + GROUP] = down
                up = drops[first - 1 : first - 1 + GROUP]
                left = [
                    jnp.where(lane == 0, shifts[1 - slot, part, group], shifts[slot, part, group])
                    for part in range(2)
                ]
                bond = half_bond(left + [power_of(*left)], here)
                bonds[slot, group] = bond
                partial[slot, group] = up - down + bond

        def finish(block, slot):
            behind = pl.ds(pl.multiple_of(jnp.maximum(block - 1, 0) * LANES, LANES), LANES)
            for group in range(groups):
                after = pltpu.roll(bonds[slot, group], LANES - 1, 1)
                first = angle * strip + group * GROUP
                source[first : first + GROUP, behind] = partial[1 - slot, group] - jnp.where(
                    lane == LANES - 1, after, afters[group]
                )
                afters[group] = after

        def step(pair, _):
            block = 2 * pair
            finish(block - 1, 1)
            combine(block, 0)
            prepare(block + 1, 1)
            finish(block, 0)
            combine(block + 1, 1)
            prepare(jnp.minimum(block + 2, blocks - 1), 0)
            return 0

        for group in range(groups):
            for part in range(2):
                shifts[1, part, group] = jnp.zeros((GROUP, LANES), f32)
        prepare(0, 0)
        lax.fori_loop(0, blocks // 2, step, 0)
        finish(blocks - 1, 1)
        for group in range(groups):
            first = angle * strip + group * GROUP
            source[first : first + GROUP, width - LANES :] = partial[1, group] - jnp.where(
                lane == LANES - 1, 0.0, afters[group]
            )

    arrive(borders)

    def line(values):
        return values + [power_of(*values)]

    for angle in range(angles):
        for border, row in ((0, 0), (1, strip - 1)):
            inner = line(
                [
                    jnp.concatenate(
                        [held[angle, part, block, row : row + 1] for block in range(blocks)], 1
                    )
                    for part in range(2)
                ]
            )
            outer = line([halo[border, angle, part] for part in range(2)])
            place = slice(angle * strip + row, angle * strip + row + 1)
            source[place] = source[place] + half_bond(outer, inner)
    for copy, sends in started:
        pl.when(sends)(copy.wait_send)


def mirror(value):
    side = value.shape[1]
    rows = lax.broadcasted_iota(jnp.int32, (side, side), 0)
    columns = lax.broadcasted_iota(jnp.int32, (side, side), 1)
    swap = jnp.where(rows + columns == side - 1, 1.0, 0.0).astype(bf16)
    high = value.astype(bf16)
    low = (value - high.astype(f32)).astype(bf16)
    return jnp.dot(high, swap, preferred_element_type=f32) + jnp.dot(
        low, swap, preferred_element_type=f32
    )


def split_store(value, high, low, columns):
    rounded = value.astype(bf16)
    high[:, columns] = rounded
    low[:, columns] = (value - rounded.astype(f32)).astype(bf16)


def forward_kernel(
    source, even_hi, even_lo, odd_hi, odd_lo, decays, joins,
    solved, carried, incoming, evens,
    xeh, xel, xoh, xol, coefs,
    out, carries, ends, heard, sums, totals, told,
    up_sems, in_sems, over_sems, across_sems, down_sems, back_sems,
):
    angles, width = ends.shape[3] // 2, source.shape[1]
    strip, blocks = source.shape[0] // angles, width // LANES
    groups = strip // GROUP
    plane, share = ends.shape[1], ends.shape[2]
    planes = totals.shape[1]
    me = lax.axis_index("tile")
    floor_at, seat = me // plane, lax.rem(me, plane)
    beside = [lax.rem(seat + by, plane) for by in range(1, plane)]
    beyond_planes = [lax.rem(floor_at + by, planes) for by in range(1, planes)]
    barrier = pltpu.get_barrier_semaphore()
    for peer in [floor_at * plane + other for other in beside] + [
        other * plane + seat for other in beyond_planes
    ]:
        pl.semaphore_signal(barrier, inc=1, device_id={"tile": peer}, device_id_type=MESH)

    def hop(source_ref, target_ref, send_sem, recv_sem, peer):
        return pltpu.make_async_remote_copy(
            src_ref=source_ref,
            dst_ref=target_ref,
            send_sem=send_sem,
            recv_sem=recv_sem,
            device_id={"tile": peer},
            device_id_type=MESH,
        )

    def up(part, other, slot):
        return hop(
            ends.at[part, other], heard.at[part, slot], up_sems.at[part, other],
            in_sems.at[part, slot], floor_at * plane + other,
        )

    def over(part, other, slot):
        return hop(
            sums.at[part], totals.at[part, slot], over_sems.at[part, other],
            across_sems.at[part, slot], other * plane + seat,
        )

    def down(part, other, slot):
        return hop(
            told.at[part, other], incoming.at[part, slot], down_sems.at[part, other],
            back_sems.at[part, slot], floor_at * plane + other,
        )

    def gather(part):
        for other in beside:
            up(part, other, seat).start()
        heard[part, seat] = ends[part, seat]

    def spread(part):
        for other in beside:
            up(part, other, other).wait_recv()
        step = joins[part, seat, 0][:, None]
        fall = heard[part, 0, :, :angles]
        rise = heard[part, plane - 1, :, angles:]
        for item in range(1, plane):
            fall = fall * step + heard[part, item, :, :angles]
            rise = rise * step + heard[part, plane - 1 - item, :, angles:]
        sums[part, :, :angles] = fall
        sums[part, :, angles:] = rise
        for other in beyond_planes:
            over(part, other, floor_at).start()
        totals[part, floor_at] = sums[part]

    def answer(part):
        for other in beyond_planes:
            over(part, other, other).wait_recv()
        step, leap, whole, closing, gain = [joins[part, seat, item][:, None] for item in range(5)]
        bottom = totals[part, 0, :, :angles]
        top = totals[part, planes - 1, :, angles:]
        for item in range(1, planes):
            bottom = bottom * leap + totals[part, item, :, :angles]
            top = top * leap + totals[part, planes - 1 - item, :, angles:]
        fall = (top + whole * bottom) * closing
        rise = (bottom + whole * top) * closing
        fall_here, rise_here = fall, rise
        for item in range(planes):
            fall_here = jnp.where(floor_at == item, fall, fall_here)
            fall = fall * leap + totals[part, item, :, :angles]
            back = planes - 1 - item
            rise_here = jnp.where(floor_at == back, rise, rise_here)
            rise = rise * leap + totals[part, back, :, angles:]
        for item in range(plane):
            told[part, item, :, :angles] = fall_here * gain
            fall_here = fall_here * step + heard[part, item, :, :angles]
            back = plane - 1 - item
            told[part, back, :, angles:] = rise_here * gain
            rise_here = rise_here * step + heard[part, back, :, angles:]
        for other in beside:
            down(part, other, seat).start()
        incoming[part, seat] = told[part, seat]

    def learn(part):
        for other in beside:
            down(part, other, other).wait_recv()

    segment = lax.broadcasted_iota(jnp.int32, (GROUP, LANES), 0)
    half = width // 2

    def tile(index):
        return slice(index * TILE, (index + 1) * TILE)

    def fold(index):
        where = tile(index)
        near = source[:, where]
        far = mirror(source[:, tile(width // TILE - 1 - index)])
        split_store(near + far, xeh, xel, where)
        split_store(near - far, xoh, xol, where)

    for index in range(half // TILE):
        fold(index)
    def transform(part, index):
        high, low, table_hi, table_lo = (
            (xeh, xel, even_hi, even_lo),
            (xoh, xol, odd_hi, odd_lo),
        )[part]
        where = tile(index)
        value = (
            jnp.dot(high[...], table_hi[:, where], preferred_element_type=f32)
            + jnp.dot(low[...], table_hi[:, where], preferred_element_type=f32)
            + jnp.dot(high[...], table_lo[:, where], preferred_element_type=f32)
        )
        for column in range(TILE // LANES):
            block = index * TILE // LANES + column
            coefs[part, block] = value[:, column * LANES : (column + 1) * LANES]

    def scan(part):
        result, carry_ref = ((out, carries), (solved, carried))[part]

        def run(chunk, _):
            table = pl.ds(pl.multiple_of(part * half + chunk * LANES, LANES), LANES)
            owner, place = chunk // share, lax.rem(chunk, share)
            gain = decays[2 * GROUP : 2 * GROUP + 1, table]
            step = decays[3 * GROUP : 3 * GROUP + 1, table]
            for angle in range(angles):
                values = [
                    coefs[part, chunk, pl.ds(angle * strip + group, GROUP, stride=groups)]
                    for group in range(groups)
                ]
                fall, falls = values[0], [values[0]]
                for group in range(1, groups):
                    fall = values[group] + step * fall
                    falls.append(fall)
                rise = values[-1]
                for group in reversed(range(groups)):
                    total = falls[group]
                    if group < groups - 1:
                        later = step * rise
                        total = total + later
                        rise = values[group] + later
                    first = angle * strip + group * GROUP
                    result[chunk, first : first + GROUP] = gain * total
                for index, by in enumerate((1, 2, 4)):
                    jump = decays[2 * GROUP + 1 + index : 2 * GROUP + 2 + index, table]
                    fall = fall + jnp.where(segment >= by, pltpu.roll(fall, by, 0), 0.0) * jump
                    rise = (
                        rise
                        + jnp.where(segment < GROUP - by, pltpu.roll(rise, GROUP - by, 0), 0.0)
                        * jump
                    )
                ends[part, owner, place, angle : angle + 1] = fall[GROUP - 1 :]
                ends[part, owner, place, angles + angle : angles + angle + 1] = rise[:1]
                carry_ref[chunk, angle] = gain * jnp.where(
                    segment >= 1, pltpu.roll(fall, 1, 0), 0.0
                )
                carry_ref[chunk, angles + angle] = gain * jnp.where(
                    segment < GROUP - 1, pltpu.roll(rise, GROUP - 1, 0), 0.0
                )
            return 0

        lax.fori_loop(0, blocks // 2, run, 0, unroll=2)

    tiles = half // TILE
    for index in range(tiles):
        transform(0, index)
    scan(0)
    pl.semaphore_wait(barrier, plane + planes - 2)
    gather(0)
    for index in range(tiles):
        transform(1, index)
    spread(0)
    scan(1)
    gather(1)
    spread(1)
    answer(0)
    learn(0)
    enter(0, out, carries, incoming, decays, xeh, xel)
    for index in range(tiles):
        if index == 1 or tiles == 1:
            answer(1)
        evens[:, tile(index)] = restored(xeh, xel, even_hi, even_lo, tile(index))
    learn(1)
    for part in range(2):
        for other in beside:
            up(part, other, seat).wait_send()
            down(part, other, seat).wait_send()
        for other in beyond_planes:
            over(part, other, floor_at).wait_send()


def enter(part, value, carries, incoming, decays, high, low):
    angles = incoming.shape[3] // 2
    strip = value.shape[1] // angles
    half = value.shape[0] * LANES
    groups = strip // GROUP
    length = min(groups, GROUP)
    share = incoming.shape[2]

    def run(chunk, _):
        where = pl.ds(pl.multiple_of(chunk * LANES, LANES), LANES)
        table = pl.ds(pl.multiple_of(part * half + chunk * LANES, LANES), LANES)
        owner, place = chunk // share, lax.rem(chunk, share)
        for angle in range(angles):
            fall = (
                carries[chunk, angle]
                + decays[:GROUP, table] * incoming[part, owner, place, angle : angle + 1]
            )
            rise = (
                carries[chunk, angles + angle]
                + decays[GROUP : 2 * GROUP, table]
                * incoming[part, owner, place, angles + angle : angles + angle + 1]
            )
            for pair in range(0, strip, 2 * GROUP):
                rows = []
                for row in range(pair, pair + 2 * GROUP, length):
                    owner_row, group = row // groups, row % groups
                    ahead = 3 * GROUP + group
                    behind = ahead + groups
                    rows.append(
                        value[
                            chunk,
                            pl.ds(angle * strip + group * GROUP + owner_row, length, stride=GROUP),
                        ]
                        + decays[ahead : ahead + length, table] * fall[owner_row : owner_row + 1]
                        + decays[behind : behind + length, table] * rise[owner_row : owner_row + 1]
                    )
                item = jnp.concatenate(rows, 0)
                rounded = item.astype(bf16)
                start = angle * strip + pair
                high[start : start + 2 * GROUP, where] = rounded
                low[start : start + 2 * GROUP, where] = (item - rounded.astype(f32)).astype(bf16)
        return 0

    lax.fori_loop(0, half // LANES, run, 0)


def restored(high, low, table_hi, table_lo, where):
    last = (((1,), (1,)), ((), ()))
    return (
        lax.dot_general(high[...], table_hi[where], last, preferred_element_type=f32)
        + lax.dot_general(low[...], table_hi[where], last, preferred_element_type=f32)
        + lax.dot_general(high[...], table_lo[where], last, preferred_element_type=f32)
    )


def inverse_kernel(
    field, value, carries, incoming, evens, odd_hi, odd_lo, decays,
    updated, out, xh, xl, parted, sems, field_sems,
):
    angles, strip, width = out.shape
    half = width // 2
    blocks = width // LANES
    copies = []
    for block in range(blocks):
        copy = pltpu.make_async_copy(
            field.at[:, :, block],
            updated.at[:, :, :, block * LANES : (block + 1) * LANES],
            field_sems.at[block],
        )
        copy.start()
        copies.append(copy)
    enter(1, value, carries, incoming, decays, xh, xl)
    tiles = [slice(first, first + TILE) for first in range(0, half, TILE)]
    later = restored(xh, xl, odd_hi, odd_lo, tiles[0])
    for index, where in enumerate(tiles):
        first, odd, even = where.start, later, evens[:, where]
        if index + 1 < len(tiles):
            later = restored(xh, xl, odd_hi, odd_lo, tiles[index + 1])
        near = even + odd
        far = mirror(even - odd)
        for item, start in ((near, first), (far, width - first - TILE)):
            where = slice(start, start + TILE)
            for angle in range(angles):
                parted[angle, :, where] = item[angle * strip : (angle + 1) * strip]
            copy = pltpu.make_async_copy(
                parted.at[:, :, where], out.at[:, :, where], sems.at[start // TILE]
            )
            copy.start()
            copies.append(copy)
    for copy in copies:
        copy.wait()


def body(object_field, probe, measured, frame_table, frame_count):
    angles, _, strip, width = object_field.shape
    side = probe.shape[1]
    cap = measured.shape[0]
    half = width // 2
    reach = side // strip
    rows = angles * strip
    strips = lax.axis_size("tile")
    blocks = width // LANES
    shape = jax.ShapeDtypeStruct

    pieces = (reach + 1) * cap
    plane = 2 ** (int(math.log2(strips)) // 2)
    share = blocks // (2 * plane)
    decays, joins = decay_tables(width, strip, plane)
    joins = jnp.asarray(joins.reshape(-1, 2, plane, share, LANES).transpose(1, 2, 0, 3, 4))

    factors = cosine_factors(width)
    table = (reach + 1, cap, 2, strip, side)
    held, source, *half_tables = pl.pallas_call(
        update_kernel,
        out_shape=[
            shape((angles, 2, blocks, strip, LANES), f32),
            shape((rows, width), f32),
        ]
        + [shape((half, half), bf16)] * 4,
        in_specs=[smem] + [hbm] * 7,
        out_specs=[vmem] * 6,
        scratch_shapes=[
            pltpu.VMEM((2, angles, 2, 1, width), f32),
            pltpu.VMEM((2, strip, LANES), f32),
            pltpu.VMEM((strip + GROUP, LANES), f32),
            pltpu.VMEM((2, 2, strip // GROUP, GROUP, LANES), f32),
            pltpu.VMEM((2, strip // GROUP, GROUP, LANES), f32),
            pltpu.VMEM((2, strip // GROUP, GROUP, LANES), f32),
            pltpu.VMEM((strip // GROUP, GROUP, LANES), f32),
            pltpu.SMEM((reach + 1, cap, 3), jnp.int32),
            pltpu.SMEM((1,), jnp.int32),
            pltpu.VMEM(probe.shape, f32),
            pltpu.VMEM((side, side), bf16),
            pltpu.VMEM((side, side), bf16),
            pltpu.VMEM(factors.shape, f32),
            pltpu.VMEM(measured.shape, bf16),
            pltpu.VMEM(table, bf16),
            pltpu.VMEM(table, bf16),
            pltpu.VMEM(table, bf16),
            pltpu.VMEM(table, bf16),
            pltpu.VMEM((cap, 2, strip, side), f32),
            pltpu.VMEM((reach + 1, cap, 2, side // LANES + 2, strip, LANES), f32),
            pltpu.VMEM(((reach + 1) * strip, side), f32),
            pltpu.VMEM((2, angles, 2, 1, width), f32),
            pltpu.SemaphoreType.DMA((5 + blocks,)),
            pltpu.SemaphoreType.DMA((2, reach + 1)),
            pltpu.SemaphoreType.DMA((2, 1)),
            pltpu.SemaphoreType.DMA((2, cap)),
            pltpu.SemaphoreType.DMA((2, pieces)),
            pltpu.SemaphoreType.DMA((2, pieces)),
            pltpu.SemaphoreType.DMA((2, 2)),
        ],
        compiler_params=params(collective_id=0, has_side_effects=True),
        cost_estimate=cost(20),
        name="update",
    )(
        frame_count,
        *[
            pltpu.with_memory_space_constraint(item, pltpu.HBM)
            for item in (
                frame_table,
                object_field,
                probe,
                measured,
                *fourier_tables(side),
                factors,
            )
        ],
    )

    planes = strips // plane
    lines = (share, 2 * angles, LANES)
    solved, carried, incoming, evens = pl.pallas_call(
        forward_kernel,
        out_shape=[
            shape((blocks // 2, rows, LANES), f32),
            shape((blocks // 2, 2 * angles, GROUP, LANES), f32),
            shape((2, plane) + lines, f32),
            shape((rows, half), f32),
        ],
        in_specs=[vmem] * 7,
        out_specs=[vmem] * 4,
        scratch_shapes=[pltpu.VMEM((rows, half), bf16)] * 4
        + [
            pltpu.VMEM((2, blocks // 2, rows, LANES), f32),
            pltpu.VMEM((blocks // 2, rows, LANES), f32),
            pltpu.VMEM((blocks // 2, 2 * angles, GROUP, LANES), f32),
            pltpu.VMEM((2, plane) + lines, f32),
            pltpu.VMEM((2, plane) + lines, f32),
            pltpu.VMEM((2,) + lines, f32),
            pltpu.VMEM((2, planes) + lines, f32),
            pltpu.VMEM((2, plane) + lines, f32),
            pltpu.SemaphoreType.DMA((2, plane)),
            pltpu.SemaphoreType.DMA((2, plane)),
            pltpu.SemaphoreType.DMA((2, planes)),
            pltpu.SemaphoreType.DMA((2, planes)),
            pltpu.SemaphoreType.DMA((2, plane)),
            pltpu.SemaphoreType.DMA((2, plane)),
        ],
        compiler_params=params(collective_id=1, has_side_effects=True),
        cost_estimate=cost(15),
        name="forward",
    )(source, *half_tables, decays, joins)
    updated, phase_map = pl.pallas_call(
        inverse_kernel,
        out_shape=[shape(object_field.shape, f32), shape((angles, strip, width), f32)],
        in_specs=[vmem] * 8,
        out_specs=[hbm, hbm],
        scratch_shapes=[
            pltpu.VMEM((rows, half), bf16),
            pltpu.VMEM((rows, half), bf16),
            pltpu.VMEM((angles, strip, width), f32),
            pltpu.SemaphoreType.DMA((width // TILE,)),
            pltpu.SemaphoreType.DMA((blocks,)),
        ],
        compiler_params=params(),
        cost_estimate=cost(6),
        name="inverse",
    )(held, solved, carried, incoming, evens, *half_tables[2:], decays)
    return (updated, phase_map)


def solution(mesh):
    return jax.shard_map(
        body,
        mesh=mesh,
        in_specs=(
            P("group", None, "tile", None),
            P(),
            P(("group", "tile"), None, None),
            P(("group", "tile"), None),
            P(("group", "tile")),
        ),
        out_specs=(P("group", None, "tile", None), P("group", "tile", None)),
        check_vma=False,
    )
```

```python
import functools
import math

import numpy as np
import jax
import jax.numpy as jnp
from jax import lax
from jax.experimental import pallas as pl
from jax.experimental.pallas import tpu as pltpu
from jax.sharding import PartitionSpec as P

magnitude_floor = 0.5
soften_term = 0.5
screen_term = 0.0001
epsilon_term = 1e-06
f32 = jnp.float32
bf16 = jnp.bfloat16
LANES = 128
GROUP = 8
TILE = 256
VMEM_BYTES = 30 * 1024 * 1024
MESH = pl.DeviceIdType.MESH
vmem = pl.BlockSpec(memory_space=pltpu.VMEM)
smem = pl.BlockSpec(memory_space=pltpu.SMEM)
hbm = pl.BlockSpec(memory_space=pltpu.HBM)


def cost(micros):
    return pl.CostEstimate(
        flops=0, bytes_accessed=int(micros * 3_000_000), transcendentals=0
    )


def params(**more):
    return pltpu.CompilerParams(vmem_limit_bytes=VMEM_BYTES, **more)


def fourier_tables(side):
    indices = np.arange(side)
    products = indices[:, None] * indices[None, :] % side
    phases = products.astype(np.float64) * (-2.0 * math.pi / side)
    scale = 1.0 / math.sqrt(side)
    return (
        jnp.asarray(np.cos(phases) * scale, f32).astype(bf16),
        jnp.asarray(np.sin(phases) * scale, f32).astype(bf16),
    )


def frequencies(grid_side):
    quarter = np.arange(grid_side // 4)
    even = np.concatenate([4 * quarter, 4 * quarter + 2])
    return even, 2 * np.arange(grid_side // 2) + 1


def cosine_factors(grid_side):
    half = grid_side // 2
    step = 32
    out = []
    for freqs in frequencies(grid_side):
        scale = np.where(freqs == 0, math.sqrt(1.0 / grid_side), math.sqrt(2.0 / grid_side))
        coarse = (2 * step * np.arange(half // step)[:, None] * freqs[None, :]) % (4 * grid_side)
        fine = ((2 * np.arange(step)[:, None] + 1) * freqs[None, :]) % (4 * grid_side)
        unit = math.pi / (2 * grid_side)
        out.append(
            np.stack(
                [
                    np.cos(coarse * unit) * scale,
                    np.sin(coarse * unit) * scale,
                    np.cos(fine * unit),
                    np.sin(fine * unit),
                ]
            )
        )
    return jnp.asarray(np.stack(out), f32)


def decay_tables(grid_side, strip_rows, plane):
    half = grid_side // 2
    freqs = np.concatenate(frequencies(grid_side)).astype(np.float64)
    shift = screen_term + 2.0 - 2.0 * np.cos(freqs * math.pi / grid_side)
    rate = 2.0 * np.arcsinh(np.sqrt(shift) / 2.0)
    gain = 2.0 / (2.0 * np.sinh(rate))
    groups = strip_rows // GROUP
    segments = np.exp(-groups * np.arange(GROUP)[:, None] * rate)
    steps = np.exp(-(np.arange(groups)[:, None] + 1) * rate)
    jumps = np.exp(-groups * np.array([[1], [2], [4]]) * rate)
    spare = np.zeros((GROUP - 4,) + gain.shape)
    decays = np.concatenate(
        [segments, segments[::-1], gain[None], jumps, spare, steps, steps[::-1]]
    )
    spans = strip_rows * np.array([[1], [plane], [grid_side // strip_rows]])
    closing = 1.0 / (1.0 - np.exp(-2.0 * grid_side * rate))
    joins = np.concatenate([np.exp(-spans * rate), closing[None], gain[None]])
    return decays.astype(np.float32), joins.astype(np.float32)


def table_rows(factors, part, high, low):
    step = factors.shape[2]

    def run(block, _):
        rows = pl.ds(pl.multiple_of(block * step, step), step)
        value = (
            factors[part, 0, pl.ds(block, 1)] * factors[part, 2]
            - factors[part, 1, pl.ds(block, 1)] * factors[part, 3]
        )
        rounded = value.astype(bf16)
        high[rows] = rounded
        low[rows] = (value - rounded.astype(f32)).astype(bf16)
        return 0

    lax.fori_loop(0, high.shape[0] // step, run, 0)


def window_start(column, width, span):
    return jnp.minimum(column // LANES, (width - span) // LANES) * LANES


def power_of(re, im):
    return re * re + im * im + 0.5 * soften_term


def half_bond(first, second):
    cross = first[0] * second[1] - first[1] * second[0]
    return cross / (first[2] + second[2])


def update_kernel(
    frame_count, frame_table, field, probe_in, measured, cos_in, sin_in, factors_in,
    held, source, even_hi, even_lo, odd_hi, odd_lo,
    halo, power, drops, shifts, bonds, partial, afters, tables, counts, probe, cos_ref, sin_ref, factors, moved, cuts, arrived, away, landed,
    own, placed, window, edges,
    load_sems, tell_sems, count_sems, moved_sems, fetch_sems, give_sems, edge_sems,
):
    count = lax.axis_size("tile")
    me = lax.axis_index("tile")
    angles, _, strip, width = field.shape
    cap, side = measured.shape[0], measured.shape[1]
    span = side + LANES
    lanes = span // LANES
    blocks = width // LANES
    reach = tables.shape[0] - 1
    middle = reach // 2
    total = (reach + 1) * strip
    others = [j for j in range(reach + 1) if j != middle]

    def inside(place):
        return (place >= 0) & (place < count)

    def load(index, source, target):
        return pltpu.make_async_copy(source, target, load_sems.at[index])

    loads = [
        load(0, frame_table, tables.at[0]),
        load(1, factors_in, factors),
        load(2, probe_in, probe),
        load(3, cos_in, cos_ref),
        load(4, sin_in, sin_ref),
    ]
    strips = [
        load(5 + block, field.at[:, :, :, block * LANES : (block + 1) * LANES], held.at[:, :, block])
        for block in range(blocks)
    ]
    for item in loads[:2] + strips + loads[2:5]:
        item.start()

    def send(source, target, sems, index, by):
        copy = pltpu.make_async_remote_copy(
            src_ref=source,
            dst_ref=target,
            send_sem=sems.at[0, index],
            recv_sem=sems.at[1, index],
            device_id={"tile": me + by},
            device_id_type=MESH,
        )
        return copy, inside(me + by), inside(me - by)

    barrier = pltpu.get_barrier_semaphore()
    met = jnp.zeros((), jnp.int32)
    for by in [sign * by for by in range(1, reach + 1) for sign in (1, -1)]:

        @pl.when(inside(me + by))
        def _():
            pl.semaphore_signal(
                barrier, inc=1, device_id={"tile": me + by}, device_id_type=MESH
            )

        met = met + jnp.where(inside(me + by), 1, 0)
    pl.semaphore_wait(barrier, met)

    tells = [
        send(tables.at[0], tables.at[j], tell_sems, j, j) for j in range(1, reach + 1)
    ]
    tells.append(send(frame_count, counts, count_sems, 0, middle))
    moves = [
        send(measured.at[s], moved.at[s], moved_sems, s, middle) for s in range(cap)
    ]
    fetches = [
        [send(cuts.at[j, s], arrived.at[j, s], fetch_sems, s * (reach + 1) + j, middle - j) for j in others]
        for s in range(cap)
    ]
    gives = [
        [send(away.at[j, s], landed.at[j, s], give_sems, s * (reach + 1) + j, j - middle) for j in others]
        for s in range(cap)
    ]
    borders = [
        send(edges.at[1], halo.at[0], edge_sems, 0, 1),
        send(edges.at[0], halo.at[1], edge_sems, 1, -1),
    ]
    started = []

    def start(items):
        for copy, sends, takes in items:
            pl.when(sends)(copy.start)
            started.append((copy, sends))

    def arrive(items):
        for copy, sends, takes in items:
            pl.when(takes)(copy.wait_recv)

    def blank(items, wipe):
        for index, (copy, sends, takes) in enumerate(items):

            @pl.when(jnp.logical_not(takes))
            def _():
                wipe(index)

    def wipe_table(index):
        if index == reach:
            counts[0] = 0
        else:
            for s in range(cap):
                for item in range(3):
                    tables[index + 1, s, item] = 0

    def wipe(ref, *first):
        ref[first] = jnp.zeros(ref.shape[len(first):], ref.dtype)

    loads[0].wait()
    start(tells)
    start(moves)
    blank(tells, wipe_table)
    blank(moves, lambda s: wipe(moved, s))
    for s in range(cap):
        blank(fetches[s], lambda index: wipe(arrived, others[index], s))
        blank(gives[s], lambda index: wipe(landed, others[index], s))
    blank(borders, lambda index: wipe(halo, index))
    for j in range(reach + 1):
        for s in range(cap):
            for part in range(2):
                placed[j, s, part, 0] = jnp.zeros((strip, LANES), f32)
    loads[1].wait()
    table_rows(factors, 0, even_hi, even_lo)
    for item in strips:
        item.wait()
    arrive(tells)

    def first_block(j, s):
        return jnp.minimum(tables[j, s, 1] // LANES, blocks - lanes)

    for s in range(cap):
        for j in others + [middle]:
            block = first_block(j, s)
            shift = tables[j, s, 1] - block * LANES
            angle = tables[j, s, 2]
            for part in range(2):
                piece = jnp.concatenate(
                    [held[angle, part, block + lane] for lane in range(lanes)], 1
                )
                turned = pltpu.roll(piece, lax.rem(span - shift, span), 1)
                target = arrived if j == middle else cuts
                target[j, s, part] = turned[:, :side].astype(bf16)
        start(fetches[s])

    table_rows(factors, 1, odd_hi, odd_lo)
    for item in loads[2:5]:
        item.wait()
    cos_part, sin_part = cos_ref[...], sin_ref[...]
    stacked = jnp.concatenate([cos_part, sin_part], 0)
    joined = jnp.concatenate([cos_part, sin_part], 1)
    probe_re, probe_im = probe[0], probe[1]
    peak = jnp.max(probe_re * probe_re + probe_im * probe_im) + epsilon_term

    def left(re, im, sign):
        products = jnp.dot(
            stacked, jnp.concatenate([re, im], 1), preferred_element_type=f32
        )
        cc, ci = products[:side, :side], products[:side, side:]
        sc, si = products[side:, :side], products[side:, side:]
        return (cc - si, ci + sc) if sign > 0 else (cc + si, ci - sc)

    def right(re, im, sign):
        products = jnp.dot(
            jnp.concatenate([re, im], 0), joined, preferred_element_type=f32
        )
        rc, rs = products[:side, :side], products[:side, side:]
        ic, js = products[side:, :side], products[side:, side:]
        return (rc - js, rs + ic) if sign > 0 else (rc + js, ic - rs)

    for s in range(cap):
        arrive(fetches[s])
        offset = tables[middle, s, 0]
        patch = []
        for part in range(2):
            for j in range(reach + 1):
                window[j * strip : (j + 1) * strip] = arrived[j, s, part].astype(f32)
            turned = pltpu.roll(window[...], lax.rem(total - offset, total), 0)
            patch.append(turned[:side])
        wave_re = (probe_re * patch[0] - probe_im * patch[1]).astype(bf16)
        wave_im = (probe_re * patch[1] + probe_im * patch[0]).astype(bf16)
        half_re, half_im = left(wave_re, wave_im, 1)
        spec_re, spec_im = right(half_re.astype(bf16), half_im.astype(bf16), 1)
        amplitude = jnp.sqrt(spec_re * spec_re + spec_im * spec_im)
        arrive(moves[s : s + 1])
        factor = moved[s].astype(f32) / jnp.maximum(amplitude, magnitude_floor) - 1.0
        back_re, back_im = left(
            (spec_re * factor).astype(bf16), (spec_im * factor).astype(bf16), -1
        )
        corr_re, corr_im = right(back_re.astype(bf16), back_im.astype(bf16), -1)
        live = s < counts[0]
        updates = (
            (probe_re * corr_re + probe_im * corr_im) / peak,
            (probe_re * corr_im - probe_im * corr_re) / peak,
        )
        for part in range(2):
            window[:side] = jnp.where(live, updates[part], 0.0)
            window[side:] = jnp.zeros((total - side, side), f32)
            turned = pltpu.roll(window[...], offset, 0)
            for j in range(reach + 1):
                piece = turned[j * strip : (j + 1) * strip]
                if j == middle:
                    own[s, part] = piece
                else:
                    away[j, s, part] = piece.astype(bf16)
        start(gives[s])

    pad = jnp.zeros((strip, LANES), f32)

    def shifted(source, j, s):
        shift = tables[j, s, 1] - first_block(j, s) * LANES
        for part in range(2):
            value = jnp.concatenate([source[part].astype(f32), pad], 1)
            turned = pltpu.roll(value, shift, 1)
            for lane in range(lanes):
                placed[j, s, part, lane + 1] = turned[:, lane * LANES : (lane + 1) * LANES]

    def add(items, rows):
        def chunk(block, _):
            for angle in range(angles):
                found = []
                for j, s in items:
                    near = block - first_block(j, s)
                    hit = (tables[j, s, 2] == angle) & (near >= 0) & (near < lanes)
                    found.append(jnp.where(hit, near + 1, 0))
                for part in range(2):
                    for row in rows:
                        value = held[angle, part, block, row]
                        for (j, s), index in zip(items, found):
                            value = value + placed[j, s, part, index, row]
                        held[angle, part, block, row] = value
            return 0

        lax.fori_loop(0, blocks, chunk, 0)

    for s in range(cap):
        shifted(own.at[s], middle, s)
    early = [(middle, s) for s in range(cap)]
    for s in range(cap - 1):
        arrive(gives[s])
        for j in others:
            shifted(landed.at[j, s], j, s)
        early += [(j, s) for j in others]
    add(early, [slice(0, strip)])
    arrive(gives[cap - 1])
    for j in others:
        shifted(landed.at[j, cap - 1], j, cap - 1)
    late = [(j, cap - 1) for j in others]
    add(late, [slice(0, GROUP), slice(strip - GROUP, strip)])
    for angle in range(angles):
        for part in range(2):
            for block in range(blocks):
                where = slice(block * LANES, (block + 1) * LANES)
                edges[0, angle, part, :, where] = held[angle, part, block, :1]
                edges[1, angle, part, :, where] = held[angle, part, block, strip - 1 :]
    start(borders)
    add(late, [slice(GROUP, strip - GROUP)])

    groups = strip // GROUP
    lane = lax.broadcasted_iota(jnp.int32, (GROUP, LANES), 1)
    segment = lax.broadcasted_iota(jnp.int32, (GROUP, LANES), 0)
    drops[:GROUP] = jnp.zeros((GROUP, LANES), f32)
    for angle in range(angles):

        def rows_of(group):
            return slice(group * GROUP, (group + 1) * GROUP)

        def prepare(block, slot):
            for group in range(groups):
                pair = [held[angle, part, block, rows_of(group)] for part in range(2)]
                power[slot, rows_of(group)] = power_of(*pair)
                for part, value in enumerate(pair):
                    shifts[slot, part, group] = pltpu.roll(value, 1, 1)

        def combine(block, slot):
            for group in range(groups):
                here = [held[angle, part, block, rows_of(group)] for part in range(2)]
                here.append(power[slot, rows_of(group)])
                if group == groups - 1:
                    below = [
                        jnp.where(segment == GROUP - 1, 0.0, pltpu.roll(value, GROUP - 1, 0))
                        for value in here[:2]
                    ]
                    below.append(power_of(*below))
                else:
                    lower = slice(group * GROUP + 1, (group + 1) * GROUP + 1)
                    below = [held[angle, part, block, lower] for part in range(2)]
                    below.append(power[slot, lower])
                down = half_bond(here, below)
                first = (group + 1) * GROUP
                drops[first : first + GROUP] = down
                up = drops[first - 1 : first - 1 + GROUP]
                left = [
                    jnp.where(lane == 0, shifts[1 - slot, part, group], shifts[slot, part, group])
                    for part in range(2)
                ]
                bond = half_bond(left + [power_of(*left)], here)
                bonds[slot, group] = bond
                partial[slot, group] = up - down + bond

        def finish(block, slot):
            behind = pl.ds(pl.multiple_of(jnp.maximum(block - 1, 0) * LANES, LANES), LANES)
            for group in range(groups):
                after = pltpu.roll(bonds[slot, group], LANES - 1, 1)
                first = angle * strip + group * GROUP
                source[first : first + GROUP, behind] = partial[1 - slot, group] - jnp.where(
                    lane == LANES - 1, after, afters[group]
                )
                afters[group] = after

        def step(pair, _):
            block = 2 * pair
            finish(block - 1, 1)
            combine(block, 0)
            prepare(block + 1, 1)
            finish(block, 0)
            combine(block + 1, 1)
            prepare(jnp.minimum(block + 2, blocks - 1), 0)
            return 0

        for group in range(groups):
            for part in range(2):
                shifts[1, part, group] = jnp.zeros((GROUP, LANES), f32)
        prepare(0, 0)
        lax.fori_loop(0, blocks // 2, step, 0)
        finish(blocks - 1, 1)
        for group in range(groups):
            first = angle * strip + group * GROUP
            source[first : first + GROUP, width - LANES :] = partial[1, group] - jnp.where(
                lane == LANES - 1, 0.0, afters[group]
            )

    arrive(borders)

    def line(values):
        return values + [power_of(*values)]

    for angle in range(angles):
        for border, row in ((0, 0), (1, strip - 1)):
            inner = line(
                [
                    jnp.concatenate(
                        [held[angle, part, block, row : row + 1] for block in range(blocks)], 1
                    )
                    for part in range(2)
                ]
            )
            outer = line([halo[border, angle, part] for part in range(2)])
            place = slice(angle * strip + row, angle * strip + row + 1)
            source[place] = source[place] + half_bond(outer, inner)
    for copy, sends in started:
        pl.when(sends)(copy.wait_send)


def mirror(value):
    side = value.shape[1]
    rows = lax.broadcasted_iota(jnp.int32, (side, side), 0)
    columns = lax.broadcasted_iota(jnp.int32, (side, side), 1)
    swap = jnp.where(rows + columns == side - 1, 1.0, 0.0).astype(bf16)
    high = value.astype(bf16)
    low = (value - high.astype(f32)).astype(bf16)
    return jnp.dot(high, swap, preferred_element_type=f32) + jnp.dot(
        low, swap, preferred_element_type=f32
    )


def split_store(value, high, low, columns):
    rounded = value.astype(bf16)
    high[:, columns] = rounded
    low[:, columns] = (value - rounded.astype(f32)).astype(bf16)


def forward_kernel(
    source, even_hi, even_lo, odd_hi, odd_lo, decays, joins,
    solved, carried, incoming, evens,
    xeh, xel, xoh, xol, coefs,
    out, carries, ends, heard, sums, totals, told,
    up_sems, in_sems, over_sems, across_sems, down_sems, back_sems,
):
    angles, width = ends.shape[3] // 2, source.shape[1]
    strip, blocks = source.shape[0] // angles, width // LANES
    groups = strip // GROUP
    plane, share = ends.shape[1], ends.shape[2]
    planes = totals.shape[1]
    me = lax.axis_index("tile")
    floor_at, seat = me // plane, lax.rem(me, plane)
    beside = [lax.rem(seat + by, plane) for by in range(1, plane)]
    beyond_planes = [lax.rem(floor_at + by, planes) for by in range(1, planes)]
    barrier = pltpu.get_barrier_semaphore()
    for peer in [floor_at * plane + other for other in beside] + [
        other * plane + seat for other in beyond_planes
    ]:
        pl.semaphore_signal(barrier, inc=1, device_id={"tile": peer}, device_id_type=MESH)

    def hop(source_ref, target_ref, send_sem, recv_sem, peer):
        return pltpu.make_async_remote_copy(
            src_ref=source_ref,
            dst_ref=target_ref,
            send_sem=send_sem,
            recv_sem=recv_sem,
            device_id={"tile": peer},
            device_id_type=MESH,
        )

    def up(part, other, slot):
        return hop(
            ends.at[part, other], heard.at[part, slot], up_sems.at[part, other],
            in_sems.at[part, slot], floor_at * plane + other,
        )

    def over(part, other, slot):
        return hop(
            sums.at[part], totals.at[part, slot], over_sems.at[part, other],
            across_sems.at[part, slot], other * plane + seat,
        )

    def down(part, other, slot):
        return hop(
            told.at[part, other], incoming.at[part, slot], down_sems.at[part, other],
            back_sems.at[part, slot], floor_at * plane + other,
        )

    def gather(part):
        for other in beside:
            up(part, other, seat).start()
        heard[part, seat] = ends[part, seat]

    def spread(part):
        for other in beside:
            up(part, other, other).wait_recv()
        step = joins[part, seat, 0][:, None]
        fall = heard[part, 0, :, :angles]
        rise = heard[part, plane - 1, :, angles:]
        for item in range(1, plane):
            fall = fall * step + heard[part, item, :, :angles]
            rise = rise * step + heard[part, plane - 1 - item, :, angles:]
        sums[part, :, :angles] = fall
        sums[part, :, angles:] = rise
        for other in beyond_planes:
            over(part, other, floor_at).start()
        totals[part, floor_at] = sums[part]

    def answer(part):
        for other in beyond_planes:
            over(part, other, other).wait_recv()
        step, leap, whole, closing, gain = [joins[part, seat, item][:, None] for item in range(5)]
        bottom = totals[part, 0, :, :angles]
        top = totals[part, planes - 1, :, angles:]
        for item in range(1, planes):
            bottom = bottom * leap + totals[part, item, :, :angles]
            top = top * leap + totals[part, planes - 1 - item, :, angles:]
        fall = (top + whole * bottom) * closing
        rise = (bottom + whole * top) * closing
        fall_here, rise_here = fall, rise
        for item in range(planes):
            fall_here = jnp.where(floor_at == item, fall, fall_here)
            fall = fall * leap + totals[part, item, :, :angles]
            back = planes - 1 - item
            rise_here = jnp.where(floor_at == back, rise, rise_here)
            rise = rise * leap + totals[part, back, :, angles:]
        for item in range(plane):
            told[part, item, :, :angles] = fall_here * gain
            fall_here = fall_here * step + heard[part, item, :, :angles]
            back = plane - 1 - item
            told[part, back, :, angles:] = rise_here * gain
            rise_here = rise_here * step + heard[part, back, :, angles:]
        for other in beside:
            down(part, other, seat).start()
        incoming[part, seat] = told[part, seat]

    def learn(part):
        for other in beside:
            down(part, other, other).wait_recv()

    segment = lax.broadcasted_iota(jnp.int32, (GROUP, LANES), 0)
    half = width // 2

    def tile(index):
        return slice(index * TILE, (index + 1) * TILE)

    tiles = half // TILE
    sums_even = []
    for index in range(tiles):
        near = source[:, tile(index)]
        far = mirror(source[:, tile(width // TILE - 1 - index)])
        sums_even.append(near + far)
        split_store(near - far, xoh, xol, tile(index))
    for index in range(tiles // 2):
        near, far = sums_even[index], mirror(sums_even[tiles - 1 - index])
        split_store(near + far, xeh, xel, tile(index))
        split_store(near - far, xeh, xel, tile(index + tiles // 2))

    def transform(part, index):
        high, low, table_hi, table_lo = (
            (xeh, xel, even_hi, even_lo),
            (xoh, xol, odd_hi, odd_lo),
        )[part]
        where = tile(index)
        depth = half if part else half // 2
        start = 0 if part or index < tiles // 2 else depth
        inner, outer = slice(start, start + depth), slice(0, depth)
        value = (
            jnp.dot(high[:, inner], table_hi[outer, where], preferred_element_type=f32)
            + jnp.dot(low[:, inner], table_hi[outer, where], preferred_element_type=f32)
            + jnp.dot(high[:, inner], table_lo[outer, where], preferred_element_type=f32)
        )
        for column in range(TILE // LANES):
            block = index * TILE // LANES + column
            coefs[part, block] = value[:, column * LANES : (column + 1) * LANES]

    def scan(part):
        result, carry_ref = ((out, carries), (solved, carried))[part]

        def run(chunk, _):
            table = pl.ds(pl.multiple_of(part * half + chunk * LANES, LANES), LANES)
            owner, place = chunk // share, lax.rem(chunk, share)
            gain = decays[2 * GROUP : 2 * GROUP + 1, table]
            step = decays[3 * GROUP : 3 * GROUP + 1, table]
            for angle in range(angles):
                values = [
                    coefs[part, chunk, pl.ds(angle * strip + group, GROUP, stride=groups)]
                    for group in range(groups)
                ]
                fall, falls = values[0], [values[0]]
                for group in range(1, groups):
                    fall = values[group] + step * fall
                    falls.append(fall)
                rise = values[-1]
                for group in reversed(range(groups)):
                    total = falls[group]
                    if group < groups - 1:
                        later = step * rise
                        total = total + later
                        rise = values[group] + later
                    first = angle * strip + group * GROUP
                    result[chunk, first : first + GROUP] = gain * total
                for index, by in enumerate((1, 2, 4)):
                    jump = decays[2 * GROUP + 1 + index : 2 * GROUP + 2 + index, table]
                    fall = fall + jnp.where(segment >= by, pltpu.roll(fall, by, 0), 0.0) * jump
                    rise = (
                        rise
                        + jnp.where(segment < GROUP - by, pltpu.roll(rise, GROUP - by, 0), 0.0)
                        * jump
                    )
                ends[part, owner, place, angle : angle + 1] = fall[GROUP - 1 :]
                ends[part, owner, place, angles + angle : angles + angle + 1] = rise[:1]
                carry_ref[chunk, angle] = gain * jnp.where(
                    segment >= 1, pltpu.roll(fall, 1, 0), 0.0
                )
                carry_ref[chunk, angles + angle] = gain * jnp.where(
                    segment < GROUP - 1, pltpu.roll(rise, GROUP - 1, 0), 0.0
                )
            return 0

        lax.fori_loop(0, blocks // 2, run, 0, unroll=2)

    for index in range(tiles):
        transform(0, index)
    scan(0)
    pl.semaphore_wait(barrier, plane + planes - 2)
    gather(0)
    for index in range(tiles):
        transform(1, index)
    spread(0)
    scan(1)
    gather(1)
    spread(1)
    answer(0)
    learn(0)
    enter(0, out, carries, incoming, decays, xeh, xel)
    for index in range(tiles // 2):
        where = tile(index)
        whole, crossed = [
            restored(xeh, xel, even_hi, even_lo, where, slice(first, first + half // 2))
            for first in (0, half // 2)
        ]
        if index == 0:
            answer(1)
        evens[:, where] = whole + crossed
        evens[:, tile(tiles - 1 - index)] = mirror(whole - crossed)
    learn(1)
    for part in range(2):
        for other in beside:
            up(part, other, seat).wait_send()
            down(part, other, seat).wait_send()
        for other in beyond_planes:
            over(part, other, floor_at).wait_send()


def enter(part, value, carries, incoming, decays, high, low):
    angles = incoming.shape[3] // 2
    strip = value.shape[1] // angles
    half = value.shape[0] * LANES
    groups = strip // GROUP
    length = min(groups, GROUP)
    share = incoming.shape[2]

    def run(chunk, _):
        where = pl.ds(pl.multiple_of(chunk * LANES, LANES), LANES)
        table = pl.ds(pl.multiple_of(part * half + chunk * LANES, LANES), LANES)
        owner, place = chunk // share, lax.rem(chunk, share)
        for angle in range(angles):
            fall = (
                carries[chunk, angle]
                + decays[:GROUP, table] * incoming[part, owner, place, angle : angle + 1]
            )
            rise = (
                carries[chunk, angles + angle]
                + decays[GROUP : 2 * GROUP, table]
                * incoming[part, owner, place, angles + angle : angles + angle + 1]
            )
            for pair in range(0, strip, 2 * GROUP):
                rows = []
                for row in range(pair, pair + 2 * GROUP, length):
                    owner_row, group = row // groups, row % groups
                    ahead = 3 * GROUP + group
                    behind = ahead + groups
                    rows.append(
                        value[
                            chunk,
                            pl.ds(angle * strip + group * GROUP + owner_row, length, stride=GROUP),
                        ]
                        + decays[ahead : ahead + length, table] * fall[owner_row : owner_row + 1]
                        + decays[behind : behind + length, table] * rise[owner_row : owner_row + 1]
                    )
                item = jnp.concatenate(rows, 0)
                rounded = item.astype(bf16)
                start = angle * strip + pair
                high[start : start + 2 * GROUP, where] = rounded
                low[start : start + 2 * GROUP, where] = (item - rounded.astype(f32)).astype(bf16)
        return 0

    lax.fori_loop(0, half // LANES, run, 0)


def restored(high, low, table_hi, table_lo, where, depth=slice(None)):
    last = (((1,), (1,)), ((), ()))
    return (
        lax.dot_general(high[:, depth], table_hi[where, depth], last, preferred_element_type=f32)
        + lax.dot_general(low[:, depth], table_hi[where, depth], last, preferred_element_type=f32)
        + lax.dot_general(high[:, depth], table_lo[where, depth], last, preferred_element_type=f32)
    )


def inverse_kernel(
    field, value, carries, incoming, evens, odd_hi, odd_lo, decays,
    updated, out, xh, xl, parted, sems, field_sems,
):
    angles, strip, width = out.shape
    half = width // 2
    blocks = width // LANES
    copies = []
    for block in range(blocks):
        copy = pltpu.make_async_copy(
            field.at[:, :, block],
            updated.at[:, :, :, block * LANES : (block + 1) * LANES],
            field_sems.at[block],
        )
        copy.start()
        copies.append(copy)
    enter(1, value, carries, incoming, decays, xh, xl)
    tiles = [slice(first, first + TILE) for first in range(0, half, TILE)]
    later = restored(xh, xl, odd_hi, odd_lo, tiles[0])
    for index, where in enumerate(tiles):
        first, odd, even = where.start, later, evens[:, where]
        if index + 1 < len(tiles):
            later = restored(xh, xl, odd_hi, odd_lo, tiles[index + 1])
        near = even + odd
        far = mirror(even - odd)
        for item, start in ((near, first), (far, width - first - TILE)):
            where = slice(start, start + TILE)
            for angle in range(angles):
                parted[angle, :, where] = item[angle * strip : (angle + 1) * strip]
            copy = pltpu.make_async_copy(
                parted.at[:, :, where], out.at[:, :, where], sems.at[start // TILE]
            )
            copy.start()
            copies.append(copy)
    for copy in copies:
        copy.wait()


def body(object_field, probe, measured, frame_table, frame_count):
    angles, _, strip, width = object_field.shape
    side = probe.shape[1]
    cap = measured.shape[0]
    half = width // 2
    reach = side // strip
    rows = angles * strip
    strips = lax.axis_size("tile")
    blocks = width // LANES
    shape = jax.ShapeDtypeStruct

    pieces = (reach + 1) * cap
    plane = 2 ** (int(math.log2(strips)) // 2)
    share = blocks // (2 * plane)
    decays, joins = decay_tables(width, strip, plane)
    joins = jnp.asarray(joins.reshape(-1, 2, plane, share, LANES).transpose(1, 2, 0, 3, 4))

    factors = cosine_factors(width)
    table = (reach + 1, cap, 2, strip, side)
    held, source, *half_tables = pl.pallas_call(
        update_kernel,
        out_shape=[
            shape((angles, 2, blocks, strip, LANES), f32),
            shape((rows, width), f32),
        ]
        + [shape((half, half), bf16)] * 4,
        in_specs=[smem] + [hbm] * 7,
        out_specs=[vmem] * 6,
        scratch_shapes=[
            pltpu.VMEM((2, angles, 2, 1, width), f32),
            pltpu.VMEM((2, strip, LANES), f32),
            pltpu.VMEM((strip + GROUP, LANES), f32),
            pltpu.VMEM((2, 2, strip // GROUP, GROUP, LANES), f32),
            pltpu.VMEM((2, strip // GROUP, GROUP, LANES), f32),
            pltpu.VMEM((2, strip // GROUP, GROUP, LANES), f32),
            pltpu.VMEM((strip // GROUP, GROUP, LANES), f32),
            pltpu.SMEM((reach + 1, cap, 3), jnp.int32),
            pltpu.SMEM((1,), jnp.int32),
            pltpu.VMEM(probe.shape, f32),
            pltpu.VMEM((side, side), bf16),
            pltpu.VMEM((side, side), bf16),
            pltpu.VMEM(factors.shape, f32),
            pltpu.VMEM(measured.shape, bf16),
            pltpu.VMEM(table, bf16),
            pltpu.VMEM(table, bf16),
            pltpu.VMEM(table, bf16),
            pltpu.VMEM(table, bf16),
            pltpu.VMEM((cap, 2, strip, side), f32),
            pltpu.VMEM((reach + 1, cap, 2, side // LANES + 2, strip, LANES), f32),
            pltpu.VMEM(((reach + 1) * strip, side), f32),
            pltpu.VMEM((2, angles, 2, 1, width), f32),
            pltpu.SemaphoreType.DMA((5 + blocks,)),
            pltpu.SemaphoreType.DMA((2, reach + 1)),
            pltpu.SemaphoreType.DMA((2, 1)),
            pltpu.SemaphoreType.DMA((2, cap)),
            pltpu.SemaphoreType.DMA((2, pieces)),
            pltpu.SemaphoreType.DMA((2, pieces)),
            pltpu.SemaphoreType.DMA((2, 2)),
        ],
        compiler_params=params(collective_id=0, has_side_effects=True),
        cost_estimate=cost(20),
        name="update",
    )(
        frame_count,
        *[
            pltpu.with_memory_space_constraint(item, pltpu.HBM)
            for item in (
                frame_table,
                object_field,
                probe,
                measured,
                *fourier_tables(side),
                factors,
            )
        ],
    )

    planes = strips // plane
    lines = (share, 2 * angles, LANES)
    solved, carried, incoming, evens = pl.pallas_call(
        forward_kernel,
        out_shape=[
            shape((blocks // 2, rows, LANES), f32),
            shape((blocks // 2, 2 * angles, GROUP, LANES), f32),
            shape((2, plane) + lines, f32),
            shape((rows, half), f32),
        ],
        in_specs=[vmem] * 7,
        out_specs=[vmem] * 4,
        scratch_shapes=[pltpu.VMEM((rows, half), bf16)] * 4
        + [
            pltpu.VMEM((2, blocks // 2, rows, LANES), f32),
            pltpu.VMEM((blocks // 2, rows, LANES), f32),
            pltpu.VMEM((blocks // 2, 2 * angles, GROUP, LANES), f32),
            pltpu.VMEM((2, plane) + lines, f32),
            pltpu.VMEM((2, plane) + lines, f32),
            pltpu.VMEM((2,) + lines, f32),
            pltpu.VMEM((2, planes) + lines, f32),
            pltpu.VMEM((2, plane) + lines, f32),
            pltpu.SemaphoreType.DMA((2, plane)),
            pltpu.SemaphoreType.DMA((2, plane)),
            pltpu.SemaphoreType.DMA((2, planes)),
            pltpu.SemaphoreType.DMA((2, planes)),
            pltpu.SemaphoreType.DMA((2, plane)),
            pltpu.SemaphoreType.DMA((2, plane)),
        ],
        compiler_params=params(collective_id=1, has_side_effects=True),
        cost_estimate=cost(15),
        name="forward",
    )(source, *half_tables, decays, joins)
    updated, phase_map = pl.pallas_call(
        inverse_kernel,
        out_shape=[shape(object_field.shape, f32), shape((angles, strip, width), f32)],
        in_specs=[vmem] * 8,
        out_specs=[hbm, hbm],
        scratch_shapes=[
            pltpu.VMEM((rows, half), bf16),
            pltpu.VMEM((rows, half), bf16),
            pltpu.VMEM((angles, strip, width), f32),
            pltpu.SemaphoreType.DMA((width // TILE,)),
            pltpu.SemaphoreType.DMA((blocks,)),
        ],
        compiler_params=params(),
        cost_estimate=cost(6),
        name="inverse",
    )(held, solved, carried, incoming, evens, *half_tables[2:], decays)
    return (updated, phase_map)


def solution(mesh):
    return jax.shard_map(
        body,
        mesh=mesh,
        in_specs=(
            P("group", None, "tile", None),
            P(),
            P(("group", "tile"), None, None),
            P(("group", "tile"), None),
            P(("group", "tile")),
        ),
        out_specs=(P("group", None, "tile", None), P("group", "tile", None)),
        check_vma=False,
    )
```

```python
import functools
import math

import numpy as np
import jax
import jax.numpy as jnp
from jax import lax
from jax.experimental import pallas as pl
from jax.experimental.pallas import tpu as pltpu
from jax.sharding import PartitionSpec as P

magnitude_floor = 0.5
soften_term = 0.5
screen_term = 0.0001
epsilon_term = 1e-06
f32 = jnp.float32
bf16 = jnp.bfloat16
LANES = 128
GROUP = 8
TILE = 256
VMEM_BYTES = 30 * 1024 * 1024
MESH = pl.DeviceIdType.MESH
vmem = pl.BlockSpec(memory_space=pltpu.VMEM)
smem = pl.BlockSpec(memory_space=pltpu.SMEM)
hbm = pl.BlockSpec(memory_space=pltpu.HBM)


def cost(micros):
    return pl.CostEstimate(
        flops=0, bytes_accessed=int(micros * 3_000_000), transcendentals=0
    )


def params(**more):
    return pltpu.CompilerParams(vmem_limit_bytes=VMEM_BYTES, **more)


def fourier_tables(side):
    indices = np.arange(side)
    products = indices[:, None] * indices[None, :] % side
    phases = products.astype(np.float64) * (-2.0 * math.pi / side)
    scale = 1.0 / math.sqrt(side)
    return (
        jnp.asarray(np.cos(phases) * scale, f32).astype(bf16),
        jnp.asarray(np.sin(phases) * scale, f32).astype(bf16),
    )


def frequencies(grid_side):
    quarter = np.arange(grid_side // 4)
    even = np.concatenate([4 * quarter, 4 * quarter + 2])
    return even, 2 * np.arange(grid_side // 2) + 1


def cosine_factors(grid_side):
    half = grid_side // 2
    step = 32
    out = []
    for freqs in frequencies(grid_side):
        scale = np.where(freqs == 0, math.sqrt(1.0 / grid_side), math.sqrt(2.0 / grid_side))
        coarse = (2 * step * np.arange(half // step)[:, None] * freqs[None, :]) % (4 * grid_side)
        fine = ((2 * np.arange(step)[:, None] + 1) * freqs[None, :]) % (4 * grid_side)
        unit = math.pi / (2 * grid_side)
        out.append(
            np.stack(
                [
                    np.cos(coarse * unit) * scale,
                    np.sin(coarse * unit) * scale,
                    np.cos(fine * unit),
                    np.sin(fine * unit),
                ]
            )
        )
    return jnp.asarray(np.stack(out), f32)


def decay_tables(grid_side, strip_rows, plane):
    half = grid_side // 2
    freqs = np.concatenate(frequencies(grid_side)).astype(np.float64)
    shift = screen_term + 2.0 - 2.0 * np.cos(freqs * math.pi / grid_side)
    rate = 2.0 * np.arcsinh(np.sqrt(shift) / 2.0)
    gain = 2.0 / (2.0 * np.sinh(rate))
    groups = strip_rows // GROUP
    segments = np.exp(-groups * np.arange(GROUP)[:, None] * rate)
    steps = np.exp(-(np.arange(groups)[:, None] + 1) * rate)
    jumps = np.exp(-groups * np.array([[1], [2], [4]]) * rate)
    spare = np.zeros((GROUP - 4,) + gain.shape)
    decays = np.concatenate(
        [segments, segments[::-1], gain[None], jumps, spare, steps, steps[::-1]]
    )
    spans = strip_rows * np.array([[1], [plane], [grid_side // strip_rows]])
    closing = 1.0 / (1.0 - np.exp(-2.0 * grid_side * rate))
    joins = np.concatenate([np.exp(-spans * rate), closing[None], gain[None]])
    return decays.astype(np.float32), joins.astype(np.float32)


def table_rows(factors, part, high, low):
    step = factors.shape[2]

    def run(block, _):
        rows = pl.ds(pl.multiple_of(block * step, step), step)
        value = (
            factors[part, 0, pl.ds(block, 1)] * factors[part, 2]
            - factors[part, 1, pl.ds(block, 1)] * factors[part, 3]
        )
        rounded = value.astype(bf16)
        high[rows] = rounded
        low[rows] = (value - rounded.astype(f32)).astype(bf16)
        return 0

    lax.fori_loop(0, high.shape[0] // step, run, 0)


def window_start(column, width, span):
    return jnp.minimum(column // LANES, (width - span) // LANES) * LANES


def power_of(re, im):
    return re * re + im * im + 0.5 * soften_term


def half_bond(first, second):
    cross = first[0] * second[1] - first[1] * second[0]
    return cross / (first[2] + second[2])


def update_kernel(
    frame_count, frame_table, field, probe_in, measured, cos_in, sin_in, factors_in,
    held, source, even_hi, even_lo, odd_hi, odd_lo,
    staged, halo, power, drops, shifts, bonds, partial, afters, tables, counts, probe, cos_ref, sin_ref, factors, moved, cuts, arrived, away, landed,
    own, placed, window, edges,
    load_sems, tell_sems, count_sems, moved_sems, fetch_sems, give_sems, edge_sems,
):
    count = lax.axis_size("tile")
    me = lax.axis_index("tile")
    angles, _, strip, width = field.shape
    cap, side = measured.shape[0], measured.shape[1]
    span = side + LANES
    lanes = span // LANES
    blocks = width // LANES
    reach = tables.shape[0] - 1
    middle = reach // 2
    total = (reach + 1) * strip
    others = [j for j in range(reach + 1) if j != middle]

    def inside(place):
        return (place >= 0) & (place < count)

    def load(index, source, target):
        return pltpu.make_async_copy(source, target, load_sems.at[index])

    loads = [
        load(0, frame_table, tables.at[0]),
        load(1, factors_in, factors),
        load(2, probe_in, probe),
        load(3, cos_in, cos_ref),
        load(4, sin_in, sin_ref),
        load(5, measured, staged),
    ]
    strips = [
        load(6 + block, field.at[:, :, :, block * LANES : (block + 1) * LANES], held.at[:, :, block])
        for block in range(blocks)
    ]
    for item in [loads[0], loads[5]] + strips + loads[1:5]:
        item.start()

    def send(source, target, sems, index, by):
        copy = pltpu.make_async_remote_copy(
            src_ref=source,
            dst_ref=target,
            send_sem=sems.at[0, index],
            recv_sem=sems.at[1, index],
            device_id={"tile": me + by},
            device_id_type=MESH,
        )
        return copy, inside(me + by), inside(me - by)

    barrier = pltpu.get_barrier_semaphore()
    met = jnp.zeros((), jnp.int32)
    for by in [sign * by for by in range(1, reach + 1) for sign in (1, -1)]:

        @pl.when(inside(me + by))
        def _():
            pl.semaphore_signal(
                barrier, inc=1, device_id={"tile": me + by}, device_id_type=MESH
            )

        met = met + jnp.where(inside(me + by), 1, 0)
    pl.semaphore_wait(barrier, met)

    tells = [
        send(tables.at[0], tables.at[j], tell_sems, j, j) for j in range(1, reach + 1)
    ]
    tells.append(send(frame_count, counts, count_sems, 0, middle))
    moves = [
        send(staged.at[s], moved.at[s], moved_sems, s, middle) for s in range(cap)
    ]
    fetches = [
        [send(cuts.at[j, s], arrived.at[j, s], fetch_sems, s * (reach + 1) + j, middle - j) for j in others]
        for s in range(cap)
    ]
    gives = [
        [send(away.at[j, s], landed.at[j, s], give_sems, s * (reach + 1) + j, j - middle) for j in others]
        for s in range(cap)
    ]
    borders = [
        send(edges.at[1], halo.at[0], edge_sems, 0, 1),
        send(edges.at[0], halo.at[1], edge_sems, 1, -1),
    ]
    started = []

    def start(items):
        for copy, sends, takes in items:
            pl.when(sends)(copy.start)
            started.append((copy, sends))

    def arrive(items):
        for copy, sends, takes in items:
            pl.when(takes)(copy.wait_recv)

    def blank(items, wipe):
        for index, (copy, sends, takes) in enumerate(items):

            @pl.when(jnp.logical_not(takes))
            def _():
                wipe(index)

    def wipe_table(index):
        if index == reach:
            counts[0] = 0
        else:
            for s in range(cap):
                for item in range(3):
                    tables[index + 1, s, item] = 0

    def wipe(ref, *first):
        ref[first] = jnp.zeros(ref.shape[len(first):], ref.dtype)

    loads[0].wait()
    start(tells)
    loads[5].wait()
    start(moves)
    blank(tells, wipe_table)
    blank(moves, lambda s: wipe(moved, s))
    for s in range(cap):
        blank(fetches[s], lambda index: wipe(arrived, others[index], s))
        blank(gives[s], lambda index: wipe(landed, others[index], s))
    blank(borders, lambda index: wipe(halo, index))
    for j in range(reach + 1):
        for s in range(cap):
            for part in range(2):
                placed[j, s, part, 0] = jnp.zeros((strip, LANES), f32)
    loads[1].wait()
    table_rows(factors, 0, even_hi, even_lo)
    for item in strips:
        item.wait()
    arrive(tells)

    def first_block(j, s):
        return jnp.minimum(tables[j, s, 1] // LANES, blocks - lanes)

    for s in range(cap):
        for j in others + [middle]:
            block = first_block(j, s)
            shift = tables[j, s, 1] - block * LANES
            angle = tables[j, s, 2]
            for part in range(2):
                piece = jnp.concatenate(
                    [held[angle, part, block + lane] for lane in range(lanes)], 1
                )
                turned = pltpu.roll(piece, lax.rem(span - shift, span), 1)
                target = arrived if j == middle else cuts
                target[j, s, part] = turned[:, :side].astype(bf16)
        start(fetches[s])

    table_rows(factors, 1, odd_hi, odd_lo)
    for item in loads[2:5]:
        item.wait()
    cos_part, sin_part = cos_ref[...], sin_ref[...]
    stacked = jnp.concatenate([cos_part, sin_part], 0)
    joined = jnp.concatenate([cos_part, sin_part], 1)
    probe_re, probe_im = probe[0], probe[1]
    peak = jnp.max(probe_re * probe_re + probe_im * probe_im) + epsilon_term

    def left(re, im, sign):
        products = jnp.dot(
            stacked, jnp.concatenate([re, im], 1), preferred_element_type=f32
        )
        cc, ci = products[:side, :side], products[:side, side:]
        sc, si = products[side:, :side], products[side:, side:]
        return (cc - si, ci + sc) if sign > 0 else (cc + si, ci - sc)

    def right(re, im, sign):
        products = jnp.dot(
            jnp.concatenate([re, im], 0), joined, preferred_element_type=f32
        )
        rc, rs = products[:side, :side], products[:side, side:]
        ic, js = products[side:, :side], products[side:, side:]
        return (rc - js, rs + ic) if sign > 0 else (rc + js, ic - rs)

    for s in range(cap):
        arrive(fetches[s])
        offset = tables[middle, s, 0]
        patch = []
        for part in range(2):
            for j in range(reach + 1):
                window[j * strip : (j + 1) * strip] = arrived[j, s, part].astype(f32)
            turned = pltpu.roll(window[...], lax.rem(total - offset, total), 0)
            patch.append(turned[:side])
        wave_re = (probe_re * patch[0] - probe_im * patch[1]).astype(bf16)
        wave_im = (probe_re * patch[1] + probe_im * patch[0]).astype(bf16)
        half_re, half_im = left(wave_re, wave_im, 1)
        spec_re, spec_im = right(half_re.astype(bf16), half_im.astype(bf16), 1)
        amplitude = jnp.sqrt(spec_re * spec_re + spec_im * spec_im)
        arrive(moves[s : s + 1])
        factor = moved[s].astype(f32) / jnp.maximum(amplitude, magnitude_floor) - 1.0
        back_re, back_im = left(
            (spec_re * factor).astype(bf16), (spec_im * factor).astype(bf16), -1
        )
        corr_re, corr_im = right(back_re.astype(bf16), back_im.astype(bf16), -1)
        live = s < counts[0]
        updates = (
            (probe_re * corr_re + probe_im * corr_im) / peak,
            (probe_re * corr_im - probe_im * corr_re) / peak,
        )
        for part in range(2):
            window[:side] = jnp.where(live, updates[part], 0.0)
            window[side:] = jnp.zeros((total - side, side), f32)
            turned = pltpu.roll(window[...], offset, 0)
            for j in range(reach + 1):
                piece = turned[j * strip : (j + 1) * strip]
                if j == middle:
                    own[s, part] = piece
                else:
                    away[j, s, part] = piece.astype(bf16)
        start(gives[s])

    pad = jnp.zeros((strip, LANES), f32)

    def shifted(source, j, s):
        shift = tables[j, s, 1] - first_block(j, s) * LANES
        for part in range(2):
            value = jnp.concatenate([source[part].astype(f32), pad], 1)
            turned = pltpu.roll(value, shift, 1)
            for lane in range(lanes):
                placed[j, s, part, lane + 1] = turned[:, lane * LANES : (lane + 1) * LANES]

    def add(items, rows):
        def chunk(block, _):
            for angle in range(angles):
                found = []
                for j, s in items:
                    near = block - first_block(j, s)
                    hit = (tables[j, s, 2] == angle) & (near >= 0) & (near < lanes)
                    found.append(jnp.where(hit, near + 1, 0))
                for part in range(2):
                    for row in rows:
                        value = held[angle, part, block, row]
                        for (j, s), index in zip(items, found):
                            value = value + placed[j, s, part, index, row]
                        held[angle, part, block, row] = value
            return 0

        lax.fori_loop(0, blocks, chunk, 0)

    for s in range(cap):
        shifted(own.at[s], middle, s)
    early = [(middle, s) for s in range(cap)]
    for s in range(cap - 1):
        arrive(gives[s])
        for j in others:
            shifted(landed.at[j, s], j, s)
        early += [(j, s) for j in others]
    add(early, [slice(0, strip)])
    arrive(gives[cap - 1])
    for j in others:
        shifted(landed.at[j, cap - 1], j, cap - 1)
    late = [(j, cap - 1) for j in others]
    add(late, [slice(0, GROUP), slice(strip - GROUP, strip)])
    for angle in range(angles):
        for part in range(2):
            for block in range(blocks):
                where = slice(block * LANES, (block + 1) * LANES)
                edges[0, angle, part, :, where] = held[angle, part, block, :1]
                edges[1, angle, part, :, where] = held[angle, part, block, strip - 1 :]
    start(borders)
    add(late, [slice(GROUP, strip - GROUP)])

    groups = strip // GROUP
    lane = lax.broadcasted_iota(jnp.int32, (GROUP, LANES), 1)
    segment = lax.broadcasted_iota(jnp.int32, (GROUP, LANES), 0)
    drops[:GROUP] = jnp.zeros((GROUP, LANES), f32)
    for angle in range(angles):

        def rows_of(group):
            return slice(group * GROUP, (group + 1) * GROUP)

        def prepare(block, slot):
            for group in range(groups):
                pair = [held[angle, part, block, rows_of(group)] for part in range(2)]
                power[slot, rows_of(group)] = power_of(*pair)
                for part, value in enumerate(pair):
                    shifts[slot, part, group] = pltpu.roll(value, 1, 1)

        def combine(block, slot):
            for group in range(groups):
                here = [held[angle, part, block, rows_of(group)] for part in range(2)]
                here.append(power[slot, rows_of(group)])
                if group == groups - 1:
                    below = [
                        jnp.where(segment == GROUP - 1, 0.0, pltpu.roll(value, GROUP - 1, 0))
                        for value in here[:2]
                    ]
                    below.append(power_of(*below))
                else:
                    lower = slice(group * GROUP + 1, (group + 1) * GROUP + 1)
                    below = [held[angle, part, block, lower] for part in range(2)]
                    below.append(power[slot, lower])
                down = half_bond(here, below)
                first = (group + 1) * GROUP
                drops[first : first + GROUP] = down
                up = drops[first - 1 : first - 1 + GROUP]
                left = [
                    jnp.where(lane == 0, shifts[1 - slot, part, group], shifts[slot, part, group])
                    for part in range(2)
                ]
                bond = half_bond(left + [power_of(*left)], here)
                bonds[slot, group] = bond
                partial[slot, group] = up - down + bond

        def finish(block, slot):
            behind = pl.ds(pl.multiple_of(jnp.maximum(block - 1, 0) * LANES, LANES), LANES)
            for group in range(groups):
                after = pltpu.roll(bonds[slot, group], LANES - 1, 1)
                first = angle * strip + group * GROUP
                source[first : first + GROUP, behind] = partial[1 - slot, group] - jnp.where(
                    lane == LANES - 1, after, afters[group]
                )
                afters[group] = after

        def step(pair, _):
            block = 2 * pair
            finish(block - 1, 1)
            combine(block, 0)
            prepare(block + 1, 1)
            finish(block, 0)
            combine(block + 1, 1)
            prepare(jnp.minimum(block + 2, blocks - 1), 0)
            return 0

        for group in range(groups):
            for part in range(2):
                shifts[1, part, group] = jnp.zeros((GROUP, LANES), f32)
        prepare(0, 0)
        lax.fori_loop(0, blocks // 2, step, 0)
        finish(blocks - 1, 1)
        for group in range(groups):
            first = angle * strip + group * GROUP
            source[first : first + GROUP, width - LANES :] = partial[1, group] - jnp.where(
                lane == LANES - 1, 0.0, afters[group]
            )

    arrive(borders)

    def line(values):
        return values + [power_of(*values)]

    for angle in range(angles):
        for border, row in ((0, 0), (1, strip - 1)):
            inner = line(
                [
                    jnp.concatenate(
                        [held[angle, part, block, row : row + 1] for block in range(blocks)], 1
                    )
                    for part in range(2)
                ]
            )
            outer = line([halo[border, angle, part] for part in range(2)])
            place = slice(angle * strip + row, angle * strip + row + 1)
            source[place] = source[place] + half_bond(outer, inner)
    for copy, sends in started:
        pl.when(sends)(copy.wait_send)


def mirror(value):
    side = value.shape[1]
    rows = lax.broadcasted_iota(jnp.int32, (side, side), 0)
    columns = lax.broadcasted_iota(jnp.int32, (side, side), 1)
    swap = jnp.where(rows + columns == side - 1, 1.0, 0.0).astype(bf16)
    high = value.astype(bf16)
    low = (value - high.astype(f32)).astype(bf16)
    return jnp.dot(high, swap, preferred_element_type=f32) + jnp.dot(
        low, swap, preferred_element_type=f32
    )


def split_store(value, high, low, columns):
    rounded = value.astype(bf16)
    high[:, columns] = rounded
    low[:, columns] = (value - rounded.astype(f32)).astype(bf16)


def forward_kernel(
    source, even_hi, even_lo, odd_hi, odd_lo, decays, joins,
    solved, carried, incoming, evens,
    xeh, xel, xoh, xol, coefs,
    out, carries, ends, heard, sums, totals, told,
    up_sems, in_sems, over_sems, across_sems, down_sems, back_sems,
):
    angles, width = ends.shape[3] // 2, source.shape[1]
    strip, blocks = source.shape[0] // angles, width // LANES
    groups = strip // GROUP
    plane, share = ends.shape[1], ends.shape[2]
    planes = totals.shape[1]
    me = lax.axis_index("tile")
    floor_at, seat = me // plane, lax.rem(me, plane)
    beside = [lax.rem(seat + by, plane) for by in range(1, plane)]
    beyond_planes = [lax.rem(floor_at + by, planes) for by in range(1, planes)]
    barrier = pltpu.get_barrier_semaphore()
    for peer in [floor_at * plane + other for other in beside] + [
        other * plane + seat for other in beyond_planes
    ]:
        pl.semaphore_signal(barrier, inc=1, device_id={"tile": peer}, device_id_type=MESH)

    def hop(source_ref, target_ref, send_sem, recv_sem, peer):
        return pltpu.make_async_remote_copy(
            src_ref=source_ref,
            dst_ref=target_ref,
            send_sem=send_sem,
            recv_sem=recv_sem,
            device_id={"tile": peer},
            device_id_type=MESH,
        )

    def up(part, other, slot):
        return hop(
            ends.at[part, other], heard.at[part, slot], up_sems.at[part, other],
            in_sems.at[part, slot], floor_at * plane + other,
        )

    def over(part, other, slot):
        return hop(
            sums.at[part], totals.at[part, slot], over_sems.at[part, other],
            across_sems.at[part, slot], other * plane + seat,
        )

    def down(part, other, slot):
        return hop(
            told.at[part, other], incoming.at[part, slot], down_sems.at[part, other],
            back_sems.at[part, slot], floor_at * plane + other,
        )

    def gather(part):
        for other in beside:
            up(part, other, seat).start()
        heard[part, seat] = ends[part, seat]

    def spread(part):
        for other in beside:
            up(part, other, other).wait_recv()
        step = joins[part, seat, 0][:, None]
        fall = heard[part, 0, :, :angles]
        rise = heard[part, plane - 1, :, angles:]
        for item in range(1, plane):
            fall = fall * step + heard[part, item, :, :angles]
            rise = rise * step + heard[part, plane - 1 - item, :, angles:]
        sums[part, :, :angles] = fall
        sums[part, :, angles:] = rise
        for other in beyond_planes:
            over(part, other, floor_at).start()
        totals[part, floor_at] = sums[part]

    def answer(part):
        for other in beyond_planes:
            over(part, other, other).wait_recv()
        step, leap, whole, closing, gain = [joins[part, seat, item][:, None] for item in range(5)]
        bottom = totals[part, 0, :, :angles]
        top = totals[part, planes - 1, :, angles:]
        for item in range(1, planes):
            bottom = bottom * leap + totals[part, item, :, :angles]
            top = top * leap + totals[part, planes - 1 - item, :, angles:]
        fall = (top + whole * bottom) * closing
        rise = (bottom + whole * top) * closing
        fall_here, rise_here = fall, rise
        for item in range(planes):
            fall_here = jnp.where(floor_at == item, fall, fall_here)
            fall = fall * leap + totals[part, item, :, :angles]
            back = planes - 1 - item
            rise_here = jnp.where(floor_at == back, rise, rise_here)
            rise = rise * leap + totals[part, back, :, angles:]
        for item in range(plane):
            told[part, item, :, :angles] = fall_here * gain
            fall_here = fall_here * step + heard[part, item, :, :angles]
            back = plane - 1 - item
            told[part, back, :, angles:] = rise_here * gain
            rise_here = rise_here * step + heard[part, back, :, angles:]
        for other in beside:
            down(part, other, seat).start()
        incoming[part, seat] = told[part, seat]

    def learn(part):
        for other in beside:
            down(part, other, other).wait_recv()

    segment = lax.broadcasted_iota(jnp.int32, (GROUP, LANES), 0)
    half = width // 2

    def tile(index):
        return slice(index * TILE, (index + 1) * TILE)

    tiles = half // TILE
    sums_even = []
    for index in range(tiles):
        near = source[:, tile(index)]
        far = mirror(source[:, tile(width // TILE - 1 - index)])
        sums_even.append(near + far)
        split_store(near - far, xoh, xol, tile(index))
    for index in range(tiles // 2):
        near, far = sums_even[index], mirror(sums_even[tiles - 1 - index])
        split_store(near + far, xeh, xel, tile(index))
        split_store(near - far, xeh, xel, tile(index + tiles // 2))

    def transform(part, index):
        high, low, table_hi, table_lo = (
            (xeh, xel, even_hi, even_lo),
            (xoh, xol, odd_hi, odd_lo),
        )[part]
        where = tile(index)
        depth = half if part else half // 2
        start = 0 if part or index < tiles // 2 else depth
        inner, outer = slice(start, start + depth), slice(0, depth)
        value = (
            jnp.dot(high[:, inner], table_hi[outer, where], preferred_element_type=f32)
            + jnp.dot(low[:, inner], table_hi[outer, where], preferred_element_type=f32)
            + jnp.dot(high[:, inner], table_lo[outer, where], preferred_element_type=f32)
        )
        for column in range(TILE // LANES):
            block = index * TILE // LANES + column
            coefs[part, block] = value[:, column * LANES : (column + 1) * LANES]

    def scan(part):
        result, carry_ref = ((out, carries), (solved, carried))[part]

        def run(chunk, _):
            table = pl.ds(pl.multiple_of(part * half + chunk * LANES, LANES), LANES)
            owner, place = chunk // share, lax.rem(chunk, share)
            gain = decays[2 * GROUP : 2 * GROUP + 1, table]
            step = decays[3 * GROUP : 3 * GROUP + 1, table]
            for angle in range(angles):
                values = [
                    coefs[part, chunk, pl.ds(angle * strip + group, GROUP, stride=groups)]
                    for group in range(groups)
                ]
                fall, falls = values[0], [values[0]]
                for group in range(1, groups):
                    fall = values[group] + step * fall
                    falls.append(fall)
                rise = values[-1]
                for group in reversed(range(groups)):
                    total = falls[group]
                    if group < groups - 1:
                        later = step * rise
                        total = total + later
                        rise = values[group] + later
                    first = angle * strip + group * GROUP
                    result[chunk, first : first + GROUP] = gain * total
                for index, by in enumerate((1, 2, 4)):
                    jump = decays[2 * GROUP + 1 + index : 2 * GROUP + 2 + index, table]
                    fall = fall + jnp.where(segment >= by, pltpu.roll(fall, by, 0), 0.0) * jump
                    rise = (
                        rise
                        + jnp.where(segment < GROUP - by, pltpu.roll(rise, GROUP - by, 0), 0.0)
                        * jump
                    )
                ends[part, owner, place, angle : angle + 1] = fall[GROUP - 1 :]
                ends[part, owner, place, angles + angle : angles + angle + 1] = rise[:1]
                carry_ref[chunk, angle] = gain * jnp.where(
                    segment >= 1, pltpu.roll(fall, 1, 0), 0.0
                )
                carry_ref[chunk, angles + angle] = gain * jnp.where(
                    segment < GROUP - 1, pltpu.roll(rise, GROUP - 1, 0), 0.0
                )
            return 0

        lax.fori_loop(0, blocks // 2, run, 0, unroll=2)

    for index in range(tiles):
        transform(0, index)
    scan(0)
    pl.semaphore_wait(barrier, plane + planes - 2)
    gather(0)
    for index in range(tiles):
        transform(1, index)
    spread(0)
    scan(1)
    gather(1)
    spread(1)
    answer(0)
    learn(0)
    answer(1)
    enter(0, out, carries, incoming, decays, xeh, xel)
    for index in range(tiles // 2):
        where = tile(index)
        whole, crossed = [
            restored(xeh, xel, even_hi, even_lo, where, slice(first, first + half // 2))
            for first in (0, half // 2)
        ]
        evens[:, where] = whole + crossed
        evens[:, tile(tiles - 1 - index)] = mirror(whole - crossed)
    learn(1)
    for part in range(2):
        for other in beside:
            up(part, other, seat).wait_send()
            down(part, other, seat).wait_send()
        for other in beyond_planes:
            over(part, other, floor_at).wait_send()


def enter(part, value, carries, incoming, decays, high, low):
    angles = incoming.shape[3] // 2
    strip = value.shape[1] // angles
    half = value.shape[0] * LANES
    groups = strip // GROUP
    length = min(groups, GROUP)
    share = incoming.shape[2]

    def run(chunk, _):
        where = pl.ds(pl.multiple_of(chunk * LANES, LANES), LANES)
        table = pl.ds(pl.multiple_of(part * half + chunk * LANES, LANES), LANES)
        owner, place = chunk // share, lax.rem(chunk, share)
        for angle in range(angles):
            fall = (
                carries[chunk, angle]
                + decays[:GROUP, table] * incoming[part, owner, place, angle : angle + 1]
            )
            rise = (
                carries[chunk, angles + angle]
                + decays[GROUP : 2 * GROUP, table]
                * incoming[part, owner, place, angles + angle : angles + angle + 1]
            )
            for pair in range(0, strip, 2 * GROUP):
                rows = []
                for row in range(pair, pair + 2 * GROUP, length):
                    owner_row, group = row // groups, row % groups
                    ahead = 3 * GROUP + group
                    behind = ahead + groups
                    rows.append(
                        value[
                            chunk,
                            pl.ds(angle * strip + group * GROUP + owner_row, length, stride=GROUP),
                        ]
                        + decays[ahead : ahead + length, table] * fall[owner_row : owner_row + 1]
                        + decays[behind : behind + length, table] * rise[owner_row : owner_row + 1]
                    )
                item = jnp.concatenate(rows, 0)
                rounded = item.astype(bf16)
                start = angle * strip + pair
                high[start : start + 2 * GROUP, where] = rounded
                low[start : start + 2 * GROUP, where] = (item - rounded.astype(f32)).astype(bf16)
        return 0

    lax.fori_loop(0, half // LANES, run, 0)


def restored(high, low, table_hi, table_lo, where, depth=slice(None)):
    last = (((1,), (1,)), ((), ()))
    return (
        lax.dot_general(high[:, depth], table_hi[where, depth], last, preferred_element_type=f32)
        + lax.dot_general(low[:, depth], table_hi[where, depth], last, preferred_element_type=f32)
        + lax.dot_general(high[:, depth], table_lo[where, depth], last, preferred_element_type=f32)
    )


def inverse_kernel(
    field, value, carries, incoming, evens, odd_hi, odd_lo, decays,
    updated, out, xh, xl, parted, sems, field_sems,
):
    angles, strip, width = out.shape
    half = width // 2
    blocks = width // LANES
    copies = []
    for block in range(blocks):
        copy = pltpu.make_async_copy(
            field.at[:, :, block],
            updated.at[:, :, :, block * LANES : (block + 1) * LANES],
            field_sems.at[block],
        )
        copy.start()
        copies.append(copy)
    enter(1, value, carries, incoming, decays, xh, xl)
    tiles = [slice(first, first + TILE) for first in range(0, half, TILE)]
    later = restored(xh, xl, odd_hi, odd_lo, tiles[0])
    for index, where in enumerate(tiles):
        first, odd, even = where.start, later, evens[:, where]
        if index + 1 < len(tiles):
            later = restored(xh, xl, odd_hi, odd_lo, tiles[index + 1])
        near = even + odd
        far = mirror(even - odd)
        for item, start in ((near, first), (far, width - first - TILE)):
            where = slice(start, start + TILE)
            for angle in range(angles):
                parted[angle, :, where] = item[angle * strip : (angle + 1) * strip]
            copy = pltpu.make_async_copy(
                parted.at[:, :, where], out.at[:, :, where], sems.at[start // TILE]
            )
            copy.start()
            copies.append(copy)
    for copy in copies:
        copy.wait()


def body(object_field, probe, measured, frame_table, frame_count):
    angles, _, strip, width = object_field.shape
    side = probe.shape[1]
    cap = measured.shape[0]
    half = width // 2
    reach = side // strip
    rows = angles * strip
    strips = lax.axis_size("tile")
    blocks = width // LANES
    shape = jax.ShapeDtypeStruct

    pieces = (reach + 1) * cap
    plane = 2 ** (int(math.log2(strips)) // 2)
    share = blocks // (2 * plane)
    decays, joins = decay_tables(width, strip, plane)
    joins = jnp.asarray(joins.reshape(-1, 2, plane, share, LANES).transpose(1, 2, 0, 3, 4))

    factors = cosine_factors(width)
    table = (reach + 1, cap, 2, strip, side)
    held, source, *half_tables = pl.pallas_call(
        update_kernel,
        out_shape=[
            shape((angles, 2, blocks, strip, LANES), f32),
            shape((rows, width), f32),
        ]
        + [shape((half, half), bf16)] * 4,
        in_specs=[smem] + [hbm] * 7,
        out_specs=[vmem] * 6,
        scratch_shapes=[
            pltpu.VMEM(measured.shape, bf16),
            pltpu.VMEM((2, angles, 2, 1, width), f32),
            pltpu.VMEM((2, strip, LANES), f32),
            pltpu.VMEM((strip + GROUP, LANES), f32),
            pltpu.VMEM((2, 2, strip // GROUP, GROUP, LANES), f32),
            pltpu.VMEM((2, strip // GROUP, GROUP, LANES), f32),
            pltpu.VMEM((2, strip // GROUP, GROUP, LANES), f32),
            pltpu.VMEM((strip // GROUP, GROUP, LANES), f32),
            pltpu.SMEM((reach + 1, cap, 3), jnp.int32),
            pltpu.SMEM((1,), jnp.int32),
            pltpu.VMEM(probe.shape, f32),
            pltpu.VMEM((side, side), bf16),
            pltpu.VMEM((side, side), bf16),
            pltpu.VMEM(factors.shape, f32),
            pltpu.VMEM(measured.shape, bf16),
            pltpu.VMEM(table, bf16),
            pltpu.VMEM(table, bf16),
            pltpu.VMEM(table, bf16),
            pltpu.VMEM(table, bf16),
            pltpu.VMEM((cap, 2, strip, side), f32),
            pltpu.VMEM((reach + 1, cap, 2, side // LANES + 2, strip, LANES), f32),
            pltpu.VMEM(((reach + 1) * strip, side), f32),
            pltpu.VMEM((2, angles, 2, 1, width), f32),
            pltpu.SemaphoreType.DMA((6 + blocks,)),
            pltpu.SemaphoreType.DMA((2, reach + 1)),
            pltpu.SemaphoreType.DMA((2, 1)),
            pltpu.SemaphoreType.DMA((2, cap)),
            pltpu.SemaphoreType.DMA((2, pieces)),
            pltpu.SemaphoreType.DMA((2, pieces)),
            pltpu.SemaphoreType.DMA((2, 2)),
        ],
        compiler_params=params(collective_id=0, has_side_effects=True),
        cost_estimate=cost(20),
        name="update",
    )(
        frame_count,
        *[
            pltpu.with_memory_space_constraint(item, pltpu.HBM)
            for item in (
                frame_table,
                object_field,
                probe,
                measured,
                *fourier_tables(side),
                factors,
            )
        ],
    )

    planes = strips // plane
    lines = (share, 2 * angles, LANES)
    solved, carried, incoming, evens = pl.pallas_call(
        forward_kernel,
        out_shape=[
            shape((blocks // 2, rows, LANES), f32),
            shape((blocks // 2, 2 * angles, GROUP, LANES), f32),
            shape((2, plane) + lines, f32),
            shape((rows, half), f32),
        ],
        in_specs=[vmem] * 7,
        out_specs=[vmem] * 4,
        scratch_shapes=[pltpu.VMEM((rows, half), bf16)] * 4
        + [
            pltpu.VMEM((2, blocks // 2, rows, LANES), f32),
            pltpu.VMEM((blocks // 2, rows, LANES), f32),
            pltpu.VMEM((blocks // 2, 2 * angles, GROUP, LANES), f32),
            pltpu.VMEM((2, plane) + lines, f32),
            pltpu.VMEM((2, plane) + lines, f32),
            pltpu.VMEM((2,) + lines, f32),
            pltpu.VMEM((2, planes) + lines, f32),
            pltpu.VMEM((2, plane) + lines, f32),
            pltpu.SemaphoreType.DMA((2, plane)),
            pltpu.SemaphoreType.DMA((2, plane)),
            pltpu.SemaphoreType.DMA((2, planes)),
            pltpu.SemaphoreType.DMA((2, planes)),
            pltpu.SemaphoreType.DMA((2, plane)),
            pltpu.SemaphoreType.DMA((2, plane)),
        ],
        compiler_params=params(collective_id=1, has_side_effects=True),
        cost_estimate=cost(15),
        name="forward",
    )(source, *half_tables, decays, joins)
    updated, phase_map = pl.pallas_call(
        inverse_kernel,
        out_shape=[shape(object_field.shape, f32), shape((angles, strip, width), f32)],
        in_specs=[vmem] * 8,
        out_specs=[hbm, hbm],
        scratch_shapes=[
            pltpu.VMEM((rows, half), bf16),
            pltpu.VMEM((rows, half), bf16),
            pltpu.VMEM((angles, strip, width), f32),
            pltpu.SemaphoreType.DMA((width // TILE,)),
            pltpu.SemaphoreType.DMA((blocks,)),
        ],
        compiler_params=params(),
        cost_estimate=cost(6),
        name="inverse",
    )(held, solved, carried, incoming, evens, *half_tables[2:], decays)
    return (updated, phase_map)


def solution(mesh):
    return jax.shard_map(
        body,
        mesh=mesh,
        in_specs=(
            P("group", None, "tile", None),
            P(),
            P(("group", "tile"), None, None),
            P(("group", "tile"), None),
            P(("group", "tile")),
        ),
        out_specs=(P("group", None, "tile", None), P("group", "tile", None)),
        check_vma=False,
    )
```

```python
import functools
import math

import numpy as np
import jax
import jax.numpy as jnp
from jax import lax
from jax.experimental import pallas as pl
from jax.experimental.pallas import tpu as pltpu
from jax.sharding import PartitionSpec as P

magnitude_floor = 0.5
soften_term = 0.5
screen_term = 0.0001
epsilon_term = 1e-06
f32 = jnp.float32
bf16 = jnp.bfloat16
LANES = 128
GROUP = 8
TILE = 256
VMEM_BYTES = 30 * 1024 * 1024
MESH = pl.DeviceIdType.MESH
vmem = pl.BlockSpec(memory_space=pltpu.VMEM)
smem = pl.BlockSpec(memory_space=pltpu.SMEM)
hbm = pl.BlockSpec(memory_space=pltpu.HBM)


def cost(micros):
    return pl.CostEstimate(
        flops=0, bytes_accessed=int(micros * 3_000_000), transcendentals=0
    )


def params(**more):
    return pltpu.CompilerParams(vmem_limit_bytes=VMEM_BYTES, **more)


def fourier_tables(side):
    indices = np.arange(side)
    products = indices[:, None] * indices[None, :] % side
    phases = products.astype(np.float64) * (-2.0 * math.pi / side)
    scale = 1.0 / math.sqrt(side)
    return (
        jnp.asarray(np.cos(phases) * scale, f32).astype(bf16),
        jnp.asarray(np.sin(phases) * scale, f32).astype(bf16),
    )


def frequencies(grid_side):
    quarter = np.arange(grid_side // 4)
    even = np.concatenate([4 * quarter, 4 * quarter + 2])
    return even, 2 * np.arange(grid_side // 2) + 1


def cosine_factors(grid_side):
    half = grid_side // 2
    step = 32
    out = []
    for freqs in frequencies(grid_side):
        scale = np.where(freqs == 0, math.sqrt(1.0 / grid_side), math.sqrt(2.0 / grid_side))
        coarse = (2 * step * np.arange(half // step)[:, None] * freqs[None, :]) % (4 * grid_side)
        fine = ((2 * np.arange(step)[:, None] + 1) * freqs[None, :]) % (4 * grid_side)
        unit = math.pi / (2 * grid_side)
        out.append(
            np.stack(
                [
                    np.cos(coarse * unit) * scale,
                    np.sin(coarse * unit) * scale,
                    np.cos(fine * unit),
                    np.sin(fine * unit),
                ]
            )
        )
    return jnp.asarray(np.stack(out), f32)


def decay_tables(grid_side, strip_rows, plane):
    half = grid_side // 2
    freqs = np.concatenate(frequencies(grid_side)).astype(np.float64)
    shift = screen_term + 2.0 - 2.0 * np.cos(freqs * math.pi / grid_side)
    rate = 2.0 * np.arcsinh(np.sqrt(shift) / 2.0)
    gain = 2.0 / (2.0 * np.sinh(rate))
    groups = strip_rows // GROUP
    segments = np.exp(-groups * np.arange(GROUP)[:, None] * rate)
    steps = np.exp(-(np.arange(groups)[:, None] + 1) * rate)
    jumps = np.exp(-groups * np.array([[1], [2], [4]]) * rate)
    spare = np.zeros((GROUP - 4,) + gain.shape)
    decays = np.concatenate(
        [segments, segments[::-1], gain[None], jumps, spare, steps, steps[::-1]]
    )
    spans = strip_rows * np.array([[1], [plane], [grid_side // strip_rows]])
    closing = 1.0 / (1.0 - np.exp(-2.0 * grid_side * rate))
    joins = np.concatenate([np.exp(-spans * rate), closing[None], gain[None]])
    return decays.astype(np.float32), joins.astype(np.float32)


def table_rows(factors, part, high, low):
    step = factors.shape[2]

    def run(block, _):
        rows = pl.ds(pl.multiple_of(block * step, step), step)
        value = (
            factors[part, 0, pl.ds(block, 1)] * factors[part, 2]
            - factors[part, 1, pl.ds(block, 1)] * factors[part, 3]
        )
        rounded = value.astype(bf16)
        high[rows] = rounded
        low[rows] = (value - rounded.astype(f32)).astype(bf16)
        return 0

    lax.fori_loop(0, high.shape[0] // step, run, 0)


def window_start(column, width, span):
    return jnp.minimum(column // LANES, (width - span) // LANES) * LANES


def power_of(re, im):
    return re * re + im * im + 0.5 * soften_term


def half_bond(first, second):
    cross = first[0] * second[1] - first[1] * second[0]
    return cross / (first[2] + second[2])


def update_kernel(
    frame_count, frame_table, field, probe_in, measured, cos_in, sin_in, factors_in,
    held, source, even_hi, even_lo, odd_hi, odd_lo,
    staged, halo, power, drops, shifts, bonds, partial, afters, tables, counts, probe, cos_ref, sin_ref, factors, moved, cuts, arrived, away, landed,
    own, placed, window, edges,
    load_sems, tell_sems, count_sems, moved_sems, fetch_sems, give_sems, edge_sems,
):
    count = lax.axis_size("tile")
    me = lax.axis_index("tile")
    angles, _, strip, width = field.shape
    cap, side = measured.shape[0], measured.shape[1]
    span = side + LANES
    lanes = span // LANES
    blocks = width // LANES
    reach = tables.shape[0] - 1
    middle = reach // 2
    total = (reach + 1) * strip
    others = [j for j in range(reach + 1) if j != middle]

    def inside(place):
        return (place >= 0) & (place < count)

    def load(index, source, target):
        return pltpu.make_async_copy(source, target, load_sems.at[index])

    loads = [
        load(0, frame_table, tables.at[0]),
        load(1, factors_in, factors),
        load(2, probe_in, probe),
        load(3, cos_in, cos_ref),
        load(4, sin_in, sin_ref),
        load(5, measured, staged),
    ]
    strips = [
        load(6 + block, field.at[:, :, :, block * LANES : (block + 1) * LANES], held.at[:, :, block])
        for block in range(blocks)
    ]
    for item in [loads[0], loads[5]] + strips + loads[1:5]:
        item.start()

    def send(source, target, sems, index, by):
        copy = pltpu.make_async_remote_copy(
            src_ref=source,
            dst_ref=target,
            send_sem=sems.at[0, index],
            recv_sem=sems.at[1, index],
            device_id={"tile": me + by},
            device_id_type=MESH,
        )
        return copy, inside(me + by), inside(me - by)

    barrier = pltpu.get_barrier_semaphore()
    met = jnp.zeros((), jnp.int32)
    for by in [sign * by for by in range(1, reach + 1) for sign in (1, -1)]:

        @pl.when(inside(me + by))
        def _():
            pl.semaphore_signal(
                barrier, inc=1, device_id={"tile": me + by}, device_id_type=MESH
            )

        met = met + jnp.where(inside(me + by), 1, 0)
    pl.semaphore_wait(barrier, met)

    tells = [
        send(tables.at[0], tables.at[j], tell_sems, j, j) for j in range(1, reach + 1)
    ]
    tells.append(send(frame_count, counts, count_sems, 0, middle))
    moves = [
        send(staged.at[s], moved.at[s], moved_sems, s, middle) for s in range(cap)
    ]
    fetches = [
        [send(cuts.at[j, s], arrived.at[j, s], fetch_sems, s * (reach + 1) + j, middle - j) for j in others]
        for s in range(cap)
    ]
    gives = [
        [send(away.at[j, s], landed.at[j, s], give_sems, s * (reach + 1) + j, j - middle) for j in others]
        for s in range(cap)
    ]
    borders = [
        send(edges.at[1], halo.at[0], edge_sems, 0, 1),
        send(edges.at[0], halo.at[1], edge_sems, 1, -1),
    ]
    started = []

    def start(items):
        for copy, sends, takes in items:
            pl.when(sends)(copy.start)
            started.append((copy, sends))

    def arrive(items):
        for copy, sends, takes in items:
            pl.when(takes)(copy.wait_recv)

    def blank(items, wipe):
        for index, (copy, sends, takes) in enumerate(items):

            @pl.when(jnp.logical_not(takes))
            def _():
                wipe(index)

    def wipe_table(index):
        if index == reach:
            counts[0] = 0
        else:
            for s in range(cap):
                for item in range(3):
                    tables[index + 1, s, item] = 0

    def wipe(ref, *first):
        ref[first] = jnp.zeros(ref.shape[len(first):], ref.dtype)

    loads[0].wait()
    start(tells)
    loads[5].wait()
    start(moves)
    blank(tells, wipe_table)
    blank(moves, lambda s: wipe(moved, s))
    for s in range(cap):
        blank(fetches[s], lambda index: wipe(arrived, others[index], s))
        blank(gives[s], lambda index: wipe(landed, others[index], s))
    blank(borders, lambda index: wipe(halo, index))
    for j in range(reach + 1):
        for s in range(cap):
            for part in range(2):
                placed[j, s, part, 0] = jnp.zeros((strip, LANES), f32)
    loads[1].wait()
    table_rows(factors, 0, even_hi, even_lo)
    for item in strips:
        item.wait()
    arrive(tells)

    def first_block(j, s):
        return jnp.minimum(tables[j, s, 1] // LANES, blocks - lanes)

    for s in range(cap):
        for j in others + [middle]:
            block = first_block(j, s)
            shift = tables[j, s, 1] - block * LANES
            angle = tables[j, s, 2]
            for part in range(2):
                piece = jnp.concatenate(
                    [held[angle, part, block + lane] for lane in range(lanes)], 1
                )
                turned = pltpu.roll(piece, lax.rem(span - shift, span), 1)
                target = arrived if j == middle else cuts
                target[j, s, part] = turned[:, :side].astype(bf16)
        start(fetches[s])

    table_rows(factors, 1, odd_hi, odd_lo)
    for item in loads[2:5]:
        item.wait()
    cos_part, sin_part = cos_ref[...], sin_ref[...]
    stacked = jnp.concatenate([cos_part, sin_part], 0)
    joined = jnp.concatenate([cos_part, sin_part], 1)
    probe_re, probe_im = probe[0], probe[1]
    peak = jnp.max(probe_re * probe_re + probe_im * probe_im) + epsilon_term

    def left(re, im, sign):
        products = jnp.dot(
            stacked, jnp.concatenate([re, im], 1), preferred_element_type=f32
        )
        cc, ci = products[:side, :side], products[:side, side:]
        sc, si = products[side:, :side], products[side:, side:]
        return (cc - si, ci + sc) if sign > 0 else (cc + si, ci - sc)

    def right(re, im, sign):
        products = jnp.dot(
            jnp.concatenate([re, im], 0), joined, preferred_element_type=f32
        )
        rc, rs = products[:side, :side], products[:side, side:]
        ic, js = products[side:, :side], products[side:, side:]
        return (rc - js, rs + ic) if sign > 0 else (rc + js, ic - rs)

    for s in range(cap):
        arrive(fetches[s])
        offset = tables[middle, s, 0]
        patch = []
        for part in range(2):
            for j in range(reach + 1):
                window[j * strip : (j + 1) * strip] = arrived[j, s, part].astype(f32)
            turned = pltpu.roll(window[...], lax.rem(total - offset, total), 0)
            patch.append(turned[:side])
        wave_re = (probe_re * patch[0] - probe_im * patch[1]).astype(bf16)
        wave_im = (probe_re * patch[1] + probe_im * patch[0]).astype(bf16)
        half_re, half_im = left(wave_re, wave_im, 1)
        spec_re, spec_im = right(half_re.astype(bf16), half_im.astype(bf16), 1)
        amplitude = jnp.sqrt(spec_re * spec_re + spec_im * spec_im)
        arrive(moves[s : s + 1])
        factor = moved[s].astype(f32) / jnp.maximum(amplitude, magnitude_floor) - 1.0
        back_re, back_im = left(
            (spec_re * factor).astype(bf16), (spec_im * factor).astype(bf16), -1
        )
        corr_re, corr_im = right(back_re.astype(bf16), back_im.astype(bf16), -1)
        live = s < counts[0]
        updates = (
            (probe_re * corr_re + probe_im * corr_im) / peak,
            (probe_re * corr_im - probe_im * corr_re) / peak,
        )
        for part in range(2):
            window[:side] = jnp.where(live, updates[part], 0.0)
            window[side:] = jnp.zeros((total - side, side), f32)
            turned = pltpu.roll(window[...], offset, 0)
            for j in range(reach + 1):
                piece = turned[j * strip : (j + 1) * strip]
                if j == middle:
                    own[s, part] = piece
                else:
                    away[j, s, part] = piece.astype(bf16)
        start(gives[s])

    pad = jnp.zeros((strip, LANES), f32)

    def shifted(source, j, s):
        shift = tables[j, s, 1] - first_block(j, s) * LANES
        for part in range(2):
            value = jnp.concatenate([source[part].astype(f32), pad], 1)
            turned = pltpu.roll(value, shift, 1)
            for lane in range(lanes):
                placed[j, s, part, lane + 1] = turned[:, lane * LANES : (lane + 1) * LANES]

    def add(items, rows):
        def chunk(block, _):
            for angle in range(angles):
                found = []
                for j, s in items:
                    near = block - first_block(j, s)
                    hit = (tables[j, s, 2] == angle) & (near >= 0) & (near < lanes)
                    found.append(jnp.where(hit, near + 1, 0))
                for part in range(2):
                    for row in rows:
                        value = held[angle, part, block, row]
                        for (j, s), index in zip(items, found):
                            value = value + placed[j, s, part, index, row]
                        held[angle, part, block, row] = value
            return 0

        lax.fori_loop(0, blocks, chunk, 0)

    for s in range(cap):
        shifted(own.at[s], middle, s)
    early = [(middle, s) for s in range(cap)]
    for s in range(cap - 1):
        arrive(gives[s])
        for j in others:
            shifted(landed.at[j, s], j, s)
        early += [(j, s) for j in others]
    add(early, [slice(0, strip)])
    arrive(gives[cap - 1])
    for j in others:
        shifted(landed.at[j, cap - 1], j, cap - 1)
    late = [(j, cap - 1) for j in others]
    add(late, [slice(0, GROUP), slice(strip - GROUP, strip)])
    for angle in range(angles):
        for part in range(2):
            for block in range(blocks):
                where = slice(block * LANES, (block + 1) * LANES)
                edges[0, angle, part, :, where] = held[angle, part, block, :1]
                edges[1, angle, part, :, where] = held[angle, part, block, strip - 1 :]
    start(borders)
    add(late, [slice(GROUP, strip - GROUP)])

    groups = strip // GROUP
    lane = lax.broadcasted_iota(jnp.int32, (GROUP, LANES), 1)
    segment = lax.broadcasted_iota(jnp.int32, (GROUP, LANES), 0)
    drops[:GROUP] = jnp.zeros((GROUP, LANES), f32)
    for angle in range(angles):

        def rows_of(group):
            return slice(group * GROUP, (group + 1) * GROUP)

        def prepare(block, slot):
            for group in range(groups):
                pair = [held[angle, part, block, rows_of(group)] for part in range(2)]
                power[slot, rows_of(group)] = power_of(*pair)
                for part, value in enumerate(pair):
                    shifts[slot, part, group] = pltpu.roll(value, 1, 1)

        def combine(block, slot):
            for group in range(groups):
                here = [held[angle, part, block, rows_of(group)] for part in range(2)]
                here.append(power[slot, rows_of(group)])
                if group == groups - 1:
                    below = [
                        jnp.where(segment == GROUP - 1, 0.0, pltpu.roll(value, GROUP - 1, 0))
                        for value in here[:2]
                    ]
                    below.append(power_of(*below))
                else:
                    lower = slice(group * GROUP + 1, (group + 1) * GROUP + 1)
                    below = [held[angle, part, block, lower] for part in range(2)]
                    below.append(power[slot, lower])
                down = half_bond(here, below)
                first = (group + 1) * GROUP
                drops[first : first + GROUP] = down
                up = drops[first - 1 : first - 1 + GROUP]
                left = [
                    jnp.where(lane == 0, shifts[1 - slot, part, group], shifts[slot, part, group])
                    for part in range(2)
                ]
                bond = half_bond(left + [power_of(*left)], here)
                bonds[slot, group] = bond
                partial[slot, group] = up - down + bond

        def finish(block, slot):
            behind = pl.ds(pl.multiple_of(jnp.maximum(block - 1, 0) * LANES, LANES), LANES)
            for group in range(groups):
                after = pltpu.roll(bonds[slot, group], LANES - 1, 1)
                first = angle * strip + group * GROUP
                source[first : first + GROUP, behind] = partial[1 - slot, group] - jnp.where(
                    lane == LANES - 1, after, afters[group]
                )
                afters[group] = after

        def step(pair, _):
            block = 2 * pair
            finish(block - 1, 1)
            combine(block, 0)
            prepare(block + 1, 1)
            finish(block, 0)
            combine(block + 1, 1)
            prepare(jnp.minimum(block + 2, blocks - 1), 0)
            return 0

        for group in range(groups):
            for part in range(2):
                shifts[1, part, group] = jnp.zeros((GROUP, LANES), f32)
        prepare(0, 0)
        lax.fori_loop(0, blocks // 2, step, 0)
        finish(blocks - 1, 1)
        for group in range(groups):
            first = angle * strip + group * GROUP
            source[first : first + GROUP, width - LANES :] = partial[1, group] - jnp.where(
                lane == LANES - 1, 0.0, afters[group]
            )

    arrive(borders)

    def line(values):
        return values + [power_of(*values)]

    for angle in range(angles):
        for border, row in ((0, 0), (1, strip - 1)):
            inner = line(
                [
                    jnp.concatenate(
                        [held[angle, part, block, row : row + 1] for block in range(blocks)], 1
                    )
                    for part in range(2)
                ]
            )
            outer = line([halo[border, angle, part] for part in range(2)])
            place = slice(angle * strip + row, angle * strip + row + 1)
            source[place] = source[place] + half_bond(outer, inner)
    for copy, sends in started:
        pl.when(sends)(copy.wait_send)


def mirror(value):
    side = value.shape[1]
    rows = lax.broadcasted_iota(jnp.int32, (side, side), 0)
    columns = lax.broadcasted_iota(jnp.int32, (side, side), 1)
    swap = jnp.where(rows + columns == side - 1, 1.0, 0.0).astype(bf16)
    high = value.astype(bf16)
    low = (value - high.astype(f32)).astype(bf16)
    return jnp.dot(high, swap, preferred_element_type=f32) + jnp.dot(
        low, swap, preferred_element_type=f32
    )


def split_store(value, high, low, columns):
    rounded = value.astype(bf16)
    high[:, columns] = rounded
    low[:, columns] = (value - rounded.astype(f32)).astype(bf16)


def forward_kernel(
    source, even_hi, even_lo, odd_hi, odd_lo, decays, joins,
    solved, carried, incoming, odds,
    xeh, xel, xoh, xol, coefs,
    out, carries, ends, heard, sums, totals, told,
    up_sems, in_sems, over_sems, across_sems, down_sems, back_sems,
):
    angles, width = ends.shape[3] // 2, source.shape[1]
    strip, blocks = source.shape[0] // angles, width // LANES
    groups = strip // GROUP
    plane, share = ends.shape[1], ends.shape[2]
    planes = totals.shape[1]
    me = lax.axis_index("tile")
    floor_at, seat = me // plane, lax.rem(me, plane)
    beside = [lax.rem(seat + by, plane) for by in range(1, plane)]
    beyond_planes = [lax.rem(floor_at + by, planes) for by in range(1, planes)]
    barrier = pltpu.get_barrier_semaphore()
    for peer in [floor_at * plane + other for other in beside] + [
        other * plane + seat for other in beyond_planes
    ]:
        pl.semaphore_signal(barrier, inc=1, device_id={"tile": peer}, device_id_type=MESH)

    def hop(source_ref, target_ref, send_sem, recv_sem, peer):
        return pltpu.make_async_remote_copy(
            src_ref=source_ref,
            dst_ref=target_ref,
            send_sem=send_sem,
            recv_sem=recv_sem,
            device_id={"tile": peer},
            device_id_type=MESH,
        )

    def up(part, other, slot):
        return hop(
            ends.at[part, other], heard.at[part, slot], up_sems.at[part, other],
            in_sems.at[part, slot], floor_at * plane + other,
        )

    def over(part, other, slot):
        return hop(
            sums.at[part], totals.at[part, slot], over_sems.at[part, other],
            across_sems.at[part, slot], other * plane + seat,
        )

    def down(part, other, slot):
        return hop(
            told.at[part, other], incoming.at[part, slot], down_sems.at[part, other],
            back_sems.at[part, slot], floor_at * plane + other,
        )

    def gather(part):
        for other in beside:
            up(part, other, seat).start()
        heard[part, seat] = ends[part, seat]

    def spread(part):
        for other in beside:
            up(part, other, other).wait_recv()
        step = joins[part, seat, 0][:, None]
        fall = heard[part, 0, :, :angles]
        rise = heard[part, plane - 1, :, angles:]
        for item in range(1, plane):
            fall = fall * step + heard[part, item, :, :angles]
            rise = rise * step + heard[part, plane - 1 - item, :, angles:]
        sums[part, :, :angles] = fall
        sums[part, :, angles:] = rise
        for other in beyond_planes:
            over(part, other, floor_at).start()
        totals[part, floor_at] = sums[part]

    def answer(part):
        for other in beyond_planes:
            over(part, other, other).wait_recv()
        step, leap, whole, closing, gain = [joins[part, seat, item][:, None] for item in range(5)]
        bottom = totals[part, 0, :, :angles]
        top = totals[part, planes - 1, :, angles:]
        for item in range(1, planes):
            bottom = bottom * leap + totals[part, item, :, :angles]
            top = top * leap + totals[part, planes - 1 - item, :, angles:]
        fall = (top + whole * bottom) * closing
        rise = (bottom + whole * top) * closing
        fall_here, rise_here = fall, rise
        for item in range(planes):
            fall_here = jnp.where(floor_at == item, fall, fall_here)
            fall = fall * leap + totals[part, item, :, :angles]
            back = planes - 1 - item
            rise_here = jnp.where(floor_at == back, rise, rise_here)
            rise = rise * leap + totals[part, back, :, angles:]
        for item in range(plane):
            told[part, item, :, :angles] = fall_here * gain
            fall_here = fall_here * step + heard[part, item, :, :angles]
            back = plane - 1 - item
            told[part, back, :, angles:] = rise_here * gain
            rise_here = rise_here * step + heard[part, back, :, angles:]
        for other in beside:
            down(part, other, seat).start()
        incoming[part, seat] = told[part, seat]

    def learn(part):
        for other in beside:
            down(part, other, other).wait_recv()

    segment = lax.broadcasted_iota(jnp.int32, (GROUP, LANES), 0)
    half = width // 2

    def tile(index):
        return slice(index * TILE, (index + 1) * TILE)

    tiles = half // TILE
    sums_even = []
    for index in range(tiles):
        near = source[:, tile(index)]
        far = mirror(source[:, tile(width // TILE - 1 - index)])
        sums_even.append(near + far)
        split_store(near - far, xoh, xol, tile(index))
    for index in range(tiles // 2):
        near, far = sums_even[index], mirror(sums_even[tiles - 1 - index])
        split_store(near + far, xeh, xel, tile(index))
        split_store(near - far, xeh, xel, tile(index + tiles // 2))

    def transform(part, index):
        high, low, table_hi, table_lo = (
            (xeh, xel, even_hi, even_lo),
            (xoh, xol, odd_hi, odd_lo),
        )[part]
        where = tile(index)
        depth = half if part else half // 2
        start = 0 if part or index < tiles // 2 else depth
        inner, outer = slice(start, start + depth), slice(0, depth)
        value = (
            jnp.dot(high[:, inner], table_hi[outer, where], preferred_element_type=f32)
            + jnp.dot(low[:, inner], table_hi[outer, where], preferred_element_type=f32)
            + jnp.dot(high[:, inner], table_lo[outer, where], preferred_element_type=f32)
        )
        for column in range(TILE // LANES):
            block = index * TILE // LANES + column
            coefs[part, block] = value[:, column * LANES : (column + 1) * LANES]

    def scan(part):
        result, carry_ref = ((solved, carried), (out, carries))[part]

        def run(chunk, _):
            table = pl.ds(pl.multiple_of(part * half + chunk * LANES, LANES), LANES)
            owner, place = chunk // share, lax.rem(chunk, share)
            gain = decays[2 * GROUP : 2 * GROUP + 1, table]
            step = decays[3 * GROUP : 3 * GROUP + 1, table]
            for angle in range(angles):
                values = [
                    coefs[part, chunk, pl.ds(angle * strip + group, GROUP, stride=groups)]
                    for group in range(groups)
                ]
                fall, falls = values[0], [values[0]]
                for group in range(1, groups):
                    fall = values[group] + step * fall
                    falls.append(fall)
                rise = values[-1]
                for group in reversed(range(groups)):
                    total = falls[group]
                    if group < groups - 1:
                        later = step * rise
                        total = total + later
                        rise = values[group] + later
                    first = angle * strip + group * GROUP
                    result[chunk, first : first + GROUP] = gain * total
                for index, by in enumerate((1, 2, 4)):
                    jump = decays[2 * GROUP + 1 + index : 2 * GROUP + 2 + index, table]
                    fall = fall + jnp.where(segment >= by, pltpu.roll(fall, by, 0), 0.0) * jump
                    rise = (
                        rise
                        + jnp.where(segment < GROUP - by, pltpu.roll(rise, GROUP - by, 0), 0.0)
                        * jump
                    )
                ends[part, owner, place, angle : angle + 1] = fall[GROUP - 1 :]
                ends[part, owner, place, angles + angle : angles + angle + 1] = rise[:1]
                carry_ref[chunk, angle] = gain * jnp.where(
                    segment >= 1, pltpu.roll(fall, 1, 0), 0.0
                )
                carry_ref[chunk, angles + angle] = gain * jnp.where(
                    segment < GROUP - 1, pltpu.roll(rise, GROUP - 1, 0), 0.0
                )
            return 0

        lax.fori_loop(0, blocks // 2, run, 0, unroll=2)

    for index in range(tiles):
        transform(1, index)
    scan(1)
    pl.semaphore_wait(barrier, plane + planes - 2)
    gather(1)
    for index in range(tiles):
        transform(0, index)
    spread(1)
    scan(0)
    gather(0)
    spread(0)
    answer(1)
    answer(0)
    learn(1)
    enter(1, out, carries, incoming, decays, xoh, xol)
    for index in range(tiles):
        odds[:, tile(index)] = restored(xoh, xol, odd_hi, odd_lo, tile(index))
    learn(0)
    for part in range(2):
        for other in beside:
            up(part, other, seat).wait_send()
            down(part, other, seat).wait_send()
        for other in beyond_planes:
            over(part, other, floor_at).wait_send()


def enter(part, value, carries, incoming, decays, high, low):
    angles = incoming.shape[3] // 2
    strip = value.shape[1] // angles
    half = value.shape[0] * LANES
    groups = strip // GROUP
    length = min(groups, GROUP)
    share = incoming.shape[2]

    def run(chunk, _):
        where = pl.ds(pl.multiple_of(chunk * LANES, LANES), LANES)
        table = pl.ds(pl.multiple_of(part * half + chunk * LANES, LANES), LANES)
        owner, place = chunk // share, lax.rem(chunk, share)
        for angle in range(angles):
            fall = (
                carries[chunk, angle]
                + decays[:GROUP, table] * incoming[part, owner, place, angle : angle + 1]
            )
            rise = (
                carries[chunk, angles + angle]
                + decays[GROUP : 2 * GROUP, table]
                * incoming[part, owner, place, angles + angle : angles + angle + 1]
            )
            for pair in range(0, strip, 2 * GROUP):
                rows = []
                for row in range(pair, pair + 2 * GROUP, length):
                    owner_row, group = row // groups, row % groups
                    ahead = 3 * GROUP + group
                    behind = ahead + groups
                    rows.append(
                        value[
                            chunk,
                            pl.ds(angle * strip + group * GROUP + owner_row, length, stride=GROUP),
                        ]
                        + decays[ahead : ahead + length, table] * fall[owner_row : owner_row + 1]
                        + decays[behind : behind + length, table] * rise[owner_row : owner_row + 1]
                    )
                item = jnp.concatenate(rows, 0)
                rounded = item.astype(bf16)
                start = angle * strip + pair
                high[start : start + 2 * GROUP, where] = rounded
                low[start : start + 2 * GROUP, where] = (item - rounded.astype(f32)).astype(bf16)
        return 0

    lax.fori_loop(0, half // LANES, run, 0)


def restored(high, low, table_hi, table_lo, where, depth=slice(None)):
    last = (((1,), (1,)), ((), ()))
    return (
        lax.dot_general(high[:, depth], table_hi[where, depth], last, preferred_element_type=f32)
        + lax.dot_general(low[:, depth], table_hi[where, depth], last, preferred_element_type=f32)
        + lax.dot_general(high[:, depth], table_lo[where, depth], last, preferred_element_type=f32)
    )


def inverse_kernel(
    field, value, carries, incoming, odds, even_hi, even_lo, decays,
    updated, out, xh, xl, parted, sems, field_sems,
):
    angles, strip, width = out.shape
    half = width // 2
    blocks = width // LANES
    copies = []
    for block in range(blocks):
        copy = pltpu.make_async_copy(
            field.at[:, :, block],
            updated.at[:, :, :, block * LANES : (block + 1) * LANES],
            field_sems.at[block],
        )
        copy.start()
        copies.append(copy)
    enter(0, value, carries, incoming, decays, xh, xl)
    tiles = [slice(first, first + TILE) for first in range(0, half, TILE)]

    def pair(index):
        return [
            restored(xh, xl, even_hi, even_lo, tiles[index], slice(first, first + half // 2))
            for first in (0, half // 2)
        ]

    later = pair(0)
    for index in range(len(tiles) // 2):
        whole, crossed = later
        if index + 1 < len(tiles) // 2:
            later = pair(index + 1)
        for place, even in (
            (index, whole + crossed),
            (len(tiles) - 1 - index, mirror(whole - crossed)),
        ):
            first, odd = tiles[place].start, odds[:, tiles[place]]
            near = even + odd
            far = mirror(even - odd)
            for item, start in ((near, first), (far, width - first - TILE)):
                where = slice(start, start + TILE)
                for angle in range(angles):
                    parted[angle, :, where] = item[angle * strip : (angle + 1) * strip]
                copy = pltpu.make_async_copy(
                    parted.at[:, :, where], out.at[:, :, where], sems.at[start // TILE]
                )
                copy.start()
                copies.append(copy)
    for copy in copies:
        copy.wait()


def body(object_field, probe, measured, frame_table, frame_count):
    angles, _, strip, width = object_field.shape
    side = probe.shape[1]
    cap = measured.shape[0]
    half = width // 2
    reach = side // strip
    rows = angles * strip
    strips = lax.axis_size("tile")
    blocks = width // LANES
    shape = jax.ShapeDtypeStruct

    pieces = (reach + 1) * cap
    plane = 2 ** (int(math.log2(strips)) // 2)
    share = blocks // (2 * plane)
    decays, joins = decay_tables(width, strip, plane)
    joins = jnp.asarray(joins.reshape(-1, 2, plane, share, LANES).transpose(1, 2, 0, 3, 4))

    factors = cosine_factors(width)
    table = (reach + 1, cap, 2, strip, side)
    held, source, *half_tables = pl.pallas_call(
        update_kernel,
        out_shape=[
            shape((angles, 2, blocks, strip, LANES), f32),
            shape((rows, width), f32),
        ]
        + [shape((half, half), bf16)] * 4,
        in_specs=[smem] + [hbm] * 7,
        out_specs=[vmem] * 6,
        scratch_shapes=[
            pltpu.VMEM(measured.shape, bf16),
            pltpu.VMEM((2, angles, 2, 1, width), f32),
            pltpu.VMEM((2, strip, LANES), f32),
            pltpu.VMEM((strip + GROUP, LANES), f32),
            pltpu.VMEM((2, 2, strip // GROUP, GROUP, LANES), f32),
            pltpu.VMEM((2, strip // GROUP, GROUP, LANES), f32),
            pltpu.VMEM((2, strip // GROUP, GROUP, LANES), f32),
            pltpu.VMEM((strip // GROUP, GROUP, LANES), f32),
            pltpu.SMEM((reach + 1, cap, 3), jnp.int32),
            pltpu.SMEM((1,), jnp.int32),
            pltpu.VMEM(probe.shape, f32),
            pltpu.VMEM((side, side), bf16),
            pltpu.VMEM((side, side), bf16),
            pltpu.VMEM(factors.shape, f32),
            pltpu.VMEM(measured.shape, bf16),
            pltpu.VMEM(table, bf16),
            pltpu.VMEM(table, bf16),
            pltpu.VMEM(table, bf16),
            pltpu.VMEM(table, bf16),
            pltpu.VMEM((cap, 2, strip, side), f32),
            pltpu.VMEM((reach + 1, cap, 2, side // LANES + 2, strip, LANES), f32),
            pltpu.VMEM(((reach + 1) * strip, side), f32),
            pltpu.VMEM((2, angles, 2, 1, width), f32),
            pltpu.SemaphoreType.DMA((6 + blocks,)),
            pltpu.SemaphoreType.DMA((2, reach + 1)),
            pltpu.SemaphoreType.DMA((2, 1)),
            pltpu.SemaphoreType.DMA((2, cap)),
            pltpu.SemaphoreType.DMA((2, pieces)),
            pltpu.SemaphoreType.DMA((2, pieces)),
            pltpu.SemaphoreType.DMA((2, 2)),
        ],
        compiler_params=params(collective_id=0, has_side_effects=True),
        cost_estimate=cost(20),
        name="update",
    )(
        frame_count,
        *[
            pltpu.with_memory_space_constraint(item, pltpu.HBM)
            for item in (
                frame_table,
                object_field,
                probe,
                measured,
                *fourier_tables(side),
                factors,
            )
        ],
    )

    planes = strips // plane
    lines = (share, 2 * angles, LANES)
    solved, carried, incoming, odds = pl.pallas_call(
        forward_kernel,
        out_shape=[
            shape((blocks // 2, rows, LANES), f32),
            shape((blocks // 2, 2 * angles, GROUP, LANES), f32),
            shape((2, plane) + lines, f32),
            shape((rows, half), f32),
        ],
        in_specs=[vmem] * 7,
        out_specs=[vmem] * 4,
        scratch_shapes=[pltpu.VMEM((rows, half), bf16)] * 4
        + [
            pltpu.VMEM((2, blocks // 2, rows, LANES), f32),
            pltpu.VMEM((blocks // 2, rows, LANES), f32),
            pltpu.VMEM((blocks // 2, 2 * angles, GROUP, LANES), f32),
            pltpu.VMEM((2, plane) + lines, f32),
            pltpu.VMEM((2, plane) + lines, f32),
            pltpu.VMEM((2,) + lines, f32),
            pltpu.VMEM((2, planes) + lines, f32),
            pltpu.VMEM((2, plane) + lines, f32),
            pltpu.SemaphoreType.DMA((2, plane)),
            pltpu.SemaphoreType.DMA((2, plane)),
            pltpu.SemaphoreType.DMA((2, planes)),
            pltpu.SemaphoreType.DMA((2, planes)),
            pltpu.SemaphoreType.DMA((2, plane)),
            pltpu.SemaphoreType.DMA((2, plane)),
        ],
        compiler_params=params(collective_id=1, has_side_effects=True),
        cost_estimate=cost(15),
        name="forward",
    )(source, *half_tables, decays, joins)
    updated, phase_map = pl.pallas_call(
        inverse_kernel,
        out_shape=[shape(object_field.shape, f32), shape((angles, strip, width), f32)],
        in_specs=[vmem] * 8,
        out_specs=[hbm, hbm],
        scratch_shapes=[
            pltpu.VMEM((rows, half), bf16),
            pltpu.VMEM((rows, half), bf16),
            pltpu.VMEM((angles, strip, width), f32),
            pltpu.SemaphoreType.DMA((width // TILE,)),
            pltpu.SemaphoreType.DMA((blocks,)),
        ],
        compiler_params=params(),
        cost_estimate=cost(6),
        name="inverse",
    )(held, solved, carried, incoming, odds, *half_tables[:2], decays)
    return (updated, phase_map)


def solution(mesh):
    return jax.shard_map(
        body,
        mesh=mesh,
        in_specs=(
            P("group", None, "tile", None),
            P(),
            P(("group", "tile"), None, None),
            P(("group", "tile"), None),
            P(("group", "tile")),
        ),
        out_specs=(P("group", None, "tile", None), P("group", "tile", None)),
        check_vma=False,
    )
```

```python
import functools
import math

import numpy as np
import jax
import jax.numpy as jnp
from jax import lax
from jax.experimental import pallas as pl
from jax.experimental.pallas import tpu as pltpu
from jax.sharding import PartitionSpec as P

magnitude_floor = 0.5
soften_term = 0.5
screen_term = 0.0001
epsilon_term = 1e-06
f32 = jnp.float32
bf16 = jnp.bfloat16
LANES = 128
GROUP = 8
TILE = 256
VMEM_BYTES = 30 * 1024 * 1024
MESH = pl.DeviceIdType.MESH
vmem = pl.BlockSpec(memory_space=pltpu.VMEM)
smem = pl.BlockSpec(memory_space=pltpu.SMEM)
hbm = pl.BlockSpec(memory_space=pltpu.HBM)


def cost(micros):
    return pl.CostEstimate(
        flops=0, bytes_accessed=int(micros * 3_000_000), transcendentals=0
    )


def params(**more):
    return pltpu.CompilerParams(vmem_limit_bytes=VMEM_BYTES, **more)


def fourier_tables(side):
    indices = np.arange(side)
    products = indices[:, None] * indices[None, :] % side
    phases = products.astype(np.float64) * (-2.0 * math.pi / side)
    scale = 1.0 / math.sqrt(side)
    return (
        jnp.asarray(np.cos(phases) * scale, f32).astype(bf16),
        jnp.asarray(np.sin(phases) * scale, f32).astype(bf16),
    )


def frequencies(grid_side):
    quarter = np.arange(grid_side // 4)
    even = np.concatenate([4 * quarter, 4 * quarter + 2])
    return even, 2 * np.arange(grid_side // 2) + 1


def cosine_factors(grid_side):
    half = grid_side // 2
    step = 32
    out = []
    for freqs in frequencies(grid_side):
        scale = np.where(freqs == 0, math.sqrt(1.0 / grid_side), math.sqrt(2.0 / grid_side))
        coarse = (2 * step * np.arange(half // step)[:, None] * freqs[None, :]) % (4 * grid_side)
        fine = ((2 * np.arange(step)[:, None] + 1) * freqs[None, :]) % (4 * grid_side)
        unit = math.pi / (2 * grid_side)
        out.append(
            np.stack(
                [
                    np.cos(coarse * unit) * scale,
                    np.sin(coarse * unit) * scale,
                    np.cos(fine * unit),
                    np.sin(fine * unit),
                ]
            )
        )
    return jnp.asarray(np.stack(out), f32)


def decay_tables(grid_side, strip_rows, plane):
    half = grid_side // 2
    freqs = np.concatenate(frequencies(grid_side)).astype(np.float64)
    shift = screen_term + 2.0 - 2.0 * np.cos(freqs * math.pi / grid_side)
    rate = 2.0 * np.arcsinh(np.sqrt(shift) / 2.0)
    gain = 2.0 / (2.0 * np.sinh(rate))
    groups = strip_rows // GROUP
    segments = np.exp(-groups * np.arange(GROUP)[:, None] * rate)
    steps = np.exp(-(np.arange(groups)[:, None] + 1) * rate)
    jumps = np.exp(-groups * np.array([[1], [2], [4]]) * rate)
    spare = np.zeros((GROUP - 4,) + gain.shape)
    decays = np.concatenate(
        [segments, segments[::-1], gain[None], jumps, spare, steps, steps[::-1]]
    )
    spans = strip_rows * np.array([[1], [plane], [grid_side // strip_rows]])
    closing = 1.0 / (1.0 - np.exp(-2.0 * grid_side * rate))
    joins = np.concatenate([np.exp(-spans * rate), closing[None], gain[None]])
    return decays.astype(np.float32), joins.astype(np.float32)


def table_rows(factors, part, high, low):
    step = factors.shape[2]

    def run(block, _):
        rows = pl.ds(pl.multiple_of(block * step, step), step)
        value = (
            factors[part, 0, pl.ds(block, 1)] * factors[part, 2]
            - factors[part, 1, pl.ds(block, 1)] * factors[part, 3]
        )
        rounded = value.astype(bf16)
        high[rows] = rounded
        low[rows] = (value - rounded.astype(f32)).astype(bf16)
        return 0

    lax.fori_loop(0, high.shape[0] // step, run, 0)


def window_start(column, width, span):
    return jnp.minimum(column // LANES, (width - span) // LANES) * LANES


def power_of(re, im):
    return re * re + im * im + 0.5 * soften_term


def half_bond(first, second):
    cross = first[0] * second[1] - first[1] * second[0]
    return cross / (first[2] + second[2])


def update_kernel(
    frame_count, frame_table, field, probe_in, measured, cos_in, sin_in, factors_in,
    held, source, even_hi, even_lo, odd_hi, odd_lo,
    staged, halo, power, drops, shifts, bonds, partial, afters, tables, counts, probe, cos_ref, sin_ref, factors, moved, cuts, arrived, away, landed,
    own, placed, window, edges,
    load_sems, tell_sems, count_sems, moved_sems, fetch_sems, give_sems, edge_sems,
):
    count = lax.axis_size("tile")
    me = lax.axis_index("tile")
    angles, _, strip, width = field.shape
    cap, side = measured.shape[0], measured.shape[1]
    span = side + LANES
    lanes = span // LANES
    blocks = width // LANES
    reach = tables.shape[0] - 1
    middle = reach // 2
    total = (reach + 1) * strip
    others = [j for j in range(reach + 1) if j != middle]

    def inside(place):
        return (place >= 0) & (place < count)

    def load(index, source, target):
        return pltpu.make_async_copy(source, target, load_sems.at[index])

    loads = [
        load(0, frame_table, tables.at[0]),
        load(1, factors_in, factors),
        load(2, probe_in, probe),
        load(3, cos_in, cos_ref),
        load(4, sin_in, sin_ref),
        load(5, measured, staged),
    ]
    strips = [
        load(6 + block, field.at[:, :, :, block * LANES : (block + 1) * LANES], held.at[:, :, block])
        for block in range(blocks)
    ]
    for item in [loads[0], loads[5]] + strips + loads[1:5]:
        item.start()

    def send(source, target, sems, index, by):
        copy = pltpu.make_async_remote_copy(
            src_ref=source,
            dst_ref=target,
            send_sem=sems.at[0, index],
            recv_sem=sems.at[1, index],
            device_id={"tile": me + by},
            device_id_type=MESH,
        )
        return copy, inside(me + by), inside(me - by)

    barrier = pltpu.get_barrier_semaphore()
    met = jnp.zeros((), jnp.int32)
    for by in [sign * by for by in range(1, reach + 1) for sign in (1, -1)]:

        @pl.when(inside(me + by))
        def _():
            pl.semaphore_signal(
                barrier, inc=1, device_id={"tile": me + by}, device_id_type=MESH
            )

        met = met + jnp.where(inside(me + by), 1, 0)
    pl.semaphore_wait(barrier, met)

    tells = [
        send(tables.at[0], tables.at[j], tell_sems, j, j) for j in range(1, reach + 1)
    ]
    tells.append(send(frame_count, counts, count_sems, 0, middle))
    moves = [
        send(staged.at[s], moved.at[s], moved_sems, s, middle) for s in range(cap)
    ]
    fetches = [
        [send(cuts.at[j, s], arrived.at[j, s], fetch_sems, s * (reach + 1) + j, middle - j) for j in others]
        for s in range(cap)
    ]
    gives = [
        [send(away.at[j, s], landed.at[j, s], give_sems, s * (reach + 1) + j, j - middle) for j in others]
        for s in range(cap)
    ]
    borders = [
        send(edges.at[1], halo.at[0], edge_sems, 0, 1),
        send(edges.at[0], halo.at[1], edge_sems, 1, -1),
    ]
    started = []

    def start(items):
        for copy, sends, takes in items:
            pl.when(sends)(copy.start)
            started.append((copy, sends))

    def arrive(items):
        for copy, sends, takes in items:
            pl.when(takes)(copy.wait_recv)

    def blank(items, wipe):
        for index, (copy, sends, takes) in enumerate(items):

            @pl.when(jnp.logical_not(takes))
            def _():
                wipe(index)

    def wipe_table(index):
        if index == reach:
            counts[0] = 0
        else:
            for s in range(cap):
                for item in range(3):
                    tables[index + 1, s, item] = 0

    def wipe(ref, *first):
        ref[first] = jnp.zeros(ref.shape[len(first):], ref.dtype)

    loads[0].wait()
    start(tells)
    loads[5].wait()
    start(moves)
    blank(tells, wipe_table)
    blank(moves, lambda s: wipe(moved, s))
    for s in range(cap):
        blank(fetches[s], lambda index: wipe(arrived, others[index], s))
        blank(gives[s], lambda index: wipe(landed, others[index], s))
    blank(borders, lambda index: wipe(halo, index))
    for j in range(reach + 1):
        for s in range(cap):
            for part in range(2):
                placed[j, s, part, 0] = jnp.zeros((strip, LANES), f32)
    loads[1].wait()
    table_rows(factors, 0, even_hi, even_lo)
    for item in strips:
        item.wait()
    arrive(tells)

    def first_block(j, s):
        return jnp.minimum(tables[j, s, 1] // LANES, blocks - lanes)

    for s in range(cap):
        for j in others + [middle]:
            block = first_block(j, s)
            shift = tables[j, s, 1] - block * LANES
            angle = tables[j, s, 2]
            for part in range(2):
                piece = jnp.concatenate(
                    [held[angle, part, block + lane] for lane in range(lanes)], 1
                )
                turned = pltpu.roll(piece, lax.rem(span - shift, span), 1)
                target = arrived if j == middle else cuts
                target[j, s, part] = turned[:, :side].astype(bf16)
        start(fetches[s])

    table_rows(factors, 1, odd_hi, odd_lo)
    for item in loads[2:5]:
        item.wait()
    cos_part, sin_part = cos_ref[...], sin_ref[...]
    stacked = jnp.concatenate([cos_part, sin_part], 0)
    joined = jnp.concatenate([cos_part, sin_part], 1)
    probe_re, probe_im = probe[0], probe[1]
    peak = jnp.max(probe_re * probe_re + probe_im * probe_im) + epsilon_term

    def left(re, im, sign):
        products = jnp.dot(
            stacked, jnp.concatenate([re, im], 1), preferred_element_type=f32
        )
        cc, ci = products[:side, :side], products[:side, side:]
        sc, si = products[side:, :side], products[side:, side:]
        return (cc - si, ci + sc) if sign > 0 else (cc + si, ci - sc)

    def right(re, im, sign):
        products = jnp.dot(
            jnp.concatenate([re, im], 0), joined, preferred_element_type=f32
        )
        rc, rs = products[:side, :side], products[:side, side:]
        ic, js = products[side:, :side], products[side:, side:]
        return (rc - js, rs + ic) if sign > 0 else (rc + js, ic - rs)

    for s in range(cap):
        arrive(fetches[s])
        offset = tables[middle, s, 0]
        patch = []
        for part in range(2):
            for j in range(reach + 1):
                window[j * strip : (j + 1) * strip] = arrived[j, s, part].astype(f32)
            turned = pltpu.roll(window[...], lax.rem(total - offset, total), 0)
            patch.append(turned[:side])
        wave_re = (probe_re * patch[0] - probe_im * patch[1]).astype(bf16)
        wave_im = (probe_re * patch[1] + probe_im * patch[0]).astype(bf16)
        half_re, half_im = left(wave_re, wave_im, 1)
        spec_re, spec_im = right(half_re.astype(bf16), half_im.astype(bf16), 1)
        amplitude = jnp.sqrt(spec_re * spec_re + spec_im * spec_im)
        arrive(moves[s : s + 1])
        factor = moved[s].astype(f32) / jnp.maximum(amplitude, magnitude_floor) - 1.0
        back_re, back_im = left(
            (spec_re * factor).astype(bf16), (spec_im * factor).astype(bf16), -1
        )
        corr_re, corr_im = right(back_re.astype(bf16), back_im.astype(bf16), -1)
        live = s < counts[0]
        updates = (
            (probe_re * corr_re + probe_im * corr_im) / peak,
            (probe_re * corr_im - probe_im * corr_re) / peak,
        )
        for part in range(2):
            window[:side] = jnp.where(live, updates[part], 0.0)
            window[side:] = jnp.zeros((total - side, side), f32)
            turned = pltpu.roll(window[...], offset, 0)
            for j in range(reach + 1):
                piece = turned[j * strip : (j + 1) * strip]
                if j == middle:
                    own[s, part] = piece
                else:
                    away[j, s, part] = piece.astype(bf16)
        start(gives[s])

    pad = jnp.zeros((strip, LANES), f32)

    def shifted(source, j, s):
        shift = tables[j, s, 1] - first_block(j, s) * LANES
        for part in range(2):
            value = jnp.concatenate([source[part].astype(f32), pad], 1)
            turned = pltpu.roll(value, shift, 1)
            for lane in range(lanes):
                placed[j, s, part, lane + 1] = turned[:, lane * LANES : (lane + 1) * LANES]

    def add(items, rows):
        def chunk(block, _):
            for angle in range(angles):
                found = []
                for j, s in items:
                    near = block - first_block(j, s)
                    hit = (tables[j, s, 2] == angle) & (near >= 0) & (near < lanes)
                    found.append(jnp.where(hit, near + 1, 0))
                for part in range(2):
                    for row in rows:
                        value = held[angle, part, block, row]
                        for (j, s), index in zip(items, found):
                            value = value + placed[j, s, part, index, row]
                        held[angle, part, block, row] = value
            return 0

        lax.fori_loop(0, blocks, chunk, 0)

    for s in range(cap):
        shifted(own.at[s], middle, s)
    early = [(middle, s) for s in range(cap)]
    for s in range(cap - 1):
        arrive(gives[s])
        for j in others:
            shifted(landed.at[j, s], j, s)
        early += [(j, s) for j in others]
    add(early, [slice(0, strip)])
    arrive(gives[cap - 1])
    for j in others:
        shifted(landed.at[j, cap - 1], j, cap - 1)
    late = [(j, cap - 1) for j in others]
    add(late, [slice(0, GROUP), slice(strip - GROUP, strip)])
    for angle in range(angles):
        for part in range(2):
            for block in range(blocks):
                where = slice(block * LANES, (block + 1) * LANES)
                edges[0, angle, part, :, where] = held[angle, part, block, :1]
                edges[1, angle, part, :, where] = held[angle, part, block, strip - 1 :]
    start(borders)
    add(late, [slice(GROUP, strip - GROUP)])

    groups = strip // GROUP
    lane = lax.broadcasted_iota(jnp.int32, (GROUP, LANES), 1)
    segment = lax.broadcasted_iota(jnp.int32, (GROUP, LANES), 0)
    drops[:GROUP] = jnp.zeros((GROUP, LANES), f32)
    for angle in range(angles):

        def rows_of(group):
            return slice(group * GROUP, (group + 1) * GROUP)

        def prepare(block, slot):
            for group in range(groups):
                pair = [held[angle, part, block, rows_of(group)] for part in range(2)]
                power[slot, rows_of(group)] = power_of(*pair)
                for part, value in enumerate(pair):
                    shifts[slot, part, group] = pltpu.roll(value, 1, 1)

        def combine(block, slot):
            for group in range(groups):
                here = [held[angle, part, block, rows_of(group)] for part in range(2)]
                here.append(power[slot, rows_of(group)])
                if group == groups - 1:
                    below = [
                        jnp.where(segment == GROUP - 1, 0.0, pltpu.roll(value, GROUP - 1, 0))
                        for value in here[:2]
                    ]
                    below.append(power_of(*below))
                else:
                    lower = slice(group * GROUP + 1, (group + 1) * GROUP + 1)
                    below = [held[angle, part, block, lower] for part in range(2)]
                    below.append(power[slot, lower])
                down = half_bond(here, below)
                first = (group + 1) * GROUP
                drops[first : first + GROUP] = down
                up = drops[first - 1 : first - 1 + GROUP]
                left = [
                    jnp.where(lane == 0, shifts[1 - slot, part, group], shifts[slot, part, group])
                    for part in range(2)
                ]
                bond = half_bond(left + [power_of(*left)], here)
                bonds[slot, group] = bond
                partial[slot, group] = up - down + bond

        def finish(block, slot):
            behind = pl.ds(pl.multiple_of(jnp.maximum(block - 1, 0) * LANES, LANES), LANES)
            for group in range(groups):
                after = pltpu.roll(bonds[slot, group], LANES - 1, 1)
                first = angle * strip + group * GROUP
                source[first : first + GROUP, behind] = partial[1 - slot, group] - jnp.where(
                    lane == LANES - 1, after, afters[group]
                )
                afters[group] = after

        def step(pair, _):
            block = 2 * pair
            finish(block - 1, 1)
            combine(block, 0)
            prepare(block + 1, 1)
            finish(block, 0)
            combine(block + 1, 1)
            prepare(jnp.minimum(block + 2, blocks - 1), 0)
            return 0

        for group in range(groups):
            for part in range(2):
                shifts[1, part, group] = jnp.zeros((GROUP, LANES), f32)
        prepare(0, 0)
        lax.fori_loop(0, blocks // 2, step, 0)
        finish(blocks - 1, 1)
        for group in range(groups):
            first = angle * strip + group * GROUP
            source[first : first + GROUP, width - LANES :] = partial[1, group] - jnp.where(
                lane == LANES - 1, 0.0, afters[group]
            )

    arrive(borders)

    def line(values):
        return values + [power_of(*values)]

    for angle in range(angles):
        for border, row in ((0, 0), (1, strip - 1)):
            inner = line(
                [
                    jnp.concatenate(
                        [held[angle, part, block, row : row + 1] for block in range(blocks)], 1
                    )
                    for part in range(2)
                ]
            )
            outer = line([halo[border, angle, part] for part in range(2)])
            place = slice(angle * strip + row, angle * strip + row + 1)
            source[place] = source[place] + half_bond(outer, inner)
    for copy, sends in started:
        pl.when(sends)(copy.wait_send)


def mirror(value):
    side = value.shape[1]
    rows = lax.broadcasted_iota(jnp.int32, (side, side), 0)
    columns = lax.broadcasted_iota(jnp.int32, (side, side), 1)
    swap = jnp.where(rows + columns == side - 1, 1.0, 0.0).astype(bf16)
    high = value.astype(bf16)
    low = (value - high.astype(f32)).astype(bf16)
    return jnp.dot(high, swap, preferred_element_type=f32) + jnp.dot(
        low, swap, preferred_element_type=f32
    )


def split_store(value, high, low, columns):
    rounded = value.astype(bf16)
    high[:, columns] = rounded
    low[:, columns] = (value - rounded.astype(f32)).astype(bf16)


def forward_kernel(
    source, even_hi, even_lo, odd_hi, odd_lo, decays, joins,
    solved, carried, incoming, odds,
    xeh, xel, xoh, xol, coefs,
    out, carries, ends, heard, sums, totals, told,
    up_sems, in_sems, over_sems, across_sems, down_sems, back_sems,
):
    angles, width = ends.shape[3] // 2, source.shape[1]
    strip, blocks = source.shape[0] // angles, width // LANES
    groups = strip // GROUP
    plane, share = ends.shape[1], ends.shape[2]
    planes = totals.shape[1]
    me = lax.axis_index("tile")
    floor_at, seat = me // plane, lax.rem(me, plane)
    beside = [lax.rem(seat + by, plane) for by in range(1, plane)]
    beyond_planes = [lax.rem(floor_at + by, planes) for by in range(1, planes)]
    barrier = pltpu.get_barrier_semaphore()
    for peer in [floor_at * plane + other for other in beside] + [
        other * plane + seat for other in beyond_planes
    ]:
        pl.semaphore_signal(barrier, inc=1, device_id={"tile": peer}, device_id_type=MESH)

    def hop(source_ref, target_ref, send_sem, recv_sem, peer):
        return pltpu.make_async_remote_copy(
            src_ref=source_ref,
            dst_ref=target_ref,
            send_sem=send_sem,
            recv_sem=recv_sem,
            device_id={"tile": peer},
            device_id_type=MESH,
        )

    def up(part, other, slot):
        return hop(
            ends.at[part, other], heard.at[part, slot], up_sems.at[part, other],
            in_sems.at[part, slot], floor_at * plane + other,
        )

    def over(part, other, slot):
        return hop(
            sums.at[part], totals.at[part, slot], over_sems.at[part, other],
            across_sems.at[part, slot], other * plane + seat,
        )

    def down(part, other, slot):
        return hop(
            told.at[part, other], incoming.at[part, slot], down_sems.at[part, other],
            back_sems.at[part, slot], floor_at * plane + other,
        )

    def gather(part):
        for other in beside:
            up(part, other, seat).start()
        heard[part, seat] = ends[part, seat]

    def spread(part):
        for other in beside:
            up(part, other, other).wait_recv()
        step = joins[part, seat, 0][:, None]
        fall = heard[part, 0, :, :angles]
        rise = heard[part, plane - 1, :, angles:]
        for item in range(1, plane):
            fall = fall * step + heard[part, item, :, :angles]
            rise = rise * step + heard[part, plane - 1 - item, :, angles:]
        sums[part, :, :angles] = fall
        sums[part, :, angles:] = rise
        for other in beyond_planes:
            over(part, other, floor_at).start()
        totals[part, floor_at] = sums[part]

    def answer(part):
        for other in beyond_planes:
            over(part, other, other).wait_recv()
        step, leap, whole, closing, gain = [joins[part, seat, item][:, None] for item in range(5)]
        bottom = totals[part, 0, :, :angles]
        top = totals[part, planes - 1, :, angles:]
        for item in range(1, planes):
            bottom = bottom * leap + totals[part, item, :, :angles]
            top = top * leap + totals[part, planes - 1 - item, :, angles:]
        fall = (top + whole * bottom) * closing
        rise = (bottom + whole * top) * closing
        fall_here, rise_here = fall, rise
        for item in range(planes):
            fall_here = jnp.where(floor_at == item, fall, fall_here)
            fall = fall * leap + totals[part, item, :, :angles]
            back = planes - 1 - item
            rise_here = jnp.where(floor_at == back, rise, rise_here)
            rise = rise * leap + totals[part, back, :, angles:]
        for item in range(plane):
            told[part, item, :, :angles] = fall_here * gain
            fall_here = fall_here * step + heard[part, item, :, :angles]
            back = plane - 1 - item
            told[part, back, :, angles:] = rise_here * gain
            rise_here = rise_here * step + heard[part, back, :, angles:]
        for other in beside:
            down(part, other, seat).start()
        incoming[part, seat] = told[part, seat]

    def learn(part):
        for other in beside:
            down(part, other, other).wait_recv()

    segment = lax.broadcasted_iota(jnp.int32, (GROUP, LANES), 0)
    half = width // 2

    def tile(index):
        return slice(index * TILE, (index + 1) * TILE)

    tiles = half // TILE
    sums_even = []
    for index in range(tiles):
        near = source[:, tile(index)]
        far = mirror(source[:, tile(width // TILE - 1 - index)])
        sums_even.append(near + far)
        split_store(near - far, xoh, xol, tile(index))
    for index in range(tiles // 2):
        near, far = sums_even[index], mirror(sums_even[tiles - 1 - index])
        split_store(near + far, xeh, xel, tile(index))
        split_store(near - far, xeh, xel, tile(index + tiles // 2))

    def transform(part, index):
        high, low, table_hi, table_lo = (
            (xeh, xel, even_hi, even_lo),
            (xoh, xol, odd_hi, odd_lo),
        )[part]
        where = tile(index)
        depth = half if part else half // 2
        start = 0 if part or index < tiles // 2 else depth
        inner, outer = slice(start, start + depth), slice(0, depth)
        value = (
            jnp.dot(high[:, inner], table_hi[outer, where], preferred_element_type=f32)
            + jnp.dot(low[:, inner], table_hi[outer, where], preferred_element_type=f32)
            + jnp.dot(high[:, inner], table_lo[outer, where], preferred_element_type=f32)
        )
        for column in range(TILE // LANES):
            block = index * TILE // LANES + column
            coefs[part, block] = value[:, column * LANES : (column + 1) * LANES]

    def scan(part):
        result, carry_ref = ((solved, carried), (out, carries))[part]

        def run(chunk, _):
            table = pl.ds(pl.multiple_of(part * half + chunk * LANES, LANES), LANES)
            owner, place = chunk // share, lax.rem(chunk, share)
            gain = decays[2 * GROUP : 2 * GROUP + 1, table]
            step = decays[3 * GROUP : 3 * GROUP + 1, table]
            for angle in range(angles):
                values = [
                    coefs[part, chunk, pl.ds(angle * strip + group, GROUP, stride=groups)]
                    for group in range(groups)
                ]
                fall, falls = values[0], [values[0]]
                for group in range(1, groups):
                    fall = values[group] + step * fall
                    falls.append(fall)
                rise = values[-1]
                for group in reversed(range(groups)):
                    total = falls[group]
                    if group < groups - 1:
                        later = step * rise
                        total = total + later
                        rise = values[group] + later
                    first = angle * strip + group * GROUP
                    result[chunk, first : first + GROUP] = gain * total
                for index, by in enumerate((1, 2, 4)):
                    jump = decays[2 * GROUP + 1 + index : 2 * GROUP + 2 + index, table]
                    fall = fall + jnp.where(segment >= by, pltpu.roll(fall, by, 0), 0.0) * jump
                    rise = (
                        rise
                        + jnp.where(segment < GROUP - by, pltpu.roll(rise, GROUP - by, 0), 0.0)
                        * jump
                    )
                ends[part, owner, place, angle : angle + 1] = fall[GROUP - 1 :]
                ends[part, owner, place, angles + angle : angles + angle + 1] = rise[:1]
                carry_ref[chunk, angle] = gain * jnp.where(
                    segment >= 1, pltpu.roll(fall, 1, 0), 0.0
                )
                carry_ref[chunk, angles + angle] = gain * jnp.where(
                    segment < GROUP - 1, pltpu.roll(rise, GROUP - 1, 0), 0.0
                )
            return 0

        lax.fori_loop(0, blocks // 2, run, 0, unroll=2)

    for index in range(tiles):
        transform(1, index)
    scan(1)
    pl.semaphore_wait(barrier, plane + planes - 2)
    gather(1)
    for index in range(tiles):
        transform(0, index)
    spread(1)
    scan(0)
    gather(0)
    spread(0)
    answer(1)
    learn(1)
    enter(1, out, carries, incoming, decays, xoh, xol)
    answer(0)
    for index in range(tiles):
        odds[:, tile(index)] = restored(xoh, xol, odd_hi, odd_lo, tile(index))
    learn(0)
    for part in range(2):
        for other in beside:
            up(part, other, seat).wait_send()
            down(part, other, seat).wait_send()
        for other in beyond_planes:
            over(part, other, floor_at).wait_send()


def enter(part, value, carries, incoming, decays, high, low):
    angles = incoming.shape[3] // 2
    strip = value.shape[1] // angles
    half = value.shape[0] * LANES
    groups = strip // GROUP
    length = min(groups, GROUP)
    share = incoming.shape[2]

    def run(chunk, _):
        where = pl.ds(pl.multiple_of(chunk * LANES, LANES), LANES)
        table = pl.ds(pl.multiple_of(part * half + chunk * LANES, LANES), LANES)
        owner, place = chunk // share, lax.rem(chunk, share)
        for angle in range(angles):
            fall = (
                carries[chunk, angle]
                + decays[:GROUP, table] * incoming[part, owner, place, angle : angle + 1]
            )
            rise = (
                carries[chunk, angles + angle]
                + decays[GROUP : 2 * GROUP, table]
                * incoming[part, owner, place, angles + angle : angles + angle + 1]
            )
            for pair in range(0, strip, 2 * GROUP):
                rows = []
                for row in range(pair, pair + 2 * GROUP, length):
                    owner_row, group = row // groups, row % groups
                    ahead = 3 * GROUP + group
                    behind = ahead + groups
                    rows.append(
                        value[
                            chunk,
                            pl.ds(angle * strip + group * GROUP + owner_row, length, stride=GROUP),
                        ]
                        + decays[ahead : ahead + length, table] * fall[owner_row : owner_row + 1]
                        + decays[behind : behind + length, table] * rise[owner_row : owner_row + 1]
                    )
                item = jnp.concatenate(rows, 0)
                rounded = item.astype(bf16)
                start = angle * strip + pair
                high[start : start + 2 * GROUP, where] = rounded
                low[start : start + 2 * GROUP, where] = (item - rounded.astype(f32)).astype(bf16)
        return 0

    lax.fori_loop(0, half // LANES, run, 0)


def restored(high, low, table_hi, table_lo, where, depth=slice(None)):
    last = (((1,), (1,)), ((), ()))
    return (
        lax.dot_general(high[:, depth], table_hi[where, depth], last, preferred_element_type=f32)
        + lax.dot_general(low[:, depth], table_hi[where, depth], last, preferred_element_type=f32)
        + lax.dot_general(high[:, depth], table_lo[where, depth], last, preferred_element_type=f32)
    )


def inverse_kernel(
    field, value, carries, incoming, odds, even_hi, even_lo, decays,
    updated, out, xh, xl, parted, sems, field_sems,
):
    angles, strip, width = out.shape
    half = width // 2
    blocks = width // LANES
    copies = []
    for block in range(blocks):
        copy = pltpu.make_async_copy(
            field.at[:, :, block],
            updated.at[:, :, :, block * LANES : (block + 1) * LANES],
            field_sems.at[block],
        )
        copy.start()
        copies.append(copy)
    enter(0, value, carries, incoming, decays, xh, xl)
    tiles = [slice(first, first + TILE) for first in range(0, half, TILE)]

    def pair(index):
        return [
            restored(xh, xl, even_hi, even_lo, tiles[index], slice(first, first + half // 2))
            for first in (0, half // 2)
        ]

    later = pair(0)
    for index in range(len(tiles) // 2):
        whole, crossed = later
        if index + 1 < len(tiles) // 2:
            later = pair(index + 1)
        for place, even in (
            (index, whole + crossed),
            (len(tiles) - 1 - index, mirror(whole - crossed)),
        ):
            first, odd = tiles[place].start, odds[:, tiles[place]]
            near = even + odd
            far = mirror(even - odd)
            for item, start in ((near, first), (far, width - first - TILE)):
                where = slice(start, start + TILE)
                for angle in range(angles):
                    parted[angle, :, where] = item[angle * strip : (angle + 1) * strip]
                copy = pltpu.make_async_copy(
                    parted.at[:, :, where], out.at[:, :, where], sems.at[start // TILE]
                )
                copy.start()
                copies.append(copy)
    for copy in copies:
        copy.wait()


def body(object_field, probe, measured, frame_table, frame_count):
    angles, _, strip, width = object_field.shape
    side = probe.shape[1]
    cap = measured.shape[0]
    half = width // 2
    reach = side // strip
    rows = angles * strip
    strips = lax.axis_size("tile")
    blocks = width // LANES
    shape = jax.ShapeDtypeStruct

    pieces = (reach + 1) * cap
    plane = 2 ** (int(math.log2(strips)) // 2)
    share = blocks // (2 * plane)
    decays, joins = decay_tables(width, strip, plane)
    joins = jnp.asarray(joins.reshape(-1, 2, plane, share, LANES).transpose(1, 2, 0, 3, 4))

    factors = cosine_factors(width)
    table = (reach + 1, cap, 2, strip, side)
    held, source, *half_tables = pl.pallas_call(
        update_kernel,
        out_shape=[
            shape((angles, 2, blocks, strip, LANES), f32),
            shape((rows, width), f32),
        ]
        + [shape((half, half), bf16)] * 4,
        in_specs=[smem] + [hbm] * 7,
        out_specs=[vmem] * 6,
        scratch_shapes=[
            pltpu.VMEM(measured.shape, bf16),
            pltpu.VMEM((2, angles, 2, 1, width), f32),
            pltpu.VMEM((2, strip, LANES), f32),
            pltpu.VMEM((strip + GROUP, LANES), f32),
            pltpu.VMEM((2, 2, strip // GROUP, GROUP, LANES), f32),
            pltpu.VMEM((2, strip // GROUP, GROUP, LANES), f32),
            pltpu.VMEM((2, strip // GROUP, GROUP, LANES), f32),
            pltpu.VMEM((strip // GROUP, GROUP, LANES), f32),
            pltpu.SMEM((reach + 1, cap, 3), jnp.int32),
            pltpu.SMEM((1,), jnp.int32),
            pltpu.VMEM(probe.shape, f32),
            pltpu.VMEM((side, side), bf16),
            pltpu.VMEM((side, side), bf16),
            pltpu.VMEM(factors.shape, f32),
            pltpu.VMEM(measured.shape, bf16),
            pltpu.VMEM(table, bf16),
            pltpu.VMEM(table, bf16),
            pltpu.VMEM(table, bf16),
            pltpu.VMEM(table, bf16),
            pltpu.VMEM((cap, 2, strip, side), f32),
            pltpu.VMEM((reach + 1, cap, 2, side // LANES + 2, strip, LANES), f32),
            pltpu.VMEM(((reach + 1) * strip, side), f32),
            pltpu.VMEM((2, angles, 2, 1, width), f32),
            pltpu.SemaphoreType.DMA((6 + blocks,)),
            pltpu.SemaphoreType.DMA((2, reach + 1)),
            pltpu.SemaphoreType.DMA((2, 1)),
            pltpu.SemaphoreType.DMA((2, cap)),
            pltpu.SemaphoreType.DMA((2, pieces)),
            pltpu.SemaphoreType.DMA((2, pieces)),
            pltpu.SemaphoreType.DMA((2, 2)),
        ],
        compiler_params=params(collective_id=0, has_side_effects=True),
        cost_estimate=cost(20),
        name="update",
    )(
        frame_count,
        *[
            pltpu.with_memory_space_constraint(item, pltpu.HBM)
            for item in (
                frame_table,
                object_field,
                probe,
                measured,
                *fourier_tables(side),
                factors,
            )
        ],
    )

    planes = strips // plane
    lines = (share, 2 * angles, LANES)
    solved, carried, incoming, odds = pl.pallas_call(
        forward_kernel,
        out_shape=[
            shape((blocks // 2, rows, LANES), f32),
            shape((blocks // 2, 2 * angles, GROUP, LANES), f32),
            shape((2, plane) + lines, f32),
            shape((rows, half), f32),
        ],
        in_specs=[vmem] * 7,
        out_specs=[vmem] * 4,
        scratch_shapes=[pltpu.VMEM((rows, half), bf16)] * 4
        + [
            pltpu.VMEM((2, blocks // 2, rows, LANES), f32),
            pltpu.VMEM((blocks // 2, rows, LANES), f32),
            pltpu.VMEM((blocks // 2, 2 * angles, GROUP, LANES), f32),
            pltpu.VMEM((2, plane) + lines, f32),
            pltpu.VMEM((2, plane) + lines, f32),
            pltpu.VMEM((2,) + lines, f32),
            pltpu.VMEM((2, planes) + lines, f32),
            pltpu.VMEM((2, plane) + lines, f32),
            pltpu.SemaphoreType.DMA((2, plane)),
            pltpu.SemaphoreType.DMA((2, plane)),
            pltpu.SemaphoreType.DMA((2, planes)),
            pltpu.SemaphoreType.DMA((2, planes)),
            pltpu.SemaphoreType.DMA((2, plane)),
            pltpu.SemaphoreType.DMA((2, plane)),
        ],
        compiler_params=params(collective_id=1, has_side_effects=True),
        cost_estimate=cost(15),
        name="forward",
    )(source, *half_tables, decays, joins)
    updated, phase_map = pl.pallas_call(
        inverse_kernel,
        out_shape=[shape(object_field.shape, f32), shape((angles, strip, width), f32)],
        in_specs=[vmem] * 8,
        out_specs=[hbm, hbm],
        scratch_shapes=[
            pltpu.VMEM((rows, half), bf16),
            pltpu.VMEM((rows, half), bf16),
            pltpu.VMEM((angles, strip, width), f32),
            pltpu.SemaphoreType.DMA((width // TILE,)),
            pltpu.SemaphoreType.DMA((blocks,)),
        ],
        compiler_params=params(),
        cost_estimate=cost(6),
        name="inverse",
    )(held, solved, carried, incoming, odds, *half_tables[:2], decays)
    return (updated, phase_map)


def solution(mesh):
    return jax.shard_map(
        body,
        mesh=mesh,
        in_specs=(
            P("group", None, "tile", None),
            P(),
            P(("group", "tile"), None, None),
            P(("group", "tile"), None),
            P(("group", "tile")),
        ),
        out_specs=(P("group", None, "tile", None), P("group", "tile", None)),
        check_vma=False,
    )
```

```python
import functools
import math

import numpy as np
import jax
import jax.numpy as jnp
from jax import lax
from jax.experimental import pallas as pl
from jax.experimental.pallas import tpu as pltpu
from jax.sharding import PartitionSpec as P

magnitude_floor = 0.5
soften_term = 0.5
screen_term = 0.0001
epsilon_term = 1e-06
f32 = jnp.float32
bf16 = jnp.bfloat16
LANES = 128
GROUP = 8
TILE = 256
VMEM_BYTES = 30 * 1024 * 1024
MESH = pl.DeviceIdType.MESH
vmem = pl.BlockSpec(memory_space=pltpu.VMEM)
smem = pl.BlockSpec(memory_space=pltpu.SMEM)
hbm = pl.BlockSpec(memory_space=pltpu.HBM)


def cost(micros):
    return pl.CostEstimate(
        flops=0, bytes_accessed=int(micros * 3_000_000), transcendentals=0
    )


def params(**more):
    return pltpu.CompilerParams(vmem_limit_bytes=VMEM_BYTES, **more)


def fourier_tables(side):
    indices = np.arange(side)
    products = indices[:, None] * indices[None, :] % side
    phases = products.astype(np.float64) * (-2.0 * math.pi / side)
    scale = 1.0 / math.sqrt(side)
    return (
        jnp.asarray(np.cos(phases) * scale, f32).astype(bf16),
        jnp.asarray(np.sin(phases) * scale, f32).astype(bf16),
    )


def frequencies(grid_side):
    quarter = np.arange(grid_side // 4)
    even = np.concatenate([4 * quarter, 4 * quarter + 2])
    return even, 2 * np.arange(grid_side // 2) + 1


def cosine_factors(grid_side):
    half = grid_side // 2
    step = 32
    out = []
    for freqs in frequencies(grid_side):
        scale = np.where(freqs == 0, math.sqrt(1.0 / grid_side), math.sqrt(2.0 / grid_side))
        coarse = (2 * step * np.arange(half // step)[:, None] * freqs[None, :]) % (4 * grid_side)
        fine = ((2 * np.arange(step)[:, None] + 1) * freqs[None, :]) % (4 * grid_side)
        unit = math.pi / (2 * grid_side)
        out.append(
            np.stack(
                [
                    np.cos(coarse * unit) * scale,
                    np.sin(coarse * unit) * scale,
                    np.cos(fine * unit),
                    np.sin(fine * unit),
                ]
            )
        )
    return jnp.asarray(np.stack(out), f32)


def decay_tables(grid_side, strip_rows, plane):
    half = grid_side // 2
    freqs = np.concatenate(frequencies(grid_side)).astype(np.float64)
    shift = screen_term + 2.0 - 2.0 * np.cos(freqs * math.pi / grid_side)
    rate = 2.0 * np.arcsinh(np.sqrt(shift) / 2.0)
    gain = 2.0 / (2.0 * np.sinh(rate))
    groups = strip_rows // GROUP
    segments = np.exp(-groups * np.arange(GROUP)[:, None] * rate)
    steps = np.exp(-(np.arange(groups)[:, None] + 1) * rate)
    jumps = np.exp(-groups * np.array([[1], [2], [4]]) * rate)
    spare = np.zeros((GROUP - 4,) + gain.shape)
    decays = np.concatenate(
        [segments, segments[::-1], gain[None], jumps, spare, steps, steps[::-1]]
    )
    spans = strip_rows * np.array([[1], [plane], [grid_side // strip_rows]])
    closing = 1.0 / (1.0 - np.exp(-2.0 * grid_side * rate))
    joins = np.concatenate([np.exp(-spans * rate), closing[None], gain[None]])
    return decays.astype(np.float32), joins.astype(np.float32)


def table_rows(factors, part, high, low):
    step = factors.shape[2]

    def run(block, _):
        rows = pl.ds(pl.multiple_of(block * step, step), step)
        value = (
            factors[part, 0, pl.ds(block, 1)] * factors[part, 2]
            - factors[part, 1, pl.ds(block, 1)] * factors[part, 3]
        )
        rounded = value.astype(bf16)
        high[rows] = rounded
        low[rows] = (value - rounded.astype(f32)).astype(bf16)
        return 0

    lax.fori_loop(0, high.shape[0] // step, run, 0)


def window_start(column, width, span):
    return jnp.minimum(column // LANES, (width - span) // LANES) * LANES


def power_of(re, im):
    return re * re + im * im + 0.5 * soften_term


def half_bond(first, second):
    cross = first[0] * second[1] - first[1] * second[0]
    return cross / (first[2] + second[2])


def update_kernel(
    frame_count, frame_table, field, probe_in, measured, cos_in, sin_in, factors_in,
    held, source, even_hi, even_lo, odd_hi, odd_lo,
    staged, halo, power, drops, shifts, bonds, partial, afters, tables, counts, probe, cos_ref, sin_ref, factors, moved, cuts, arrived, away, landed,
    own, placed, window, edges,
    load_sems, tell_sems, count_sems, moved_sems, fetch_sems, give_sems, edge_sems,
):
    count = lax.axis_size("tile")
    me = lax.axis_index("tile")
    angles, _, strip, width = field.shape
    cap, side = measured.shape[0], measured.shape[1]
    span = side + LANES
    lanes = span // LANES
    blocks = width // LANES
    reach = tables.shape[0] - 1
    middle = reach // 2
    total = (reach + 1) * strip
    others = [j for j in range(reach + 1) if j != middle]

    def inside(place):
        return (place >= 0) & (place < count)

    def load(index, source, target):
        return pltpu.make_async_copy(source, target, load_sems.at[index])

    loads = [
        load(0, frame_table, tables.at[0]),
        load(1, factors_in, factors),
        load(2, probe_in, probe),
        load(3, cos_in, cos_ref),
        load(4, sin_in, sin_ref),
        load(5, measured, staged),
    ]
    strips = [
        load(6 + block, field.at[:, :, :, block * LANES : (block + 1) * LANES], held.at[:, :, block])
        for block in range(blocks)
    ]
    for item in [loads[0], loads[5]] + strips + loads[1:5]:
        item.start()

    def send(source, target, sems, index, by):
        copy = pltpu.make_async_remote_copy(
            src_ref=source,
            dst_ref=target,
            send_sem=sems.at[0, index],
            recv_sem=sems.at[1, index],
            device_id={"tile": me + by},
            device_id_type=MESH,
        )
        return copy, inside(me + by), inside(me - by)

    barrier = pltpu.get_barrier_semaphore()
    met = jnp.zeros((), jnp.int32)
    for by in [sign * by for by in range(1, reach + 1) for sign in (1, -1)]:

        @pl.when(inside(me + by))
        def _():
            pl.semaphore_signal(
                barrier, inc=1, device_id={"tile": me + by}, device_id_type=MESH
            )

        met = met + jnp.where(inside(me + by), 1, 0)
    pl.semaphore_wait(barrier, met)

    tells = [
        send(tables.at[0], tables.at[j], tell_sems, j, j) for j in range(1, reach + 1)
    ]
    tells.append(send(frame_count, counts, count_sems, 0, middle))
    moves = [
        send(staged.at[s], moved.at[s], moved_sems, s, middle) for s in range(cap)
    ]
    fetches = [
        [send(cuts.at[j, s], arrived.at[j, s], fetch_sems, s * (reach + 1) + j, middle - j) for j in others]
        for s in range(cap)
    ]
    gives = [
        [send(away.at[j, s], landed.at[j, s], give_sems, s * (reach + 1) + j, j - middle) for j in others]
        for s in range(cap)
    ]
    borders = [
        send(edges.at[1], halo.at[0], edge_sems, 0, 1),
        send(edges.at[0], halo.at[1], edge_sems, 1, -1),
    ]
    started = []

    def start(items):
        for copy, sends, takes in items:
            pl.when(sends)(copy.start)
            started.append((copy, sends))

    def arrive(items):
        for copy, sends, takes in items:
            pl.when(takes)(copy.wait_recv)

    def blank(items, wipe):
        for index, (copy, sends, takes) in enumerate(items):

            @pl.when(jnp.logical_not(takes))
            def _():
                wipe(index)

    def wipe_table(index):
        if index == reach:
            counts[0] = 0
        else:
            for s in range(cap):
                for item in range(3):
                    tables[index + 1, s, item] = 0

    def wipe(ref, *first):
        ref[first] = jnp.zeros(ref.shape[len(first):], ref.dtype)

    loads[0].wait()
    start(tells)
    loads[5].wait()
    start(moves)
    blank(tells, wipe_table)
    blank(moves, lambda s: wipe(moved, s))
    for s in range(cap):
        blank(fetches[s], lambda index: wipe(arrived, others[index], s))
        blank(gives[s], lambda index: wipe(landed, others[index], s))
    blank(borders, lambda index: wipe(halo, index))
    for j in range(reach + 1):
        for s in range(cap):
            for part in range(2):
                placed[j, s, part, 0] = jnp.zeros((strip, LANES), f32)
    loads[1].wait()
    table_rows(factors, 0, even_hi, even_lo)
    for item in strips:
        item.wait()
    arrive(tells)

    def first_block(j, s):
        return jnp.minimum(tables[j, s, 1] // LANES, blocks - lanes)

    for s in range(cap):
        for j in others + [middle]:
            block = first_block(j, s)
            shift = tables[j, s, 1] - block * LANES
            angle = tables[j, s, 2]
            for part in range(2):
                piece = jnp.concatenate(
                    [held[angle, part, block + lane] for lane in range(lanes)], 1
                )
                turned = pltpu.roll(piece, lax.rem(span - shift, span), 1)
                target = arrived if j == middle else cuts
                target[j, s, part] = turned[:, :side].astype(bf16)
        start(fetches[s])

    table_rows(factors, 1, odd_hi, odd_lo)
    for item in loads[2:5]:
        item.wait()
    cos_part, sin_part = cos_ref[...], sin_ref[...]
    stacked = jnp.concatenate([cos_part, sin_part], 0)
    joined = jnp.concatenate([cos_part, sin_part], 1)
    probe_re, probe_im = probe[0], probe[1]
    peak = jnp.max(probe_re * probe_re + probe_im * probe_im) + epsilon_term

    def left(re, im, sign):
        products = jnp.dot(
            stacked, jnp.concatenate([re, im], 1), preferred_element_type=f32
        )
        cc, ci = products[:side, :side], products[:side, side:]
        sc, si = products[side:, :side], products[side:, side:]
        return (cc - si, ci + sc) if sign > 0 else (cc + si, ci - sc)

    def right(re, im, sign):
        products = jnp.dot(
            jnp.concatenate([re, im], 0), joined, preferred_element_type=f32
        )
        rc, rs = products[:side, :side], products[:side, side:]
        ic, js = products[side:, :side], products[side:, side:]
        return (rc - js, rs + ic) if sign > 0 else (rc + js, ic - rs)

    for s in range(cap):
        arrive(fetches[s])
        offset = tables[middle, s, 0]
        patch = []
        for part in range(2):
            for j in range(reach + 1):
                window[j * strip : (j + 1) * strip] = arrived[j, s, part].astype(f32)
            turned = pltpu.roll(window[...], lax.rem(total - offset, total), 0)
            patch.append(turned[:side])
        wave_re = (probe_re * patch[0] - probe_im * patch[1]).astype(bf16)
        wave_im = (probe_re * patch[1] + probe_im * patch[0]).astype(bf16)
        half_re, half_im = left(wave_re, wave_im, 1)
        spec_re, spec_im = right(half_re.astype(bf16), half_im.astype(bf16), 1)
        amplitude = jnp.sqrt(spec_re * spec_re + spec_im * spec_im)
        arrive(moves[s : s + 1])
        factor = moved[s].astype(f32) / jnp.maximum(amplitude, magnitude_floor) - 1.0
        back_re, back_im = left(
            (spec_re * factor).astype(bf16), (spec_im * factor).astype(bf16), -1
        )
        corr_re, corr_im = right(back_re.astype(bf16), back_im.astype(bf16), -1)
        live = s < counts[0]
        updates = (
            (probe_re * corr_re + probe_im * corr_im) / peak,
            (probe_re * corr_im - probe_im * corr_re) / peak,
        )
        for part in range(2):
            window[:side] = jnp.where(live, updates[part], 0.0)
            window[side:] = jnp.zeros((total - side, side), f32)
            turned = pltpu.roll(window[...], offset, 0)
            for j in range(reach + 1):
                piece = turned[j * strip : (j + 1) * strip]
                if j == middle:
                    own[s, part] = piece
                else:
                    away[j, s, part] = piece.astype(bf16)
        start(gives[s])

    pad = jnp.zeros((strip, LANES), f32)

    def shifted(source, j, s):
        shift = tables[j, s, 1] - first_block(j, s) * LANES
        for part in range(2):
            value = jnp.concatenate([source[part].astype(f32), pad], 1)
            turned = pltpu.roll(value, shift, 1)
            for lane in range(lanes):
                placed[j, s, part, lane + 1] = turned[:, lane * LANES : (lane + 1) * LANES]

    def add(items, rows):
        def chunk(block, _):
            for angle in range(angles):
                found = []
                for j, s in items:
                    near = block - first_block(j, s)
                    hit = (tables[j, s, 2] == angle) & (near >= 0) & (near < lanes)
                    found.append(jnp.where(hit, near + 1, 0))
                for part in range(2):
                    for row in rows:
                        value = held[angle, part, block, row]
                        for (j, s), index in zip(items, found):
                            value = value + placed[j, s, part, index, row]
                        held[angle, part, block, row] = value
            return 0

        lax.fori_loop(0, blocks, chunk, 0)

    for s in range(cap):
        shifted(own.at[s], middle, s)
    early = [(middle, s) for s in range(cap)]
    for s in range(cap - 1):
        arrive(gives[s])
        for j in others:
            shifted(landed.at[j, s], j, s)
        early += [(j, s) for j in others]
    add(early, [slice(0, strip)])
    arrive(gives[cap - 1])
    for j in others:
        shifted(landed.at[j, cap - 1], j, cap - 1)
    late = [(j, cap - 1) for j in others]
    add(late, [slice(0, GROUP), slice(strip - GROUP, strip)])
    for angle in range(angles):
        for part in range(2):
            for block in range(blocks):
                where = slice(block * LANES, (block + 1) * LANES)
                edges[0, angle, part, :, where] = held[angle, part, block, :1]
                edges[1, angle, part, :, where] = held[angle, part, block, strip - 1 :]
    start(borders)
    add(late, [slice(GROUP, strip - GROUP)])

    groups = strip // GROUP
    lane = lax.broadcasted_iota(jnp.int32, (GROUP, LANES), 1)
    segment = lax.broadcasted_iota(jnp.int32, (GROUP, LANES), 0)
    drops[:GROUP] = jnp.zeros((GROUP, LANES), f32)
    for angle in range(angles):

        def rows_of(group):
            return slice(group * GROUP, (group + 1) * GROUP)

        def prepare(block, slot):
            for group in range(groups):
                pair = [held[angle, part, block, rows_of(group)] for part in range(2)]
                power[slot, rows_of(group)] = power_of(*pair)
                for part, value in enumerate(pair):
                    shifts[slot, part, group] = pltpu.roll(value, 1, 1)

        def combine(block, slot):
            for group in range(groups):
                here = [held[angle, part, block, rows_of(group)] for part in range(2)]
                here.append(power[slot, rows_of(group)])
                if group == groups - 1:
                    below = [
                        jnp.where(segment == GROUP - 1, 0.0, pltpu.roll(value, GROUP - 1, 0))
                        for value in here[:2]
                    ]
                    below.append(power_of(*below))
                else:
                    lower = slice(group * GROUP + 1, (group + 1) * GROUP + 1)
                    below = [held[angle, part, block, lower] for part in range(2)]
                    below.append(power[slot, lower])
                down = half_bond(here, below)
                first = (group + 1) * GROUP
                drops[first : first + GROUP] = down
                up = drops[first - 1 : first - 1 + GROUP]
                left = [
                    jnp.where(lane == 0, shifts[1 - slot, part, group], shifts[slot, part, group])
                    for part in range(2)
                ]
                bond = half_bond(left + [power_of(*left)], here)
                bonds[slot, group] = bond
                partial[slot, group] = up - down + bond

        def finish(block, slot):
            behind = pl.ds(pl.multiple_of(jnp.maximum(block - 1, 0) * LANES, LANES), LANES)
            for group in range(groups):
                after = pltpu.roll(bonds[slot, group], LANES - 1, 1)
                first = angle * strip + group * GROUP
                source[first : first + GROUP, behind] = partial[1 - slot, group] - jnp.where(
                    lane == LANES - 1, after, afters[group]
                )
                afters[group] = after

        def step(pair, _):
            block = 2 * pair
            finish(block - 1, 1)
            combine(block, 0)
            prepare(block + 1, 1)
            finish(block, 0)
            combine(block + 1, 1)
            prepare(jnp.minimum(block + 2, blocks - 1), 0)
            return 0

        for group in range(groups):
            for part in range(2):
                shifts[1, part, group] = jnp.zeros((GROUP, LANES), f32)
        prepare(0, 0)
        lax.fori_loop(0, blocks // 2, step, 0)
        finish(blocks - 1, 1)
        for group in range(groups):
            first = angle * strip + group * GROUP
            source[first : first + GROUP, width - LANES :] = partial[1, group] - jnp.where(
                lane == LANES - 1, 0.0, afters[group]
            )

    arrive(borders)

    def line(values):
        return values + [power_of(*values)]

    for angle in range(angles):
        for border, row in ((0, 0), (1, strip - 1)):
            inner = line(
                [
                    jnp.concatenate(
                        [held[angle, part, block, row : row + 1] for block in range(blocks)], 1
                    )
                    for part in range(2)
                ]
            )
            outer = line([halo[border, angle, part] for part in range(2)])
            place = slice(angle * strip + row, angle * strip + row + 1)
            source[place] = source[place] + half_bond(outer, inner)
    for copy, sends in started:
        pl.when(sends)(copy.wait_send)


def mirror(value):
    side = value.shape[1]
    rows = lax.broadcasted_iota(jnp.int32, (side, side), 0)
    columns = lax.broadcasted_iota(jnp.int32, (side, side), 1)
    swap = jnp.where(rows + columns == side - 1, 1.0, 0.0).astype(bf16)
    high = value.astype(bf16)
    low = (value - high.astype(f32)).astype(bf16)
    return jnp.dot(high, swap, preferred_element_type=f32) + jnp.dot(
        low, swap, preferred_element_type=f32
    )


def split_store(value, high, low, columns):
    rounded = value.astype(bf16)
    high[:, columns] = rounded
    low[:, columns] = (value - rounded.astype(f32)).astype(bf16)


def forward_kernel(
    source, even_hi, even_lo, odd_hi, odd_lo, decays, joins,
    solved, carried, incoming, evens,
    xeh, xel, xoh, xol, coefs,
    out, carries, ends, heard, sums, totals, told,
    up_sems, in_sems, over_sems, across_sems, down_sems, back_sems,
):
    angles, width = ends.shape[3] // 2, source.shape[1]
    strip, blocks = source.shape[0] // angles, width // LANES
    groups = strip // GROUP
    plane, share = ends.shape[1], ends.shape[2]
    planes = totals.shape[1]
    me = lax.axis_index("tile")
    floor_at, seat = me // plane, lax.rem(me, plane)
    beside = [lax.rem(seat + by, plane) for by in range(1, plane)]
    beyond_planes = [lax.rem(floor_at + by, planes) for by in range(1, planes)]
    barrier = pltpu.get_barrier_semaphore()
    for peer in [floor_at * plane + other for other in beside] + [
        other * plane + seat for other in beyond_planes
    ]:
        pl.semaphore_signal(barrier, inc=1, device_id={"tile": peer}, device_id_type=MESH)

    def hop(source_ref, target_ref, send_sem, recv_sem, peer):
        return pltpu.make_async_remote_copy(
            src_ref=source_ref,
            dst_ref=target_ref,
            send_sem=send_sem,
            recv_sem=recv_sem,
            device_id={"tile": peer},
            device_id_type=MESH,
        )

    def up(part, other, slot):
        return hop(
            ends.at[part, other], heard.at[part, slot], up_sems.at[part, other],
            in_sems.at[part, slot], floor_at * plane + other,
        )

    def over(part, other, slot):
        return hop(
            sums.at[part], totals.at[part, slot], over_sems.at[part, other],
            across_sems.at[part, slot], other * plane + seat,
        )

    def down(part, other, slot):
        return hop(
            told.at[part, other], incoming.at[part, slot], down_sems.at[part, other],
            back_sems.at[part, slot], floor_at * plane + other,
        )

    def gather(part):
        for other in beside:
            up(part, other, seat).start()
        heard[part, seat] = ends[part, seat]

    def spread(part):
        for other in beside:
            up(part, other, other).wait_recv()
        step = joins[part, seat, 0][:, None]
        fall = heard[part, 0, :, :angles]
        rise = heard[part, plane - 1, :, angles:]
        for item in range(1, plane):
            fall = fall * step + heard[part, item, :, :angles]
            rise = rise * step + heard[part, plane - 1 - item, :, angles:]
        sums[part, :, :angles] = fall
        sums[part, :, angles:] = rise
        for other in beyond_planes:
            over(part, other, floor_at).start()
        totals[part, floor_at] = sums[part]

    def answer(part):
        for other in beyond_planes:
            over(part, other, other).wait_recv()
        step, leap, whole, closing, gain = [joins[part, seat, item][:, None] for item in range(5)]
        bottom = totals[part, 0, :, :angles]
        top = totals[part, planes - 1, :, angles:]
        for item in range(1, planes):
            bottom = bottom * leap + totals[part, item, :, :angles]
            top = top * leap + totals[part, planes - 1 - item, :, angles:]
        fall = (top + whole * bottom) * closing
        rise = (bottom + whole * top) * closing
        fall_here, rise_here = fall, rise
        for item in range(planes):
            fall_here = jnp.where(floor_at == item, fall, fall_here)
            fall = fall * leap + totals[part, item, :, :angles]
            back = planes - 1 - item
            rise_here = jnp.where(floor_at == back, rise, rise_here)
            rise = rise * leap + totals[part, back, :, angles:]
        for item in range(plane):
            told[part, item, :, :angles] = fall_here * gain
            fall_here = fall_here * step + heard[part, item, :, :angles]
            back = plane - 1 - item
            told[part, back, :, angles:] = rise_here * gain
            rise_here = rise_here * step + heard[part, back, :, angles:]
        for other in beside:
            down(part, other, seat).start()
        incoming[part, seat] = told[part, seat]

    def learn(part):
        for other in beside:
            down(part, other, other).wait_recv()

    segment = lax.broadcasted_iota(jnp.int32, (GROUP, LANES), 0)
    half = width // 2

    def tile(index):
        return slice(index * TILE, (index + 1) * TILE)

    tiles = half // TILE
    sums_even = []
    for index in range(tiles):
        near = source[:, tile(index)]
        far = mirror(source[:, tile(width // TILE - 1 - index)])
        sums_even.append(near + far)
        split_store(near - far, xoh, xol, tile(index))
    for index in range(tiles // 2):
        near, far = sums_even[index], mirror(sums_even[tiles - 1 - index])
        split_store(near + far, xeh, xel, tile(index))
        split_store(near - far, xeh, xel, tile(index + tiles // 2))

    def transform(part, index):
        high, low, table_hi, table_lo = (
            (xeh, xel, even_hi, even_lo),
            (xoh, xol, odd_hi, odd_lo),
        )[part]
        where = tile(index)
        depth = half if part else half // 2
        start = 0 if part or index < tiles // 2 else depth
        inner, outer = slice(start, start + depth), slice(0, depth)
        value = (
            jnp.dot(high[:, inner], table_hi[outer, where], preferred_element_type=f32)
            + jnp.dot(low[:, inner], table_hi[outer, where], preferred_element_type=f32)
            + jnp.dot(high[:, inner], table_lo[outer, where], preferred_element_type=f32)
        )
        for column in range(TILE // LANES):
            block = index * TILE // LANES + column
            coefs[part, block] = value[:, column * LANES : (column + 1) * LANES]

    def scan(part):
        result, carry_ref = ((out, carries), (solved, carried))[part]

        def run(chunk, _):
            table = pl.ds(pl.multiple_of(part * half + chunk * LANES, LANES), LANES)
            owner, place = chunk // share, lax.rem(chunk, share)
            gain = decays[2 * GROUP : 2 * GROUP + 1, table]
            step = decays[3 * GROUP : 3 * GROUP + 1, table]
            for angle in range(angles):
                values = [
                    coefs[part, chunk, pl.ds(angle * strip + group, GROUP, stride=groups)]
                    for group in range(groups)
                ]
                fall, falls = values[0], [values[0]]
                for group in range(1, groups):
                    fall = values[group] + step * fall
                    falls.append(fall)
                rise = values[-1]
                for group in reversed(range(groups)):
                    total = falls[group]
                    if group < groups - 1:
                        later = step * rise
                        total = total + later
                        rise = values[group] + later
                    first = angle * strip + group * GROUP
                    result[chunk, first : first + GROUP] = gain * total
                for index, by in enumerate((1, 2, 4)):
                    jump = decays[2 * GROUP + 1 + index : 2 * GROUP + 2 + index, table]
                    fall = fall + jnp.where(segment >= by, pltpu.roll(fall, by, 0), 0.0) * jump
                    rise = (
                        rise
                        + jnp.where(segment < GROUP - by, pltpu.roll(rise, GROUP - by, 0), 0.0)
                        * jump
                    )
                ends[part, owner, place, angle : angle + 1] = fall[GROUP - 1 :]
                ends[part, owner, place, angles + angle : angles + angle + 1] = rise[:1]
                carry_ref[chunk, angle] = gain * jnp.where(
                    segment >= 1, pltpu.roll(fall, 1, 0), 0.0
                )
                carry_ref[chunk, angles + angle] = gain * jnp.where(
                    segment < GROUP - 1, pltpu.roll(rise, GROUP - 1, 0), 0.0
                )
            return 0

        lax.fori_loop(0, blocks // 2, run, 0, unroll=2)

    for index in range(tiles):
        transform(0, index)
    scan(0)
    pl.semaphore_wait(barrier, plane + planes - 2)
    gather(0)
    for index in range(tiles):
        transform(1, index)
    spread(0)
    scan(1)
    gather(1)
    spread(1)
    answer(0)
    answer(1)
    learn(0)
    enter(0, out, carries, incoming, decays, xeh, xel)
    for index in range(tiles // 2):
        where = tile(index)
        whole, crossed = [
            restored(xeh, xel, even_hi, even_lo, where, slice(first, first + half // 2))
            for first in (0, half // 2)
        ]
        evens[:, where] = whole + crossed
        evens[:, tile(tiles - 1 - index)] = mirror(whole - crossed)
    learn(1)
    for part in range(2):
        for other in beside:
            up(part, other, seat).wait_send()
            down(part, other, seat).wait_send()
        for other in beyond_planes:
            over(part, other, floor_at).wait_send()


def enter(part, value, carries, incoming, decays, high, low):
    angles = incoming.shape[3] // 2
    strip = value.shape[1] // angles
    half = value.shape[0] * LANES
    groups = strip // GROUP
    length = min(groups, GROUP)
    share = incoming.shape[2]

    def run(chunk, _):
        where = pl.ds(pl.multiple_of(chunk * LANES, LANES), LANES)
        table = pl.ds(pl.multiple_of(part * half + chunk * LANES, LANES), LANES)
        owner, place = chunk // share, lax.rem(chunk, share)
        for angle in range(angles):
            fall = (
                carries[chunk, angle]
                + decays[:GROUP, table] * incoming[part, owner, place, angle : angle + 1]
            )
            rise = (
                carries[chunk, angles + angle]
                + decays[GROUP : 2 * GROUP, table]
                * incoming[part, owner, place, angles + angle : angles + angle + 1]
            )
            for pair in range(0, strip, 2 * GROUP):
                rows = []
                for row in range(pair, pair + 2 * GROUP, length):
                    owner_row, group = row // groups, row % groups
                    ahead = 3 * GROUP + group
                    behind = ahead + groups
                    rows.append(
                        value[
                            chunk,
                            pl.ds(angle * strip + group * GROUP + owner_row, length, stride=GROUP),
                        ]
                        + decays[ahead : ahead + length, table] * fall[owner_row : owner_row + 1]
                        + decays[behind : behind + length, table] * rise[owner_row : owner_row + 1]
                    )
                item = jnp.concatenate(rows, 0)
                rounded = item.astype(bf16)
                start = angle * strip + pair
                high[start : start + 2 * GROUP, where] = rounded
                low[start : start + 2 * GROUP, where] = (item - rounded.astype(f32)).astype(bf16)
        return 0

    lax.fori_loop(0, half // LANES, run, 0)


def restored(high, low, table_hi, table_lo, where, depth=slice(None)):
    last = (((1,), (1,)), ((), ()))
    return (
        lax.dot_general(high[:, depth], table_hi[where, depth], last, preferred_element_type=f32)
        + lax.dot_general(low[:, depth], table_hi[where, depth], last, preferred_element_type=f32)
        + lax.dot_general(high[:, depth], table_lo[where, depth], last, preferred_element_type=f32)
    )


def inverse_kernel(
    field, value, carries, incoming, evens, odd_hi, odd_lo, decays,
    updated, out, xh, xl, parted, sems, field_sems,
):
    angles, strip, width = out.shape
    half = width // 2
    blocks = width // LANES
    copies = []
    for block in range(blocks):
        copy = pltpu.make_async_copy(
            field.at[:, :, block],
            updated.at[:, :, :, block * LANES : (block + 1) * LANES],
            field_sems.at[block],
        )
        copy.start()
        copies.append(copy)
    enter(1, value, carries, incoming, decays, xh, xl)
    tiles = [slice(first, first + TILE) for first in range(0, half, TILE)]
    later = restored(xh, xl, odd_hi, odd_lo, tiles[0])
    for index, where in enumerate(tiles):
        first, odd, even = where.start, later, evens[:, where]
        if index + 1 < len(tiles):
            later = restored(xh, xl, odd_hi, odd_lo, tiles[index + 1])
        near = even + odd
        far = mirror(even - odd)
        for item, start in ((near, first), (far, width - first - TILE)):
            where = slice(start, start + TILE)
            for angle in range(angles):
                parted[angle, :, where] = item[angle * strip : (angle + 1) * strip]
            copy = pltpu.make_async_copy(
                parted.at[:, :, where], out.at[:, :, where], sems.at[start // TILE]
            )
            copy.start()
            copies.append(copy)
    for copy in copies:
        copy.wait()


def body(object_field, probe, measured, frame_table, frame_count):
    angles, _, strip, width = object_field.shape
    side = probe.shape[1]
    cap = measured.shape[0]
    half = width // 2
    reach = side // strip
    rows = angles * strip
    strips = lax.axis_size("tile")
    blocks = width // LANES
    shape = jax.ShapeDtypeStruct

    pieces = (reach + 1) * cap
    plane = 2 ** (int(math.log2(strips)) // 2)
    share = blocks // (2 * plane)
    decays, joins = decay_tables(width, strip, plane)
    joins = jnp.asarray(joins.reshape(-1, 2, plane, share, LANES).transpose(1, 2, 0, 3, 4))

    factors = cosine_factors(width)
    table = (reach + 1, cap, 2, strip, side)
    held, source, *half_tables = pl.pallas_call(
        update_kernel,
        out_shape=[
            shape((angles, 2, blocks, strip, LANES), f32),
            shape((rows, width), f32),
        ]
        + [shape((half, half), bf16)] * 4,
        in_specs=[smem] + [hbm] * 7,
        out_specs=[vmem] * 6,
        scratch_shapes=[
            pltpu.VMEM(measured.shape, bf16),
            pltpu.VMEM((2, angles, 2, 1, width), f32),
            pltpu.VMEM((2, strip, LANES), f32),
            pltpu.VMEM((strip + GROUP, LANES), f32),
            pltpu.VMEM((2, 2, strip // GROUP, GROUP, LANES), f32),
            pltpu.VMEM((2, strip // GROUP, GROUP, LANES), f32),
            pltpu.VMEM((2, strip // GROUP, GROUP, LANES), f32),
            pltpu.VMEM((strip // GROUP, GROUP, LANES), f32),
            pltpu.SMEM((reach + 1, cap, 3), jnp.int32),
            pltpu.SMEM((1,), jnp.int32),
            pltpu.VMEM(probe.shape, f32),
            pltpu.VMEM((side, side), bf16),
            pltpu.VMEM((side, side), bf16),
            pltpu.VMEM(factors.shape, f32),
            pltpu.VMEM(measured.shape, bf16),
            pltpu.VMEM(table, bf16),
            pltpu.VMEM(table, bf16),
            pltpu.VMEM(table, bf16),
            pltpu.VMEM(table, bf16),
            pltpu.VMEM((cap, 2, strip, side), f32),
            pltpu.VMEM((reach + 1, cap, 2, side // LANES + 2, strip, LANES), f32),
            pltpu.VMEM(((reach + 1) * strip, side), f32),
            pltpu.VMEM((2, angles, 2, 1, width), f32),
            pltpu.SemaphoreType.DMA((6 + blocks,)),
            pltpu.SemaphoreType.DMA((2, reach + 1)),
            pltpu.SemaphoreType.DMA((2, 1)),
            pltpu.SemaphoreType.DMA((2, cap)),
            pltpu.SemaphoreType.DMA((2, pieces)),
            pltpu.SemaphoreType.DMA((2, pieces)),
            pltpu.SemaphoreType.DMA((2, 2)),
        ],
        compiler_params=params(collective_id=0, has_side_effects=True),
        cost_estimate=cost(20),
        name="update",
    )(
        frame_count,
        *[
            pltpu.with_memory_space_constraint(item, pltpu.HBM)
            for item in (
                frame_table,
                object_field,
                probe,
                measured,
                *fourier_tables(side),
                factors,
            )
        ],
    )

    planes = strips // plane
    lines = (share, 2 * angles, LANES)
    solved, carried, incoming, evens = pl.pallas_call(
        forward_kernel,
        out_shape=[
            shape((blocks // 2, rows, LANES), f32),
            shape((blocks // 2, 2 * angles, GROUP, LANES), f32),
            shape((2, plane) + lines, f32),
            shape((rows, half), f32),
        ],
        in_specs=[vmem] * 7,
        out_specs=[vmem] * 4,
        scratch_shapes=[pltpu.VMEM((rows, half), bf16)] * 4
        + [
            pltpu.VMEM((2, blocks // 2, rows, LANES), f32),
            pltpu.VMEM((blocks // 2, rows, LANES), f32),
            pltpu.VMEM((blocks // 2, 2 * angles, GROUP, LANES), f32),
            pltpu.VMEM((2, plane) + lines, f32),
            pltpu.VMEM((2, plane) + lines, f32),
            pltpu.VMEM((2,) + lines, f32),
            pltpu.VMEM((2, planes) + lines, f32),
            pltpu.VMEM((2, plane) + lines, f32),
            pltpu.SemaphoreType.DMA((2, plane)),
            pltpu.SemaphoreType.DMA((2, plane)),
            pltpu.SemaphoreType.DMA((2, planes)),
            pltpu.SemaphoreType.DMA((2, planes)),
            pltpu.SemaphoreType.DMA((2, plane)),
            pltpu.SemaphoreType.DMA((2, plane)),
        ],
        compiler_params=params(collective_id=1, has_side_effects=True),
        cost_estimate=cost(15),
        name="forward",
    )(source, *half_tables, decays, joins)
    updated, phase_map = pl.pallas_call(
        inverse_kernel,
        out_shape=[shape(object_field.shape, f32), shape((angles, strip, width), f32)],
        in_specs=[vmem] * 8,
        out_specs=[hbm, hbm],
        scratch_shapes=[
            pltpu.VMEM((rows, half), bf16),
            pltpu.VMEM((rows, half), bf16),
            pltpu.VMEM((angles, strip, width), f32),
            pltpu.SemaphoreType.DMA((width // TILE,)),
            pltpu.SemaphoreType.DMA((blocks,)),
        ],
        compiler_params=params(),
        cost_estimate=cost(6),
        name="inverse",
    )(held, solved, carried, incoming, evens, *half_tables[2:], decays)
    return (updated, phase_map)


def solution(mesh):
    return jax.shard_map(
        body,
        mesh=mesh,
        in_specs=(
            P("group", None, "tile", None),
            P(),
            P(("group", "tile"), None, None),
            P(("group", "tile"), None),
            P(("group", "tile")),
        ),
        out_specs=(P("group", None, "tile", None), P("group", "tile", None)),
        check_vma=False,
    )
```
